32 devices in a mesh: gx: 8 (over z, core), gy: 4 (over y, x).
Axes of the slice: x: 2, y: 2, z: 4, core: 2. Of those that a mesh axis runs over, the one named last changes fastest.
Arguments:
- e_init: float32 [3, 64, 32, 512], P(None, 'gx', None, 'gy'), may hold values from -13.5 to 13.5
- h_init: float32 [3, 64, 32, 512], P(None, 'gx', None, 'gy'), may hold values from -13.5 to 13.5
- material: int32 [64, 32, 512], P('gx', None, 'gy'), may hold values from 0 to 7
- eps_table: float32 [8], replicated, may hold values from 1 to 12
- target: float32 [8, 64, 64], replicated, may hold values from 0 to 2
Outputs:
- sensitivity: float32 [64, 32, 512], P('gx', None, 'gy')
The draws below stay inside these ranges and needn't reach their ends.
All inputs are finite; a program needn't handle non-finite values.
Results may differ from the reference program's by a relative error of at most 0.0001.
Values sent between devices are 32-bit elements; how exact they have to be, the bound alone decides.
No kernel may reach another device: no remote copies, remote signals or barrier semaphores. Data moves between devices by JAX's collectives and lax.ppermute only.
A program may use at most 128 MiB of HBM per device.

```python
import math
import jax
import jax.numpy as jnp
from jax import lax

CY = 128
CZ = 32
ITERS = 6
NF = 8
FAR = 64
NMAT = 8
NX = 64
NY = 512


def field_draw(key, salt):
    key = jax.random.fold_in(key, salt)
    first = jax.random.fold_in(key, 0)
    rows = jnp.arange(NX, dtype=jnp.float32) / NX
    cols = jnp.arange(NY, dtype=jnp.float32) / NY
    amplitude = 0.6 * jnp.exp(math.log(3.0) * rows)[:, None, None] * jnp.exp(math.log(1.5) * cols)[None, None, :]
    base = jnp.clip(jax.random.normal(first, (3, NX, CZ, NY), jnp.float32), -5.0, 5.0)
    return base * amplitude


def draw_e_init(key, part):
    return field_draw(key, 11)


def draw_h_init(key, part):
    return field_draw(key, 23)


def place_ends(drawn, rng, low, largest):
    dims = drawn.shape
    spot = [jax.random.randint(jax.random.fold_in(rng, axis), (), 0, dims[axis]) for axis in range(len(dims))]
    drawn = drawn.at[tuple(spot)].set(low)
    longest = dims.index(max(dims))
    spot[longest] = (spot[longest] + 1) % dims[longest]
    return drawn.at[tuple(spot)].set(largest)


def setup_inputs(seed: int = 0) -> dict:
    key_of = jax.random.split(jax.random.key(seed), 6)
    e_init = draw_e_init(jax.random.fold_in(key_of[5], 71), 0)
    h_init = draw_h_init(jax.random.fold_in(key_of[5], 71), 0)
    material = place_ends(jax.random.randint(key_of[2], (NX, CZ, NY), 0, NMAT), jax.random.fold_in(key_of[2], 1), 0, NMAT - 1).astype(jnp.int32)
    eps_table = jnp.clip(jnp.exp(jax.random.uniform(key_of[3], (NMAT,), jnp.float32, math.log(1.0), math.log(12.0))), 1.0, 12.0)
    target = jnp.clip(jax.random.uniform(key_of[4], (NF, FAR, FAR), jnp.float32, 0.0, 2.0), 0.0, 2.0)
    return {"e_init": e_init, "h_init": h_init, "material": material, "eps_table": eps_table, "target": target}


COURANT = 0.5
TWO_PI = 2.0 * math.pi
HIGHEST = lax.Precision.HIGHEST

def fold_next(part, edge, axis):
    rest = lax.slice_in_dim(part, 1, part.shape[axis], axis=axis)
    return jnp.concatenate([rest, jnp.expand_dims(edge, axis)], axis=axis) - part

def fold_prev(part, edge, axis):
    rest = lax.slice_in_dim(part, 0, part.shape[axis] - 1, axis=axis)
    return part - jnp.concatenate([jnp.expand_dims(edge, axis), rest], axis=axis)

def curl_grid(field, fold):
    edge_rows = jnp.zeros((field.shape[2], field.shape[3]), jnp.float32)
    edge_depth = jnp.zeros((field.shape[1], field.shape[3]), jnp.float32)
    edge_cols = jnp.zeros((field.shape[1], field.shape[2]), jnp.float32)
    curl_x = fold(field[2], edge_cols, 2) - fold(field[1], edge_depth, 1)
    curl_y = fold(field[0], edge_depth, 1) - fold(field[2], edge_rows, 0)
    curl_z = fold(field[1], edge_rows, 0) - fold(field[0], edge_cols, 2)
    return jnp.stack([curl_x, curl_y, curl_z])

def time_weights(moment):
    freq = jnp.arange(NF, dtype=jnp.int32)[:, None]
    depth = jnp.arange(CZ, dtype=jnp.int32)[None, :]
    turns = jnp.mod((2 * freq + 1) * (7 * moment + depth), 64)
    angle = turns.astype(jnp.float32) * (TWO_PI / 64)
    return jnp.concatenate([jnp.cos(angle), -jnp.sin(angle)], axis=0)

def plane_phase(count, offset, length):
    freq = jnp.arange(NF, dtype=jnp.int32)[:, None, None]
    order = jnp.arange(FAR, dtype=jnp.int32)[None, :, None] - FAR // 2
    cell = (offset + jnp.arange(count, dtype=jnp.int32))[None, None, :]
    period = 4 * length * NF
    turns = jnp.mod(order * (2 * cell + 1) * (NF + freq), period)
    angle = turns.astype(jnp.float32) * (TWO_PI / period)
    return (jnp.cos(angle), jnp.sin(angle))

def far_field(lens_real, lens_imag, rows_cos, rows_sin, cols_cos, cols_sin):
    mid_real = jnp.einsum('pfxy,fvy->pfxv', lens_real, cols_cos, precision=HIGHEST) + jnp.einsum('pfxy,fvy->pfxv', lens_imag, cols_sin, precision=HIGHEST)
    mid_imag = jnp.einsum('pfxy,fvy->pfxv', lens_imag, cols_cos, precision=HIGHEST) - jnp.einsum('pfxy,fvy->pfxv', lens_real, cols_sin, precision=HIGHEST)
    far_real = jnp.einsum('fux,pfxv->pfuv', rows_cos, mid_real, precision=HIGHEST) + jnp.einsum('fux,pfxv->pfuv', rows_sin, mid_imag, precision=HIGHEST)
    far_imag = jnp.einsum('fux,pfxv->pfuv', rows_cos, mid_imag, precision=HIGHEST) - jnp.einsum('fux,pfxv->pfuv', rows_sin, mid_real, precision=HIGHEST)
    return (far_real, far_imag)

def far_back(grad_real, grad_imag, rows_cos, rows_sin, cols_cos, cols_sin):
    back_mid_real = jnp.einsum('fux,pfuv->pfxv', rows_cos, grad_real, precision=HIGHEST) - jnp.einsum('fux,pfuv->pfxv', rows_sin, grad_imag, precision=HIGHEST)
    back_mid_imag = jnp.einsum('fux,pfuv->pfxv', rows_sin, grad_real, precision=HIGHEST) + jnp.einsum('fux,pfuv->pfxv', rows_cos, grad_imag, precision=HIGHEST)
    back_real = jnp.einsum('pfxv,fvy->pfxy', back_mid_real, cols_cos, precision=HIGHEST) - jnp.einsum('pfxv,fvy->pfxy', back_mid_imag, cols_sin, precision=HIGHEST)
    back_imag = jnp.einsum('pfxv,fvy->pfxy', back_mid_real, cols_sin, precision=HIGHEST) + jnp.einsum('pfxv,fvy->pfxy', back_mid_imag, cols_cos, precision=HIGHEST)
    return jnp.concatenate([back_real, back_imag], axis=1)

def reference(e_init, h_init, material, eps_table, target):
    inverse = 1.0 / eps_table[material]
    electric, magnetic = (e_init, h_init)
    lens = jnp.zeros((2, 2 * NF, NX, NY), jnp.float32)
    kept = []
    for moment in range(ITERS):
        magnetic = magnetic - COURANT * curl_grid(electric, fold_next)
        curl_mag = curl_grid(magnetic, fold_prev)
        kept.append(curl_mag)
        electric = electric + COURANT * inverse * curl_mag
        lens = lens + jnp.einsum('wz,pxzy->pwxy', time_weights(moment + 1), electric[:2], precision=HIGHEST)
    rows_cos, rows_sin = plane_phase(NX, 0, NX)
    cols_cos, cols_sin = plane_phase(NY, 0, CY)
    far_real, far_imag = far_field(lens[:, :NF], lens[:, NF:], rows_cos, rows_sin, cols_cos, cols_sin)
    intensity = lax.optimization_barrier(jnp.sum(far_real * far_real + far_imag * far_imag, axis=0))
    samples = NF * FAR * FAR
    power = jnp.sum(intensity) / samples
    misfit = intensity / power - target
    spread = jnp.sum(misfit * intensity) / (samples * power)
    slope = 2.0 / power * (misfit - spread)
    back = far_back(2.0 * slope * far_real, 2.0 * slope * far_imag, rows_cos, rows_sin, cols_cos, cols_sin)
    back_electric = jnp.zeros_like(e_init)
    back_magnetic = jnp.zeros_like(h_init)
    accum = jnp.zeros_like(inverse)
    for moment in reversed(range(ITERS)):
        source = jnp.einsum('wz,pwxy->pxzy', time_weights(moment + 1), back, precision=HIGHEST)
        source = jnp.concatenate([source, jnp.zeros_like(source[:1])], axis=0)
        back_electric = back_electric + source
        accum = accum + COURANT * lax.optimization_barrier(jnp.sum(back_electric * kept[moment], axis=0))
        back_magnetic = back_magnetic + COURANT * curl_grid(inverse * back_electric, fold_next)
        back_electric = back_electric - COURANT * curl_grid(back_magnetic, fold_prev)
    gradient = -(inverse * inverse) * accum
    return gradient / jnp.sqrt(jnp.mean(gradient * gradient) + 1e-06)
```

```python
import functools
import math

import jax
import jax.numpy as jnp
import ml_dtypes
import numpy as np
from jax import lax
from jax.experimental import pallas as pl
from jax.experimental.pallas import tpu as pltpu
from jax.sharding import PartitionSpec as P

ITERS = 6
NF = 8
FAR = 64
NMAT = 8
GHOST = ITERS
BACK = ITERS - 1
TWO_PI = 2.0 * math.pi
F32 = jnp.float32
BF16 = jnp.bfloat16
VMEM_BYTES = 56 * 1024 * 1024


def split_table(table):
    high = table.astype(np.float32).astype(ml_dtypes.bfloat16)
    low = (table - high.astype(np.float64)).astype(np.float32).astype(ml_dtypes.bfloat16)
    return high, low


def time_table(depth):
    freq = np.arange(NF)[None, :, None]
    moment = np.arange(1, ITERS + 1)[:, None, None]
    turns = ((2 * freq + 1) * (7 * moment + np.arange(depth)[None, None, :])) % 64
    angle = turns * (TWO_PI / 64)
    return np.concatenate([np.cos(angle), -np.sin(angle)], axis=1)


def lens_table(depth):
    weights = time_table(depth)
    wide = np.stack([weights, weights], axis=2)
    wide = wide.transpose(1, 0, 2, 3).reshape(2 * NF, -1)
    return np.concatenate(split_table(wide), axis=0)


def source_table(depth):
    flat = time_table(depth).transpose(0, 2, 1).reshape(ITERS * depth, 2 * NF)
    high, low = split_table(flat)
    return np.concatenate([high, high, low], axis=1)


def phase(cells, length):
    freq = np.arange(NF)[:, None, None]
    order = np.arange(FAR)[None, :, None] - FAR // 2
    period = 4 * length * NF
    turns = (order * (2 * cells[None, None, :] + 1) * (NF + freq)) % period
    angle = turns * (TWO_PI / period)
    return np.cos(angle), np.sin(angle)


def column_table(tile_cols, width):
    lanes = np.arange(width)
    cells = np.where(lanes >= width - GHOST, lanes - width, lanes)
    used = (lanes < tile_cols + GHOST) | (lanes >= width - GHOST)
    cos, sin = (t * used[None, None, :] for t in phase(cells, tile_cols))
    table = np.concatenate(
        [np.concatenate([cos, sin], axis=2), np.concatenate([-sin, cos], axis=2)], axis=1
    )
    return np.concatenate(split_table(table), axis=1)


def column_twist(count_cols):
    freq = np.arange(NF)[None, :, None]
    order = np.arange(FAR)[None, None, :] - FAR // 2
    place = np.arange(count_cols)[:, None, None]
    angle = ((order * (NF + freq) * place) % 16) * (TWO_PI / 16)
    cos, sin = np.cos(angle), np.sin(angle)
    return np.stack(
        [np.concatenate([cos, cos], axis=2), np.concatenate([sin, -sin], axis=2)]
    ).astype(np.float32)


def row_table(rows):
    table = np.concatenate(phase(np.arange(rows), rows), axis=1)
    high, low = split_table(table)
    return np.concatenate([high, high, low], axis=2)


def row_back_table(rows):
    cells = np.arange(rows + 16) - BACK
    cos, sin = phase(cells, rows)
    return np.stack([cos, sin], axis=1).transpose(0, 1, 3, 2).astype(np.float32)


def split(value):
    high = value.astype(BF16)
    return high, (value - high.astype(F32)).astype(BF16)


def dot(left, right):
    return jnp.dot(left, right, preferred_element_type=F32)


def half_turn(value):
    return pltpu.roll(value, FAR, 1)


def z_index(shape):
    return lax.broadcasted_iota(jnp.int32, shape, 0)


def curl_ahead(x, y, z, y_next, z_next):
    depth, width = x.shape
    last = z_index(x.shape) == depth - 1

    def by_y(v):
        return pltpu.roll(v, width - 1, 1) - v

    def by_z(v):
        return jnp.where(last, 0.0, pltpu.roll(v, depth - 1, 0)) - v

    return (by_y(z) - by_z(y), by_z(x) - (z_next - z), (y_next - y) - by_y(x))


def curl_behind(x, y, z, y_prev, z_prev):
    first = z_index(x.shape) == 0

    def by_y(v):
        return v - pltpu.roll(v, 1, 1)

    def by_z(v):
        return v - jnp.where(first, 0.0, pltpu.roll(v, 1, 0))

    return (by_y(z) - by_z(y), by_z(x) - (z - z_prev), (y - y_prev) - by_y(x))


def lane_mask(width, tile_cols, column, count_cols):
    lane = lax.broadcasted_iota(jnp.int32, (1, width), 1)
    upper = tile_cols + jnp.where(column < count_cols - 1, GHOST, 0)
    lower = width - jnp.where(column > 0, GHOST, 0)
    return jnp.where((lane < upper) | (lane >= lower), 1.0, 0.0)


def row_mask(row, ghost, tile_rows, place, count_rows):
    low = jnp.where(place > 0, 1.0, 0.0)
    high = jnp.where(place < count_rows - 1, 1.0, 0.0)
    return jnp.where(row < ghost, low, jnp.where(row >= ghost + tile_rows, high, 1.0))


def pack_kernel(place, e, h, material, row_a, row_b, col_a, col_b):
    tile_rows, depth, tile_cols = material.shape
    even_x = place[0] % 2 == 0
    even_y = place[1] % 2 == 0
    start_a = jnp.where(even_x, tile_rows - GHOST, 0)
    start_b = jnp.where(even_x, 0, tile_rows - GHOST)
    lane = lax.broadcasted_iota(jnp.int32, (depth, tile_cols), 1)
    for part in range(7):

        def planes(index):
            if part < 3:
                return e[part, index]
            if part < 6:
                return h[part - 3, index]
            return material[index].astype(F32)

        row_a[part] = planes(pl.ds(start_a, GHOST))
        row_b[part] = planes(pl.ds(start_b, GHOST))
        first = jnp.zeros((depth, tile_cols), F32)
        last = first
        for x in range(tile_rows):
            plane = planes(x)
            spot = (lane >= GHOST * x) & (lane < GHOST * (x + 1))
            shift = GHOST * x
            first = jnp.where(spot, pltpu.roll(plane, shift, 1) if shift else plane, first)
            shift = (GHOST * (x + 1)) % tile_cols
            last = jnp.where(spot, pltpu.roll(plane, shift, 1) if shift else plane, last)
        col_a[part] = jnp.where(even_y, last, first)
        col_b[part] = jnp.where(even_y, first, last)


def forward_kernel(
    counts, place, eps, e, h, material, row_a, row_b, col_a, col_b, cor_a, cor_b, weights, table, twist,
    kept, inverse, mid, field, stash, lens,
):
    tile_rows, depth, tile_cols = material.shape
    width = field.shape[3]
    count_rows, count_cols = counts
    i, j = place[0], place[1]
    even_x = i % 2 == 0
    even_y = j % 2 == 0
    far_edge = GHOST + tile_rows
    off_a = jnp.where(even_x, far_edge, 0)
    off_b = jnp.where(even_x, 0, far_edge)
    lane = lax.broadcasted_iota(jnp.int32, (depth, tile_cols), 1)

    def turn(value, shift):
        shift = shift % tile_cols
        return pltpu.roll(value, shift, 1) if shift else value

    def ghosts(right, left, x):
        left = jnp.where(lane >= tile_cols - GHOST, turn(left, -GHOST - GHOST * x), 0.0)
        return jnp.where(lane < GHOST, turn(right, -GHOST * x), left)

    for part in range(7):
        target = field.at[part] if part < 6 else inverse
        if part < 3:
            target[GHOST:far_edge, :, :tile_cols] = e[part]
        elif part < 6:
            target[GHOST:far_edge, :, :tile_cols] = h[part - 3]
        else:
            target[GHOST:far_edge, :, :tile_cols] = material[...].astype(F32)
        target[pl.ds(off_a, GHOST), :, :tile_cols] = row_a[part]
        target[pl.ds(off_b, GHOST), :, :tile_cols] = row_b[part]
        a, b = col_a[part], col_b[part]
        right, left = jnp.where(even_y, a, b), jnp.where(even_y, b, a)
        for x in range(tile_rows):
            target[GHOST + x, :, tile_cols:] = ghosts(right, left, x)
        a, b = cor_a[part], cor_b[part]
        for corner, base, skip in (
            (jnp.where(even_x, b, a), 0, tile_rows - GHOST),
            (jnp.where(even_x, a, b), far_edge, 0),
        ):
            turned = turn(corner, -GHOST * tile_rows)
            right, left = jnp.where(even_y, corner, turned), jnp.where(even_y, turned, corner)
            for x in range(GHOST):
                target[base + x, :, tile_cols:] = ghosts(right, left, skip + x)

    mask = lane_mask(width, tile_cols, j, count_cols)

    def masked(row):
        return (0.5 * row_mask(row, GHOST, tile_rows, i, count_rows)) * mask

    def invert(row, carry):
        index = inverse[row]
        permittivity = jnp.full(index.shape, eps[0], F32)
        for m in range(1, NMAT):
            permittivity = jnp.where(index == float(m), eps[m], permittivity)
        inverse[row] = masked(row) / permittivity
        return carry

    lax.fori_loop(0, tile_rows + 2 * GHOST, invert, 0)

    for n in range(ITERS):

        def magnetic_row(r, carry):
            curl = curl_ahead(field[0, r], field[1, r], field[2, r], field[1, r + 1], field[2, r + 1])
            scale = masked(r)
            for part in range(3):
                field[3 + part, r] = field[3 + part, r] - scale * curl[part]
            return carry

        def electric_row(r, carry):
            curl = curl_behind(field[3, r], field[4, r], field[5, r], field[4, r - 1], field[5, r - 1])
            scale = inverse[r]
            new = []
            for part in range(3):
                value = field[part, r] + scale * curl[part]
                field[part, r] = value
                new.append(value)
            return (curl, new) if carry is None else carry

        def own_rows(q, carry):
            for s in range(2):
                x = 2 * q + s
                curl, new = electric_row(GHOST + x, None)
                for part in range(3):
                    kept[n, part, x] = curl[part][:, :tile_cols]
                for part in range(2):
                    high, low = split(new[part][:, :tile_cols])
                    spot = slice(s * tile_cols, (s + 1) * tile_cols)
                    stash[part, q, 2 * n * depth : (2 * n + 1) * depth, spot] = high
                    stash[part, q, (2 * n + 1) * depth : (2 * n + 2) * depth, spot] = low
            return carry

        last = tile_rows + 2 * GHOST - 1 - n
        lax.fori_loop(n, last, magnetic_row, 0)
        if n + 1 < GHOST:
            lax.fori_loop(n + 1, GHOST, electric_row, 0)
        lax.fori_loop(0, tile_rows // 2, own_rows, 0)
        if last > far_edge:
            lax.fori_loop(far_edge, last, electric_row, 0)

    waves = 2 * NF
    for p in range(2):
        for q in range(tile_rows // 2):
            both = dot(weights[...], stash[p, q])
            both = both[:waves] + both[waves:]
            for s in range(2):
                base = (p * tile_rows + 2 * q + s) * waves
                lens[base : base + waves, :] = both[:, s * tile_cols : (s + 1) * tile_cols]
    planes = 2 * tile_rows
    for f in range(NF):
        real = lens[pl.ds(f, planes, stride=waves), :]
        imag = lens[pl.ds(NF + f, planes, stride=waves), :]
        high, low = split(jnp.concatenate([real, imag], axis=1))
        phases = jnp.concatenate([table[f, :, :tile_cols], table[f, :, width : width + tile_cols]], axis=1)
        both = lax.dot_general(
            jnp.concatenate([high, low], axis=0), phases, (((1,), (1,)), ((), ())), preferred_element_type=F32
        )
        both = both[:planes] + both[planes:]
        both = both[:, : 2 * FAR] + both[:, 2 * FAR :]
        mid[f] = both * twist[0, j, f : f + 1, :] + half_turn(both) * twist[1, j, f : f + 1, :]


def backward_kernel(
    counts, place, own, sibling, target, kept, inverse, rows_far, rows_back, table, twist, weights,
    gradient, squares, mid, far, intensity, back, source, electric, magnetic, scaled, accum,
):
    tile_rows, depth, tile_cols = gradient.shape
    width = inverse.shape[2]
    count_rows, count_cols = counts
    i, j = place[0], place[1]
    samples = NF * FAR * FAR
    wide = 2 * FAR
    for k in range(count_rows // 2):
        near = i ^ (2 * k)
        for block, index in ((own, near), (sibling, near ^ 1)):
            spot = pl.ds(pl.multiple_of(index * tile_rows, 8), tile_rows)
            for p in range(2):
                for f in range(NF):
                    mid[f, spot, p * wide : (p + 1) * wide] = block[k, f, p * tile_rows : (p + 1) * tile_rows, :]

    sign = jnp.where(lax.broadcasted_iota(jnp.int32, (1, wide), 1) < FAR, 1.0, -1.0)
    total = jnp.zeros((FAR, wide), F32)
    for f in range(NF):
        high, low = split(mid[f])
        both = dot(rows_far[f], jnp.concatenate([high, low, high], axis=0))
        level = jnp.zeros((FAR, wide), F32)
        for p in range(2):
            cos = both[:FAR, p * wide : (p + 1) * wide]
            sin = both[FAR:, p * wide : (p + 1) * wide]
            value = cos + sign * half_turn(sin)
            far[f, :, p * wide : (p + 1) * wide] = value
            level = level + value * value
        level = level + half_turn(level)
        intensity[f] = level
        total = total + level
    power = jnp.sum(total, keepdims=True) / (2.0 * samples)
    total = jnp.zeros((FAR, wide), F32)
    for f in range(NF):
        level = intensity[f]
        total = total + (level / power - target[f]) * level
    spread = jnp.sum(total, keepdims=True) / (2.0 * samples * power)

    mask = lane_mask(width, tile_cols, j, count_cols)
    span = rows_back.shape[2] - count_rows * tile_rows + tile_rows
    row = lax.broadcasted_iota(jnp.int32, (2 * span, 1), 0)
    row = jnp.where(row >= span, row - span, row)
    lowest = jnp.where(i > 0, 0, BACK)
    highest = jnp.where(i < count_rows - 1, span, BACK + tile_rows)
    inside = jnp.where((row >= lowest) & (row < highest), 1.0, 0.0)
    waves = 2 * NF
    for f in range(NF):
        slope = 2.0 / power * (intensity[f] / power - target[f] - spread)
        slope = 2.0 * slope
        high, low = split(far[f] * jnp.concatenate([slope, slope], axis=1))
        start = pl.multiple_of(i * tile_rows, 8)
        phases = jnp.concatenate(
            [rows_back[f, 0, pl.ds(start, span), :], rows_back[f, 1, pl.ds(start, span), :]], axis=0
        )
        phase_high, phase_low = split(phases)
        both = dot(phase_high, high) + dot(phase_high, low) + dot(phase_low, high)
        turned = []
        for p in range(2):
            cos = both[:span, p * wide : (p + 1) * wide]
            sin = both[span:, p * wide : (p + 1) * wide]
            value = cos - sign * half_turn(sin)
            turned.append(value * twist[0, j, f : f + 1, :] - half_turn(value) * twist[1, j, f : f + 1, :])
        high, low = split(jnp.concatenate(turned, axis=0))
        left = jnp.concatenate(
            [jnp.concatenate([high, high], axis=1), jnp.concatenate([low, low], axis=1)], axis=0
        )
        both = dot(left, table[f])
        both = (both[: 2 * span] + both[2 * span :]) * inside
        for part in range(2):
            value = both[:, part * width : (part + 1) * width] * mask
            for p in range(2):
                for s in range(width // 128):
                    back[2 * p + s, pl.ds(part * NF + f, span, stride=waves), :] = value[
                        p * span : (p + 1) * span, s * 128 : (s + 1) * 128
                    ]

    ext = tile_rows + 2 * BACK

    def source_row(r, carry):
        spot = pl.ds(pl.multiple_of(r * waves, 8), waves)
        for p in range(2):
            high, low = split(jnp.concatenate([back[2 * p, spot, :], back[2 * p + 1, spot, :]], axis=1))
            both = dot(weights[...], jnp.concatenate([high, low, high], axis=0))
            for n in range(ITERS):
                source[n, p, r] = both[n * depth : (n + 1) * depth]
        return carry

    lax.fori_loop(0, ext, source_row, 0)

    def masked(r):
        return (0.5 * row_mask(r, BACK, tile_rows, i, count_rows)) * mask

    for n in reversed(range(ITERS)):
        first = n == ITERS - 1

        def add_source(r):
            new = []
            for part in range(3):
                if part == 2:
                    value = jnp.zeros((depth, width), F32) if first else electric[2, r]
                elif first:
                    value = source[n, part, r]
                else:
                    value = electric[part, r] + source[n, part, r]
                if n > 0:
                    electric[part, r] = value
                    scaled[part, r] = inverse[r + GHOST - BACK] * value
                new.append(value)
            return new

        def ghost_row(r, carry):
            add_source(r)
            return carry

        def own_row(x, carry):
            new = add_source(BACK + x)
            value = new[0][:, :tile_cols] * kept[n, 0, x]
            for part in range(1, 3):
                value = value + new[part][:, :tile_cols] * kept[n, part, x]
            accum[x] = value if first else accum[x] + value
            return carry

        def magnetic_row(r, carry):
            curl = curl_ahead(scaled[0, r], scaled[1, r], scaled[2, r], scaled[1, r + 1], scaled[2, r + 1])
            scale = masked(r)
            for part in range(3):
                value = scale * curl[part]
                magnetic[part, r] = value if first else magnetic[part, r] + value
            return carry

        def electric_row(r, carry):
            curl = curl_behind(
                magnetic[0, r], magnetic[1, r], magnetic[2, r], magnetic[1, r - 1], magnetic[2, r - 1]
            )
            for part in range(3):
                electric[part, r] = electric[part, r] - curl[part]
            return carry

        low, high = BACK - n, BACK + tile_rows + n
        if n > 0:
            lax.fori_loop(low, BACK, ghost_row, 0)
        lax.fori_loop(0, tile_rows, own_row, 0)
        if n > 0:
            lax.fori_loop(BACK + tile_rows, high, ghost_row, 0)
            lax.fori_loop(low, high - 1, magnetic_row, 0)
            lax.fori_loop(low + 1, high - 1, electric_row, 0)

    total = jnp.zeros((depth, tile_cols), F32)
    for x in range(tile_rows):
        value = inverse[GHOST + x, :, :tile_cols]
        value = -2.0 * (value * value) * accum[x]
        gradient[x] = value
        total = total + value * value
    squares[...] = jnp.broadcast_to(jnp.sum(total, keepdims=True), squares.shape)


def scale_kernel(cells, squares, gradient, result):
    copies = 8 * squares.shape[1]
    total = jnp.sum(squares[...], keepdims=True) / copies
    scale = 1.0 / jnp.sqrt(total / cells + 1e-06)
    for x in range(gradient.shape[0]):
        result[x] = gradient[x] * scale


SMEM = pl.BlockSpec(memory_space=pltpu.SMEM)
VMEM = pl.BlockSpec(memory_space=pltpu.VMEM)


def call(kernel, name, specs, outs, scratch=()):
    return pl.pallas_call(
        kernel,
        name=name,
        in_specs=specs,
        out_specs=jax.tree.map(lambda _: VMEM, outs),
        out_shape=outs,
        scratch_shapes=scratch,
        compiler_params=pltpu.CompilerParams(vmem_limit_bytes=VMEM_BYTES),
    )


def array(*shape):
    return jax.ShapeDtypeStruct(shape, F32)


def even_pairs(count):
    return [(k, k ^ 1) for k in range(count)]


def odd_pairs(count):
    return [(k, k + 1 if k % 2 else k - 1) for k in range(1, count - 1)]


def body(count_rows, count_cols, e_init, h_init, material, eps_table, target):
    tile_rows, depth, tile_cols = material.shape
    width = 2 * tile_cols
    counts = (count_rows, count_cols)
    place = jnp.stack([lax.axis_index("gx"), lax.axis_index("gy")]).astype(jnp.int32)

    edge = array(7, GHOST, depth, tile_cols)
    side = array(7, depth, tile_cols)
    row_a, row_b, col_a, col_b = call(
        pack_kernel, "pack", [SMEM, VMEM, VMEM, VMEM], (edge, edge, side, side)
    )(place, e_init, h_init, material)
    col_a = lax.ppermute(col_a, "gy", even_pairs(count_cols))
    col_b = lax.ppermute(col_b, "gy", odd_pairs(count_cols))
    row_b = lax.ppermute(row_b, "gx", odd_pairs(count_rows))
    row_a = lax.ppermute(row_a, "gx", even_pairs(count_rows))
    used = GHOST * tile_rows
    corner = jnp.concatenate(
        [col_a[..., :used], col_b[..., :used], jnp.zeros(side.shape[:2] + (tile_cols - 2 * used,), F32)], axis=2
    )
    cor_b = lax.ppermute(corner, "gx", odd_pairs(count_rows))
    cor_a = lax.ppermute(corner, "gx", even_pairs(count_rows))

    table = jnp.asarray(column_table(tile_cols, width))
    twist = jnp.asarray(column_twist(count_cols))
    ext = tile_rows + 2 * GHOST
    waves = 2 * NF
    kept, inverse, mid = call(
        functools.partial(forward_kernel, counts),
        "forward",
        [SMEM, SMEM] + [VMEM] * 12,
        (
            array(ITERS, 3, tile_rows, depth, tile_cols),
            array(ext, depth, width),
            array(NF, 2 * tile_rows, 2 * FAR),
        ),
        [
            pltpu.VMEM((6, ext, depth, width), F32),
            pltpu.VMEM((2, tile_rows // 2, 2 * ITERS * depth, 2 * tile_cols), BF16),
            pltpu.VMEM((2 * tile_rows * waves, tile_cols), F32),
        ],
    )(
        place, eps_table, e_init, h_init, material, row_a, row_b, col_a, col_b, cor_a, cor_b,
        jnp.asarray(lens_table(depth)), table, twist,
    )

    whole = mid
    for k in range(1, count_cols):
        whole = whole + lax.ppermute(mid, "gy", [(n, n ^ k) for n in range(count_cols)])
    own = jnp.stack(
        [whole]
        + [lax.ppermute(whole, "gx", [(n, n ^ k) for n in range(count_rows)]) for k in range(2, count_rows, 2)]
    )
    sibling = lax.ppermute(own, "gx", even_pairs(count_rows))

    rows = count_rows * tile_rows
    ext = tile_rows + 2 * BACK
    span = tile_rows + 16
    devices = count_rows * count_cols
    grid = pltpu.VMEM((3, ext, depth, width), F32)
    gradient, squares = call(
        functools.partial(backward_kernel, counts),
        "backward",
        [SMEM] + [VMEM] * 10,
        (array(tile_rows, depth, tile_cols), array(8 * devices, 128)),
        [
            pltpu.VMEM((NF, rows, 4 * FAR), F32),
            pltpu.VMEM((NF, FAR, 4 * FAR), F32),
            pltpu.VMEM((NF, FAR, 2 * FAR), F32),
            pltpu.VMEM((2 * width // 128, span * waves, 128), F32),
            pltpu.VMEM((ITERS, 2, ext, depth, width), F32),
            grid,
            grid,
            grid,
            pltpu.VMEM((tile_rows, depth, tile_cols), F32),
        ],
    )(
        place, own, sibling, jnp.concatenate([target, target], axis=2), kept, inverse,
        jnp.asarray(row_table(rows)), jnp.asarray(row_back_table(rows)), table, twist,
        jnp.asarray(source_table(depth)),
    )
    squares = lax.all_to_all(squares, ("gx", "gy"), 0, 0, tiled=True)
    cells = rows * depth * tile_cols * count_cols
    return call(
        functools.partial(scale_kernel, cells), "scale", [VMEM, VMEM], array(tile_rows, depth, tile_cols)
    )(squares, gradient)


def solution(mesh):
    in_specs = (P(None, "gx", None, "gy"), P(None, "gx", None, "gy"), P("gx", None, "gy"), P(), P())
    out_specs = P("gx", None, "gy")
    part = functools.partial(body, mesh.shape["gx"], mesh.shape["gy"])
    return jax.shard_map(part, mesh=mesh, in_specs=in_specs, out_specs=out_specs, check_vma=False)
```

```python
import functools
import math

import jax
import jax.numpy as jnp
import ml_dtypes
import numpy as np
from jax import lax
from jax.experimental import pallas as pl
from jax.experimental.pallas import tpu as pltpu
from jax.sharding import PartitionSpec as P

ITERS = 6
NF = 8
FAR = 64
NMAT = 8
GHOST = ITERS
BACK = ITERS - 1
TWO_PI = 2.0 * math.pi
F32 = jnp.float32
BF16 = jnp.bfloat16
PAD = 8
VMEM_BYTES = 64 * 1024 * 1024 - 65536
OWN_GROUP = 8
GROUP = 8


def split_table(table):
    high = table.astype(np.float32).astype(ml_dtypes.bfloat16)
    low = (table - high.astype(np.float64)).astype(np.float32).astype(ml_dtypes.bfloat16)
    return high, low


def time_table(depth):
    freq = np.arange(NF)[None, :, None]
    moment = np.arange(1, ITERS + 1)[:, None, None]
    turns = ((2 * freq + 1) * (7 * moment + np.arange(depth)[None, None, :])) % 64
    angle = turns * (TWO_PI / 64)
    return np.concatenate([np.cos(angle), -np.sin(angle)], axis=1)


def lens_table(depth):
    weights = time_table(depth)
    wide = np.stack([weights, weights], axis=2)
    wide = wide.transpose(1, 0, 2, 3).reshape(2 * NF, -1)
    return np.concatenate(split_table(wide), axis=0)


def source_table(depth):
    flat = time_table(depth).transpose(0, 2, 1).reshape(ITERS * depth, 2 * NF)
    high, low = split_table(flat)
    return np.concatenate([high, high, low], axis=1)


def phase(cells, length):
    freq = np.arange(NF)[:, None, None]
    order = np.arange(FAR)[None, :, None] - FAR // 2
    period = 4 * length * NF
    turns = (order * (2 * cells[None, None, :] + 1) * (NF + freq)) % period
    angle = turns * (TWO_PI / period)
    return np.cos(angle), np.sin(angle)


def column_table(tile_cols, width):
    lanes = np.arange(width)
    cells = np.where(lanes >= width - GHOST, lanes - width, lanes)
    used = (lanes < tile_cols + GHOST) | (lanes >= width - GHOST)
    cos, sin = (t * used[None, None, :] for t in phase(cells, tile_cols))
    return np.stack([np.concatenate(split_table(t), axis=1) for t in (cos, sin, -sin)])


def column_blocks(table, target, lanes):
    pairs = []
    for half in range(2):
        for row, col, block in ((0, 0, 0), (0, 1, 1), (1, 0, 2), (1, 1, 0)):
            start = (2 * half + row) * FAR
            pairs.append(
                (
                    table.at[block, :, half * FAR : (half + 1) * FAR, 0:lanes],
                    target.at[:, start : start + FAR, col * lanes : (col + 1) * lanes],
                )
            )
    return pairs


def column_twist(count_cols):
    freq = np.arange(NF)[None, :, None]
    order = np.arange(FAR)[None, None, :] - FAR // 2
    place = np.arange(count_cols)[:, None, None]
    angle = ((order * (NF + freq) * place) % 16) * (TWO_PI / 16)
    cos, sin = np.cos(angle), np.sin(angle)
    return np.stack(
        [np.concatenate([cos, cos], axis=2), np.concatenate([sin, -sin], axis=2)]
    ).astype(np.float32)


def row_table(rows):
    table = np.concatenate(phase(np.arange(rows), rows), axis=1)
    high, low = split_table(table)
    return np.concatenate([high, high, low], axis=2)


def row_back_table(rows):
    cells = np.arange(rows + 16) - BACK
    cos, sin = phase(cells, rows)
    return np.stack([cos, sin], axis=1).transpose(0, 1, 3, 2).astype(np.float32)


def split(value):
    high = value.astype(BF16)
    return high, (value - high.astype(F32)).astype(BF16)


def dot(left, right):
    return jnp.dot(left, right, preferred_element_type=F32)


def half_turn(value):
    return pltpu.roll(value, FAR, 1)


def ahead_y(own, ghost):
    last = lax.broadcasted_iota(jnp.int32, own.shape, 1) == own.shape[1] - 1
    a, b = (pltpu.roll(v, v.shape[1] - 1, 1) for v in (own, ghost))
    return (jnp.where(last, b, a) - own, jnp.where(last, a, b) - ghost)


def behind_y(own, ghost):
    first = lax.broadcasted_iota(jnp.int32, own.shape, 1) == 0
    a, b = (pltpu.roll(v, 1, 1) for v in (own, ghost))
    return (own - jnp.where(first, b, a), ghost - jnp.where(first, a, b))


def depths(ref, shift=0):
    return slice(PAD + shift, ref.shape[3] - PAD + shift)


def curl_ahead(ref, r):
    def row(part, step=0, shift=0):
        return [ref[part, r + step, s, depths(ref, shift), :] for s in range(2)]

    x, y, z = row(0), row(1), row(2)
    y_next, z_next = row(1, 1), row(2, 1)
    x_deep, y_deep = row(0, 0, 1), row(1, 0, 1)
    zy, xy = ahead_y(*z), ahead_y(*x)
    return (
        [zy[s] - (y_deep[s] - y[s]) for s in range(2)],
        [(x_deep[s] - x[s]) - (z_next[s] - z[s]) for s in range(2)],
        [(y_next[s] - y[s]) - xy[s] for s in range(2)],
    )


def curl_behind(ref, r):
    def row(part, step=0, shift=0):
        return [ref[part, r + step, s, depths(ref, shift), :] for s in range(2)]

    x, y, z = row(0), row(1), row(2)
    y_prev, z_prev = row(1, -1), row(2, -1)
    x_deep, y_deep = row(0, 0, -1), row(1, 0, -1)
    zy, xy = behind_y(*z), behind_y(*x)
    return (
        [zy[s] - (y[s] - y_deep[s]) for s in range(2)],
        [(x[s] - x_deep[s]) - (z[s] - z_prev[s]) for s in range(2)],
        [(y[s] - y_prev[s]) - xy[s] for s in range(2)],
    )


def clear_pads(ref):
    for part in range(ref.shape[0]):
        for start in (0, ref.shape[3] - PAD):
            shape = ref.shape[1:3] + (PAD,) + ref.shape[4:]
            ref[part, :, :, start : start + PAD, :] = jnp.zeros(shape, F32)


def sweep(low, high, *steps):
    def group(start, rows):
        stores = []
        for k in range(rows):
            for step in steps:
                stores += step(start + k)
        for ref, index, value in stores:
            ref[index] = value

    whole = (high - low) // GROUP
    if whole:

        def body(k, carry):
            group(low + GROUP * k, GROUP)
            return carry

        lax.fori_loop(0, whole, body, 0)
    if (high - low) % GROUP:
        group(low + GROUP * whole, (high - low) % GROUP)


def copies(pairs, semaphores):
    started = []
    for k, (source, target) in enumerate(pairs):
        started.append(pltpu.make_async_copy(source, target, semaphores.at[k]))
        started[-1].start()
    return started


def ghost_mask(tile_cols, column, count_cols):
    lane = lax.broadcasted_iota(jnp.int32, (1, tile_cols), 1)
    upper = jnp.where(column < count_cols - 1, GHOST, 0)
    lower = tile_cols - jnp.where(column > 0, GHOST, 0)
    return jnp.where((lane < upper) | (lane >= lower), 1.0, 0.0)


def row_mask(row, ghost, tile_rows, place, count_rows):
    low = jnp.where(place > 0, 1.0, 0.0)
    high = jnp.where(place < count_rows - 1, 1.0, 0.0)
    return jnp.where(row < ghost, low, jnp.where(row >= ghost + tile_rows, high, 1.0))


def pack_rows_kernel(e, h, material, rows_a, rows_b, fields, cells, edges, semaphores):
    tile_rows = material.shape[0]
    even = lax.axis_index("gx") % 2 == 0
    last = tile_rows - GHOST
    starts = (jnp.where(even, last, 0), jnp.where(even, 0, last))
    loads = copies([(e, fields.at[0:3]), (h, fields.at[3:6]), (material, cells)], semaphores)
    for load in loads:
        load.wait()
    pairs = [(fields.at[:, pl.ds(starts[1], GHOST)], rows_b.at[0:6])]
    pairs.append((fields.at[:, pl.ds(starts[0], GHOST)], rows_a.at[0:6]))
    sends = copies(pairs, semaphores)
    for k, out in enumerate((rows_a, rows_b)):
        edges[k] = cells[pl.ds(starts[k], GHOST)].astype(F32)
    sends += copies([(edges.at[0], rows_a.at[6]), (edges.at[1], rows_b.at[6])], semaphores.at[2:4])
    for send in sends:
        send.wait()


def pack_columns_kernel(e, h, material, cols_a, cols_b):
    tile_rows, depth, tile_cols = material.shape
    even = lax.axis_index("gy") % 2 == 0
    lane = lax.broadcasted_iota(jnp.int32, (depth, tile_cols), 1)
    used = GHOST * tile_rows
    for pair in range(4):
        first = last = jnp.zeros((depth, tile_cols), F32)
        for part in range(2 * pair, min(2 * pair + 2, 7)):
            for x in range(tile_rows):
                if part < 3:
                    plane = e[part, x]
                elif part < 6:
                    plane = h[part - 3, x]
                else:
                    plane = material[x].astype(F32)
                shift = used * (part % 2) + GHOST * x
                spot = (lane >= shift) & (lane < shift + GHOST)
                first = jnp.where(spot, pltpu.roll(plane, shift, 1) if shift else plane, first)
                shift = (shift + GHOST) % tile_cols
                last = jnp.where(spot, pltpu.roll(plane, shift, 1) if shift else plane, last)
        cols_a[pair] = jnp.where(even, last, first)
        cols_b[pair] = jnp.where(even, first, last)


def forward_kernel(
    counts, eps, weights, twist, e, h, material, row_a, row_b, own_a, own_b, corner_a, corner_b, table,
    kept_out, inverse_out, mid, electric, magnetic, inverse, kept, index, cols, phases, stash, lens, semaphores,
):
    tile_rows, depth, tile_cols = material.shape
    count_rows, count_cols = counts
    i, j = lax.axis_index("gx"), lax.axis_index("gy")
    even_x = i % 2 == 0
    even_y = j % 2 == 0
    far_edge = GHOST + tile_rows
    ext = tile_rows + 2 * GHOST
    spots = [
        pl.ds(jnp.where(even_x, far_edge, 0), GHOST),
        pl.ds(jnp.where(even_x, 0, far_edge), GHOST),
    ]
    own = pl.ds(GHOST, tile_rows)
    inner = pl.ds(PAD, depth)
    pairs = [(material, index)]
    pairs += [(own_a, cols.at[0, 0]), (own_b, cols.at[0, 1]), (corner_a, cols.at[1]), (corner_b, cols.at[2])]
    for part, spot in ((row_a, spots[0]), (row_b, spots[1])):
        pairs.append((part.at[6], inverse.at[spot, 0]))
        pairs.append((part.at[0:3], electric.at[:, spot, 0, inner, :]))
        pairs.append((part.at[3:6], magnetic.at[:, spot, 0, inner, :]))
    pairs.append((e, electric.at[:, own, 0, inner, :]))
    pairs.append((h, magnetic.at[:, own, 0, inner, :]))
    early = len(pairs)
    pairs += column_blocks(table, phases, tile_cols)
    started = copies(pairs, semaphores)
    clear_pads(electric)
    clear_pads(magnetic)
    for copy in started[:early]:
        copy.wait()

    lane = lax.broadcasted_iota(jnp.int32, (depth, tile_cols), 1)
    right_at = jnp.where(even_y, 0, 1)
    left_at = jnp.where(even_y, 1, 0)
    used = GHOST * tile_rows

    def turn(value, shift):
        shift = shift % tile_cols
        return pltpu.roll(value, shift, 1) if shift else value

    inverse[GHOST:far_edge, 0] = index[...].astype(F32)
    for part in range(7):
        for base, block, skip, rows in (
            (GHOST, 0, 0, tile_rows),
            (0, jnp.where(even_x, 2, 1), tile_rows - GHOST, GHOST),
            (far_edge, jnp.where(even_x, 1, 2), 0, GHOST),
        ):
            right = cols[block, right_at, part // 2]
            left = cols[block, left_at, part // 2]
            for x in range(rows):
                shift = used * (part % 2) + GHOST * (skip + x)
                value = jnp.where(lane >= tile_cols - GHOST, turn(left, -GHOST - shift), 0.0)
                value = jnp.where(lane < GHOST, turn(right, -shift), value)
                if part < 6:
                    (electric, magnetic)[part // 3][part % 3, base + x, 1, inner, :] = value
                else:
                    inverse[base + x, 1] = value

    mask = ghost_mask(tile_cols, j, count_cols)

    def masked(row):
        scale = 0.5 * row_mask(row, GHOST, tile_rows, i, count_rows)
        return (scale, scale * mask)

    def invert(row, carry):
        scale = masked(row)
        for s in range(2):
            value = inverse[row, s]
            permittivity = jnp.full(value.shape, eps[0], F32)
            for m in range(1, NMAT):
                permittivity = jnp.where(value == float(m), eps[m], permittivity)
            inverse[row, s] = scale[s] / permittivity
        return carry

    lax.fori_loop(0, ext, invert, 0)
    sends = copies([(inverse, inverse_out)], semaphores)

    for n in range(ITERS):

        def magnetic_row(r):
            curl = curl_ahead(electric, r)
            scale = masked(r)
            stores = []
            for part in range(3):
                for s in range(2):
                    spot = (part, r, s, inner)
                    stores.append((magnetic, spot, magnetic[spot] - scale[s] * curl[part][s]))
            return stores

        def electric_row(r, x=None, q=None, side=0):
            curl = curl_behind(magnetic, r)
            stores = []
            for part in range(3):
                for s in range(2):
                    spot = (part, r, s, inner)
                    value = electric[spot] + inverse[r, s] * curl[part][s]
                    stores.append((electric, spot, value))
                    if s == 0 and x is not None:
                        stores.append((kept, (n, part, x), curl[part][0]))
                        if part < 2:
                            lanes = slice(side * tile_cols, (side + 1) * tile_cols)
                            for k, half in enumerate(split(value)):
                                start = (2 * n + k) * depth
                                stores.append((stash, (part, q, slice(start, start + depth), lanes), half))
            return stores

        def own_rows(k, carry):
            stores = []
            for step in range(OWN_GROUP):
                q, side = OWN_GROUP // 2 * k + step // 2, step % 2
                x = 2 * q + side
                stores += electric_row(GHOST + x, x, q, side)
            for ref, index, value in stores:
                ref[index] = value
            return carry

        sweep(n, ext - 1 - n, magnetic_row)
        sweep(n + 1, GHOST, electric_row)
        lax.fori_loop(0, tile_rows // OWN_GROUP, own_rows, 0)
        sweep(far_edge, ext - 1 - n, electric_row)
        sends += copies([(kept.at[n], kept_out.at[n])], semaphores.at[n + 1 : n + 2])

    waves = 2 * NF
    for p in range(2):
        for q in range(tile_rows // 2):
            value = dot(weights[...], stash[p, q])
            value = value[:waves] + value[waves:]
            for s in range(2):
                base = (p * tile_rows + 2 * q + s) * waves
                lens[base : base + waves, :] = value[:, s * tile_cols : (s + 1) * tile_cols]
    for copy in started[early:]:
        copy.wait()
    planes = 2 * tile_rows
    for f in range(NF):
        real = lens[pl.ds(f, planes, stride=waves), :]
        imag = lens[pl.ds(NF + f, planes, stride=waves), :]
        high, low = split(jnp.concatenate([real, imag], axis=1))
        value = lax.dot_general(
            jnp.concatenate([high, low], axis=0), phases[f], (((1,), (1,)), ((), ())), preferred_element_type=F32
        )
        value = value[:planes] + value[planes:]
        value = value[:, : 2 * FAR] + value[:, 2 * FAR :]
        mid[f] = value * twist[0, j, f : f + 1, :] + half_turn(value) * twist[1, j, f : f + 1, :]
    for copy in sends:
        copy.wait()


def backward_kernel(
    counts, own, sibling, target, twist, weights, kept_in, inverse_in, rows_far, rows_back_in, table_in,
    gradient, squares, mid, far, intensity, back, source, electric, magnetic, scaled, accum,
    kept, inverse, rows_back, table, semaphores,
):
    tile_rows, depth, tile_cols = gradient.shape
    width = 2 * tile_cols
    count_rows, count_cols = counts
    i, j = lax.axis_index("gx"), lax.axis_index("gy")
    samples = NF * FAR * FAR
    wide = 2 * FAR
    pairs = []
    for k in range(count_rows // 2):
        near = i ^ (2 * k)
        for block, index in ((own, near), (sibling, near ^ 1)):
            spot = pl.ds(pl.multiple_of(index * tile_rows, 8), tile_rows)
            for p in range(2):
                pairs.append(
                    (block.at[k, :, p * tile_rows : (p + 1) * tile_rows], mid.at[:, spot, p * wide : (p + 1) * wide])
                )
    first = len(pairs)
    pairs += [(rows_back_in, rows_back)] + column_blocks(table_in, table, width)
    second = len(pairs)
    pairs += [(inverse_in, inverse), (kept_in, kept)]
    started = copies(pairs, semaphores)
    clear_pads(scaled)
    clear_pads(magnetic)
    for copy in started[:first]:
        copy.wait()
    sign = jnp.where(lax.broadcasted_iota(jnp.int32, (1, wide), 1) < FAR, 1.0, -1.0)
    total = jnp.zeros((FAR, wide), F32)
    for f in range(NF):
        high, low = split(mid[f])
        both = dot(rows_far[f], jnp.concatenate([high, low, high], axis=0))
        level = jnp.zeros((FAR, wide), F32)
        for p in range(2):
            cos = both[:FAR, p * wide : (p + 1) * wide]
            sin = both[FAR:, p * wide : (p + 1) * wide]
            value = cos + sign * half_turn(sin)
            far[f, :, p * wide : (p + 1) * wide] = value
            level = level + value * value
        level = level + half_turn(level)
        intensity[f] = level
        total = total + level
    def wanted(f):
        return jnp.concatenate([target[f], target[f]], axis=1)

    power = jnp.sum(total, keepdims=True) / (2.0 * samples)
    total = jnp.zeros((FAR, wide), F32)
    for f in range(NF):
        level = intensity[f]
        total = total + (level / power - wanted(f)) * level
    spread = jnp.sum(total, keepdims=True) / (2.0 * samples * power)

    for copy in started[first:second]:
        copy.wait()
    mask = ghost_mask(tile_cols, j, count_cols)
    span = rows_back.shape[2] - count_rows * tile_rows + tile_rows
    row = lax.broadcasted_iota(jnp.int32, (2 * span, 1), 0)
    row = jnp.where(row >= span, row - span, row)
    lowest = jnp.where(i > 0, 0, BACK)
    highest = jnp.where(i < count_rows - 1, span, BACK + tile_rows)
    inside = jnp.where((row >= lowest) & (row < highest), 1.0, 0.0)
    waves = 2 * NF
    for f in range(NF):
        slope = 2.0 / power * (intensity[f] / power - wanted(f) - spread)
        slope = 2.0 * slope
        high, low = split(far[f] * jnp.concatenate([slope, slope], axis=1))
        start = pl.multiple_of(i * tile_rows, 8)
        phases = jnp.concatenate(
            [rows_back[f, 0, pl.ds(start, span), :], rows_back[f, 1, pl.ds(start, span), :]], axis=0
        )
        phase_high, phase_low = split(phases)
        both = dot(phase_high, high) + dot(phase_high, low) + dot(phase_low, high)
        turned = []
        for p in range(2):
            cos = both[:span, p * wide : (p + 1) * wide]
            sin = both[span:, p * wide : (p + 1) * wide]
            value = cos - sign * half_turn(sin)
            turned.append(value * twist[0, j, f : f + 1, :] - half_turn(value) * twist[1, j, f : f + 1, :])
        high, low = split(jnp.concatenate(turned, axis=0))
        left = jnp.concatenate(
            [jnp.concatenate([high, high], axis=1), jnp.concatenate([low, low], axis=1)], axis=0
        )
        both = dot(left, table[f])
        both = (both[: 2 * span] + both[2 * span :]) * inside
        for part in range(2):
            for s in range(2):
                start = part * width + s * tile_cols
                value = both[:, start : start + tile_cols]
                value = value * mask if s else value
                for p in range(2):
                    back[2 * p + s, pl.ds(part * NF + f, span, stride=waves), :] = value[p * span : (p + 1) * span]

    ext = tile_rows + 2 * BACK

    def source_row(r):
        spot = pl.ds(pl.multiple_of(r * waves, 8), waves)
        stores = []
        for p in range(2):
            high, low = split(jnp.concatenate([back[2 * p, spot, :], back[2 * p + 1, spot, :]], axis=1))
            both = dot(weights[...], jnp.concatenate([high, low, high], axis=0))
            for n in range(ITERS):
                for s in range(2):
                    value = both[n * depth : (n + 1) * depth, s * tile_cols : (s + 1) * tile_cols]
                    stores.append((source, (n, p, r, s), value))
        return stores

    sweep(0, ext, source_row)
    for copy in started[second:]:
        copy.wait()
    inner = pl.ds(PAD, depth)

    def masked(r):
        scale = 0.5 * row_mask(r, BACK, tile_rows, i, count_rows)
        return (scale, scale * mask)

    def take(n, r, value, own):
        stores = []
        total = accum[r - BACK] if own and n < ITERS - 1 else None
        for part in range(3):
            for s in range(2):
                now = value[part][s]
                if part < 2:
                    extra = source[n, part, r, s]
                    now = extra if now is None else now + extra
                elif now is None:
                    now = jnp.zeros((depth, tile_cols), F32)
                if n > 0:
                    stores.append((electric, (part, r, s), now))
                    stores.append((scaled, (part, r, s, inner), inverse[r + GHOST - BACK, s] * now))
                if own and s == 0:
                    term = now * kept[n, part, r - BACK]
                    total = term if total is None else total + term
        if own:
            stores.append((accum, r - BACK, total))
        return stores

    def first_row(own):
        return lambda r: take(ITERS - 1, r, [[None, None]] * 3, own)

    sweep(0, BACK, first_row(False))
    sweep(BACK, BACK + tile_rows, first_row(True))
    sweep(BACK + tile_rows, ext, first_row(False))
    for n in range(ITERS - 1, 0, -1):

        def magnetic_row(r):
            curl = curl_ahead(scaled, r)
            scale = masked(r)
            stores = []
            for part in range(3):
                for s in range(2):
                    spot = (part, r, s, inner)
                    value = scale[s] * curl[part][s]
                    stores.append((magnetic, spot, value if n == ITERS - 1 else value + magnetic[spot]))
            return stores

        def electric_row(own):
            def step(r):
                curl = curl_behind(magnetic, r)
                value = [[electric[part, r, s] - curl[part][s] for s in range(2)] for part in range(3)]
                return take(n - 1, r, value, own)

            return step

        low, high = BACK - n, BACK + tile_rows + n - 1
        sweep(low, high, magnetic_row)
        sweep(low + 1, BACK, electric_row(False))
        sweep(BACK, BACK + tile_rows, electric_row(True))
        sweep(BACK + tile_rows, high, electric_row(False))

    total = jnp.zeros((depth, tile_cols), F32)
    for x in range(tile_rows):
        value = inverse[GHOST + x, 0]
        value = -2.0 * (value * value) * accum[x]
        gradient[x] = value
        total = total + value * value
    squares[...] = jnp.broadcast_to(jnp.sum(total, keepdims=True), squares.shape)


def scale_kernel(cells, squares, gradient, result):
    total = jnp.sum(squares[...], keepdims=True) / squares.shape[1]
    scale = 1.0 / jnp.sqrt(total / cells + 1e-06)
    for x in range(gradient.shape[0]):
        result[x] = gradient[x] * scale


SMEM = pl.BlockSpec(memory_space=pltpu.SMEM)
VMEM = pl.BlockSpec(memory_space=pltpu.VMEM)
HBM = pl.BlockSpec(memory_space=pltpu.HBM)
DMA = pltpu.SemaphoreType.DMA


def call(kernel, name, specs, outs, scratch=(), out_specs=VMEM):
    return pl.pallas_call(
        kernel,
        name=name,
        in_specs=specs,
        out_specs=out_specs,
        out_shape=outs,
        scratch_shapes=scratch,
        compiler_params=pltpu.CompilerParams(vmem_limit_bytes=VMEM_BYTES),
    )


def array(*shape):
    return jax.ShapeDtypeStruct(shape, F32)


def buffer(*shape):
    return pltpu.VMEM(shape, F32)


def even_swaps(count):
    return [(k, k ^ 1) for k in range(count)]


def odd_swaps(count):
    return [(k, k + 1 if k % 2 else k - 1) for k in range(1, count - 1)]


def body(count_rows, count_cols, e_init, h_init, material, eps_table, target):
    tile_rows, depth, tile_cols = material.shape
    counts = (count_rows, count_cols)
    edge = array(7, GHOST, depth, tile_cols)
    side = array(4, depth, tile_cols)
    row_a, row_b = call(
        pack_rows_kernel,
        "pack_rows",
        [HBM] * 3,
        (edge, edge),
        [
            buffer(6, tile_rows, depth, tile_cols),
            pltpu.VMEM((tile_rows, depth, tile_cols), jnp.int32),
            buffer(2, GHOST, depth, tile_cols),
            DMA((4,)),
        ],
        (HBM, HBM),
    )(e_init, h_init, material)
    rows_a, rows_b = even_swaps(count_rows), odd_swaps(count_rows)
    cols_a, cols_b = even_swaps(count_cols), odd_swaps(count_cols)
    row_b = lax.ppermute(row_b, "gx", rows_b)
    row_a = lax.ppermute(row_a, "gx", rows_a)
    col_a, col_b = call(pack_columns_kernel, "pack_columns", [VMEM] * 3, (side, side), (), (VMEM, VMEM))(
        e_init, h_init, material
    )
    col_b = lax.ppermute(col_b, "gy", cols_b)
    col_a = lax.ppermute(col_a, "gy", cols_a)
    corner = jnp.stack([col_a, col_b])
    corner_b = lax.ppermute(corner, "gx", rows_b)
    corner_a = lax.ppermute(corner, "gx", rows_a)

    table = jnp.asarray(column_table(tile_cols, 2 * tile_cols))
    twist = jnp.asarray(column_twist(count_cols))
    ext = tile_rows + 2 * GHOST
    waves = 2 * NF
    kept = (ITERS, 3, tile_rows, depth, tile_cols)
    inverse = (ext, 2, depth, tile_cols)
    kept_out, inverse_out, mid = call(
        functools.partial(forward_kernel, counts),
        "forward",
        [SMEM, VMEM, VMEM] + [HBM] * 10,
        (array(*kept), array(*inverse), array(NF, 2 * tile_rows, 2 * FAR)),
        [
            buffer(3, ext, 2, depth + 2 * PAD, tile_cols),
            buffer(3, ext, 2, depth + 2 * PAD, tile_cols),
            buffer(*inverse),
            buffer(*kept),
            pltpu.VMEM((tile_rows, depth, tile_cols), jnp.int32),
            buffer(3, 2, 4, depth, tile_cols),
            pltpu.VMEM((NF, 4 * FAR, 2 * tile_cols), BF16),
            pltpu.VMEM((2, tile_rows // 2, 2 * ITERS * depth, 2 * tile_cols), BF16),
            buffer(2 * tile_rows * waves, tile_cols),
            DMA((21,)),
        ],
        (HBM, HBM, VMEM),
    )(
        eps_table, jnp.asarray(lens_table(depth)), twist, e_init, h_init, material, row_a, row_b, col_a, col_b,
        corner_a, corner_b, table,
    )

    whole = mid
    for k in range(1, count_cols):
        whole = whole + lax.ppermute(mid, "gy", [(n, n ^ k) for n in range(count_cols)])
    own = jnp.stack(
        [whole]
        + [lax.ppermute(whole, "gx", [(n, n ^ k) for n in range(count_rows)]) for k in range(2, count_rows, 2)]
    )
    sibling = lax.ppermute(own, "gx", rows_a)

    rows = count_rows * tile_rows
    ext = tile_rows + 2 * BACK
    span = tile_rows + 16
    devices = count_rows * count_cols
    grid = (3, ext, 2, depth + 2 * PAD, tile_cols)
    back_rows = row_back_table(rows)
    gradient, squares = call(
        functools.partial(backward_kernel, counts),
        "backward",
        [HBM] * 2 + [VMEM] * 3 + [HBM] * 2 + [VMEM] + [HBM] * 2,
        (array(tile_rows, depth, tile_cols), array(devices, 128)),
        [
            buffer(NF, rows, 4 * FAR),
            buffer(NF, FAR, 4 * FAR),
            buffer(NF, FAR, 2 * FAR),
            buffer(4, span * waves, tile_cols),
            buffer(ITERS, 2, ext, 2, depth, tile_cols),
            buffer(3, ext, 2, depth, tile_cols),
            buffer(*grid),
            buffer(*grid),
            buffer(tile_rows, depth, tile_cols),
            buffer(*kept),
            buffer(*inverse),
            buffer(*back_rows.shape),
            pltpu.VMEM((NF, 4 * FAR, 4 * tile_cols), BF16),
            DMA((2 * count_rows + 11,)),
        ],
        (VMEM, VMEM),
    )(
        own, sibling, target, twist, jnp.asarray(source_table(depth)),
        kept_out, inverse_out, jnp.asarray(row_table(rows)), jnp.asarray(back_rows), table,
    )
    squares = lax.all_to_all(squares, ("gx", "gy"), 0, 0, tiled=True)
    cells = rows * depth * tile_cols * count_cols
    return call(
        functools.partial(scale_kernel, cells), "scale", [VMEM, VMEM], array(tile_rows, depth, tile_cols)
    )(squares, gradient)


def solution(mesh):
    in_specs = (P(None, "gx", None, "gy"), P(None, "gx", None, "gy"), P("gx", None, "gy"), P(), P())
    out_specs = P("gx", None, "gy")
    part = functools.partial(body, mesh.shape["gx"], mesh.shape["gy"])
    return jax.shard_map(part, mesh=mesh, in_specs=in_specs, out_specs=out_specs, check_vma=False)
```

```python
import functools
import math

import jax
import jax.numpy as jnp
import ml_dtypes
import numpy as np
from jax import lax
from jax.experimental import pallas as pl
from jax.experimental.pallas import tpu as pltpu
from jax.sharding import PartitionSpec as P

ITERS = 6
NF = 8
FAR = 64
NMAT = 8
GHOST = ITERS
BACK = ITERS - 1
TWO_PI = 2.0 * math.pi
F32 = jnp.float32
BF16 = jnp.bfloat16
PAD = 8
VMEM_BYTES = 40 * 1024 * 1024
OWN_GROUP = 8
GROUP = 8


def split_table(table):
    high = table.astype(np.float32).astype(ml_dtypes.bfloat16)
    low = (table - high.astype(np.float64)).astype(np.float32).astype(ml_dtypes.bfloat16)
    return high, low


def time_table(depth):
    freq = np.arange(NF)[None, :, None]
    moment = np.arange(1, ITERS + 1)[:, None, None]
    turns = ((2 * freq + 1) * (7 * moment + np.arange(depth)[None, None, :])) % 64
    angle = turns * (TWO_PI / 64)
    return np.concatenate([np.cos(angle), -np.sin(angle)], axis=1)


def lens_table(depth):
    weights = time_table(depth)
    wide = np.stack([weights, weights], axis=2)
    wide = wide.transpose(1, 0, 2, 3).reshape(2 * NF, -1)
    return np.concatenate(split_table(wide), axis=0)


def source_table(depth):
    flat = time_table(depth).transpose(0, 2, 1).reshape(ITERS * depth, 2 * NF)
    high, low = split_table(flat)
    return np.concatenate([high, high, low], axis=1)


def phase(cells, length):
    freq = np.arange(NF)[:, None, None]
    order = np.arange(FAR)[None, :, None] - FAR // 2
    period = 4 * length * NF
    turns = (order * (2 * cells[None, None, :] + 1) * (NF + freq)) % period
    angle = turns * (TWO_PI / period)
    return np.cos(angle), np.sin(angle)


def column_table(tile_cols, width):
    lanes = np.arange(width)
    cells = np.where(lanes >= width - GHOST, lanes - width, lanes)
    used = (lanes < tile_cols + GHOST) | (lanes >= width - GHOST)
    cos, sin = (t * used[None, None, :] for t in phase(cells, tile_cols))
    return np.stack([np.concatenate(split_table(t), axis=1) for t in (cos, sin, -sin)])


def column_blocks(table, target, lanes):
    pairs = []
    for half in range(2):
        for row, col, block in ((0, 0, 0), (0, 1, 1), (1, 0, 2), (1, 1, 0)):
            start = (2 * half + row) * FAR
            pairs.append(
                (
                    table.at[block, :, half * FAR : (half + 1) * FAR, 0:lanes],
                    target.at[:, start : start + FAR, col * lanes : (col + 1) * lanes],
                )
            )
    return pairs


def column_twist(count_cols):
    freq = np.arange(NF)[None, :, None]
    order = np.arange(FAR)[None, None, :] - FAR // 2
    place = np.arange(count_cols)[:, None, None]
    angle = ((order * (NF + freq) * place) % 16) * (TWO_PI / 16)
    cos, sin = np.cos(angle), np.sin(angle)
    return np.stack(
        [np.concatenate([cos, cos], axis=2), np.concatenate([sin, -sin], axis=2)]
    ).astype(np.float32)


def row_table(rows):
    table = np.concatenate(phase(np.arange(rows), rows), axis=1)
    high, low = split_table(table)
    return np.concatenate([high, high, low], axis=2)


def row_back_table(rows):
    cells = np.arange(rows + 16) - BACK
    cos, sin = phase(cells, rows)
    return np.stack([cos, sin], axis=1).transpose(0, 1, 3, 2).astype(np.float32)


def split(value):
    high = value.astype(BF16)
    return high, (value - high.astype(F32)).astype(BF16)


def dot(left, right):
    return jnp.dot(left, right, preferred_element_type=F32)


def half_turn(value):
    return pltpu.roll(value, FAR, 1)


def ahead_y(own, ghost):
    last = lax.broadcasted_iota(jnp.int32, own.shape, 1) == own.shape[1] - 1
    a, b = (pltpu.roll(v, v.shape[1] - 1, 1) for v in (own, ghost))
    return (jnp.where(last, b, a) - own, jnp.where(last, a, b) - ghost)


def behind_y(own, ghost):
    first = lax.broadcasted_iota(jnp.int32, own.shape, 1) == 0
    a, b = (pltpu.roll(v, 1, 1) for v in (own, ghost))
    return (own - jnp.where(first, b, a), ghost - jnp.where(first, a, b))


def depths(ref, shift=0):
    return slice(PAD + shift, ref.shape[3] - PAD + shift)


def curl_ahead(ref, r):
    def row(part, step=0, shift=0):
        return [ref[part, r + step, s, depths(ref, shift), :] for s in range(2)]

    x, y, z = row(0), row(1), row(2)
    y_next, z_next = row(1, 1), row(2, 1)
    x_deep, y_deep = row(0, 0, 1), row(1, 0, 1)
    zy, xy = ahead_y(*z), ahead_y(*x)
    return (
        [zy[s] - (y_deep[s] - y[s]) for s in range(2)],
        [(x_deep[s] - x[s]) - (z_next[s] - z[s]) for s in range(2)],
        [(y_next[s] - y[s]) - xy[s] for s in range(2)],
    )


def curl_behind(ref, r):
    def row(part, step=0, shift=0):
        return [ref[part, r + step, s, depths(ref, shift), :] for s in range(2)]

    x, y, z = row(0), row(1), row(2)
    y_prev, z_prev = row(1, -1), row(2, -1)
    x_deep, y_deep = row(0, 0, -1), row(1, 0, -1)
    zy, xy = behind_y(*z), behind_y(*x)
    return (
        [zy[s] - (y[s] - y_deep[s]) for s in range(2)],
        [(x[s] - x_deep[s]) - (z[s] - z_prev[s]) for s in range(2)],
        [(y[s] - y_prev[s]) - xy[s] for s in range(2)],
    )


def clear_pads(ref):
    for part in range(ref.shape[0]):
        for start in (0, ref.shape[3] - PAD):
            shape = ref.shape[1:3] + (PAD,) + ref.shape[4:]
            ref[part, :, :, start : start + PAD, :] = jnp.zeros(shape, F32)


def sweep(low, high, *steps):
    def group(start, rows):
        stores = []
        for k in range(rows):
            for step in steps:
                stores += step(start + k)
        for ref, index, value in stores:
            ref[index] = value

    whole = (high - low) // GROUP
    if whole:

        def body(k, carry):
            group(low + GROUP * k, GROUP)
            return carry

        lax.fori_loop(0, whole, body, 0)
    if (high - low) % GROUP:
        group(low + GROUP * whole, (high - low) % GROUP)


def copies(pairs, semaphores):
    started = []
    for k, (source, target) in enumerate(pairs):
        started.append(pltpu.make_async_copy(source, target, semaphores.at[k]))
        started[-1].start()
    return started


def ghost_mask(tile_cols, column, count_cols):
    lane = lax.broadcasted_iota(jnp.int32, (1, tile_cols), 1)
    upper = jnp.where(column < count_cols - 1, GHOST, 0)
    lower = tile_cols - jnp.where(column > 0, GHOST, 0)
    return jnp.where((lane < upper) | (lane >= lower), 1.0, 0.0)


def row_mask(row, ghost, tile_rows, place, count_rows):
    low = jnp.where(place > 0, 1.0, 0.0)
    high = jnp.where(place < count_rows - 1, 1.0, 0.0)
    return jnp.where(row < ghost, low, jnp.where(row >= ghost + tile_rows, high, 1.0))


def pack_rows_kernel(e, h, material, rows_a, rows_b, fields, cells, edges, semaphores):
    tile_rows = material.shape[0]
    even = lax.axis_index("gx") % 2 == 0
    last = tile_rows - GHOST
    starts = (jnp.where(even, last, 0), jnp.where(even, 0, last))
    loads = copies([(e, fields.at[0:3]), (h, fields.at[3:6]), (material, cells)], semaphores)
    for load in loads:
        load.wait()
    pairs = [(fields.at[:, pl.ds(starts[1], GHOST)], rows_b.at[0:6])]
    pairs.append((fields.at[:, pl.ds(starts[0], GHOST)], rows_a.at[0:6]))
    sends = copies(pairs, semaphores)
    for k, out in enumerate((rows_a, rows_b)):
        edges[k] = cells[pl.ds(starts[k], GHOST)].astype(F32)
    sends += copies([(edges.at[0], rows_a.at[6]), (edges.at[1], rows_b.at[6])], semaphores.at[2:4])
    for send in sends:
        send.wait()


def pack_columns_kernel(e, h, material, cols_a, cols_b):
    tile_rows, depth, tile_cols = material.shape
    even = lax.axis_index("gy") % 2 == 0
    lane = lax.broadcasted_iota(jnp.int32, (depth, tile_cols), 1)
    used = GHOST * tile_rows
    for pair in range(4):
        first = last = jnp.zeros((depth, tile_cols), F32)
        for part in range(2 * pair, min(2 * pair + 2, 7)):
            for x in range(tile_rows):
                if part < 3:
                    plane = e[part, x]
                elif part < 6:
                    plane = h[part - 3, x]
                else:
                    plane = material[x].astype(F32)
                shift = used * (part % 2) + GHOST * x
                spot = (lane >= shift) & (lane < shift + GHOST)
                first = jnp.where(spot, pltpu.roll(plane, shift, 1) if shift else plane, first)
                shift = (shift + GHOST) % tile_cols
                last = jnp.where(spot, pltpu.roll(plane, shift, 1) if shift else plane, last)
        cols_a[pair] = jnp.where(even, last, first)
        cols_b[pair] = jnp.where(even, first, last)


def forward_kernel(
    counts, eps_in, weights_in, twist_in, e, h, material, row_a, row_b, own_a, own_b, corner_a, corner_b, table,
    kept_out, inverse_out, mid, electric, magnetic, inverse, kept, index, cols, phases, stash, lens, eps, weights, twist, semaphores,
):
    tile_rows, depth, tile_cols = material.shape
    count_rows, count_cols = counts
    i, j = lax.axis_index("gx"), lax.axis_index("gy")
    even_x = i % 2 == 0
    even_y = j % 2 == 0
    far_edge = GHOST + tile_rows
    ext = tile_rows + 2 * GHOST
    spots = [
        pl.ds(jnp.where(even_x, far_edge, 0), GHOST),
        pl.ds(jnp.where(even_x, 0, far_edge), GHOST),
    ]
    own = pl.ds(GHOST, tile_rows)
    inner = pl.ds(PAD, depth)
    pairs = [(material, index)]
    pairs += [(own_a, cols.at[0, 0]), (own_b, cols.at[0, 1]), (corner_a, cols.at[1]), (corner_b, cols.at[2])]
    for part, spot in ((row_a, spots[0]), (row_b, spots[1])):
        pairs.append((part.at[6], inverse.at[spot, 0]))
        pairs.append((part.at[0:3], electric.at[:, spot, 0, inner, :]))
        pairs.append((part.at[3:6], magnetic.at[:, spot, 0, inner, :]))
    pairs.append((e, electric.at[:, own, 0, inner, :]))
    pairs.append((h, magnetic.at[:, own, 0, inner, :]))
    pairs.append((eps_in, eps))
    early = len(pairs)
    pairs += [(weights_in, weights), (twist_in, twist)] + column_blocks(table, phases, tile_cols)
    started = copies(pairs, semaphores)
    clear_pads(electric)
    clear_pads(magnetic)
    for copy in started[:early]:
        copy.wait()

    lane = lax.broadcasted_iota(jnp.int32, (depth, tile_cols), 1)
    right_at = jnp.where(even_y, 0, 1)
    left_at = jnp.where(even_y, 1, 0)
    used = GHOST * tile_rows

    def turn(value, shift):
        shift = shift % tile_cols
        return pltpu.roll(value, shift, 1) if shift else value

    inverse[GHOST:far_edge, 0] = index[...].astype(F32)
    for part in range(7):
        for base, block, skip, rows in (
            (GHOST, 0, 0, tile_rows),
            (0, jnp.where(even_x, 2, 1), tile_rows - GHOST, GHOST),
            (far_edge, jnp.where(even_x, 1, 2), 0, GHOST),
        ):
            right = cols[block, right_at, part // 2]
            left = cols[block, left_at, part // 2]
            for x in range(rows):
                shift = used * (part % 2) + GHOST * (skip + x)
                value = jnp.where(lane >= tile_cols - GHOST, turn(left, -GHOST - shift), 0.0)
                value = jnp.where(lane < GHOST, turn(right, -shift), value)
                if part < 6:
                    (electric, magnetic)[part // 3][part % 3, base + x, 1, inner, :] = value
                else:
                    inverse[base + x, 1] = value

    mask = ghost_mask(tile_cols, j, count_cols)

    def masked(row):
        scale = 0.5 * row_mask(row, GHOST, tile_rows, i, count_rows)
        return (scale, scale * mask)

    def invert(row, carry):
        scale = masked(row)
        for s in range(2):
            value = inverse[row, s]
            permittivity = jnp.full(value.shape, eps[0], F32)
            for m in range(1, NMAT):
                permittivity = jnp.where(value == float(m), eps[m], permittivity)
            inverse[row, s] = scale[s] / permittivity
        return carry

    lax.fori_loop(0, ext, invert, 0)
    sends = copies([(inverse, inverse_out)], semaphores)

    for n in range(ITERS):

        def magnetic_row(r):
            curl = curl_ahead(electric, r)
            scale = masked(r)
            stores = []
            for part in range(3):
                for s in range(2):
                    spot = (part, r, s, inner)
                    stores.append((magnetic, spot, magnetic[spot] - scale[s] * curl[part][s]))
            return stores

        def electric_row(r, x=None, q=None, side=0):
            curl = curl_behind(magnetic, r)
            stores = []
            for part in range(3):
                for s in range(2):
                    spot = (part, r, s, inner)
                    value = electric[spot] + inverse[r, s] * curl[part][s]
                    stores.append((electric, spot, value))
                    if s == 0 and x is not None:
                        stores.append((kept, (n, part, x), curl[part][0]))
                        if part < 2:
                            lanes = slice(side * tile_cols, (side + 1) * tile_cols)
                            for k, half in enumerate(split(value)):
                                start = (2 * n + k) * depth
                                stores.append((stash, (part, q, slice(start, start + depth), lanes), half))
            return stores

        def own_rows(k, carry):
            stores = []
            for step in range(OWN_GROUP):
                q, side = OWN_GROUP // 2 * k + step // 2, step % 2
                x = 2 * q + side
                stores += electric_row(GHOST + x, x, q, side)
            for ref, index, value in stores:
                ref[index] = value
            return carry

        sweep(n, ext - 1 - n, magnetic_row)
        sweep(n + 1, GHOST, electric_row)
        lax.fori_loop(0, tile_rows // OWN_GROUP, own_rows, 0)
        sweep(far_edge, ext - 1 - n, electric_row)
        sends += copies([(kept.at[n], kept_out.at[n])], semaphores.at[n + 1 : n + 2])

    for copy in started[early:]:
        copy.wait()
    waves = 2 * NF
    for p in range(2):
        for q in range(tile_rows // 2):
            value = dot(weights[...], stash[p, q])
            value = value[:waves] + value[waves:]
            for s in range(2):
                base = (p * tile_rows + 2 * q + s) * waves
                lens[base : base + waves, :] = value[:, s * tile_cols : (s + 1) * tile_cols]
    planes = 2 * tile_rows
    for f in range(NF):
        real = lens[pl.ds(f, planes, stride=waves), :]
        imag = lens[pl.ds(NF + f, planes, stride=waves), :]
        high, low = split(jnp.concatenate([real, imag], axis=1))
        value = lax.dot_general(
            jnp.concatenate([high, low], axis=0), phases[f], (((1,), (1,)), ((), ())), preferred_element_type=F32
        )
        value = value[:planes] + value[planes:]
        value = value[:, : 2 * FAR] + value[:, 2 * FAR :]
        mid[f] = value * twist[0, j, f : f + 1, :] + half_turn(value) * twist[1, j, f : f + 1, :]
    for copy in sends:
        copy.wait()


def backward_kernel(
    counts, own, sibling, target, twist, weights, kept_in, inverse_in, rows_far, rows_back_in, table_in,
    gradient, squares, mid, far, intensity, back, source, electric, magnetic, scaled, accum,
    kept, inverse, rows_back, table, semaphores,
):
    tile_rows, depth, tile_cols = gradient.shape
    width = 2 * tile_cols
    count_rows, count_cols = counts
    i, j = lax.axis_index("gx"), lax.axis_index("gy")
    samples = NF * FAR * FAR
    wide = 2 * FAR
    pairs = []
    for k in range(count_rows // 2):
        near = i ^ (2 * k)
        for block, index in ((own, near), (sibling, near ^ 1)):
            spot = pl.ds(pl.multiple_of(index * tile_rows, 8), tile_rows)
            for p in range(2):
                pairs.append(
                    (block.at[k, :, p * tile_rows : (p + 1) * tile_rows], mid.at[:, spot, p * wide : (p + 1) * wide])
                )
    first = len(pairs)
    pairs += [(rows_back_in, rows_back)] + column_blocks(table_in, table, width)
    second = len(pairs)
    pairs += [(inverse_in, inverse), (kept_in, kept)]
    started = copies(pairs, semaphores)
    clear_pads(scaled)
    clear_pads(magnetic)
    for copy in started[:first]:
        copy.wait()
    sign = jnp.where(lax.broadcasted_iota(jnp.int32, (1, wide), 1) < FAR, 1.0, -1.0)
    total = jnp.zeros((FAR, wide), F32)
    for f in range(NF):
        high, low = split(mid[f])
        both = dot(rows_far[f], jnp.concatenate([high, low, high], axis=0))
        level = jnp.zeros((FAR, wide), F32)
        for p in range(2):
            cos = both[:FAR, p * wide : (p + 1) * wide]
            sin = both[FAR:, p * wide : (p + 1) * wide]
            value = cos + sign * half_turn(sin)
            far[f, :, p * wide : (p + 1) * wide] = value
            level = level + value * value
        level = level + half_turn(level)
        intensity[f] = level
        total = total + level
    def wanted(f):
        return jnp.concatenate([target[f], target[f]], axis=1)

    power = jnp.sum(total, keepdims=True) / (2.0 * samples)
    total = jnp.zeros((FAR, wide), F32)
    for f in range(NF):
        level = intensity[f]
        total = total + (level / power - wanted(f)) * level
    spread = jnp.sum(total, keepdims=True) / (2.0 * samples * power)

    for copy in started[first:second]:
        copy.wait()
    mask = ghost_mask(tile_cols, j, count_cols)
    span = rows_back.shape[2] - count_rows * tile_rows + tile_rows
    row = lax.broadcasted_iota(jnp.int32, (2 * span, 1), 0)
    row = jnp.where(row >= span, row - span, row)
    lowest = jnp.where(i > 0, 0, BACK)
    highest = jnp.where(i < count_rows - 1, span, BACK + tile_rows)
    inside = jnp.where((row >= lowest) & (row < highest), 1.0, 0.0)
    waves = 2 * NF
    for f in range(NF):
        slope = 2.0 / power * (intensity[f] / power - wanted(f) - spread)
        slope = 2.0 * slope
        high, low = split(far[f] * jnp.concatenate([slope, slope], axis=1))
        start = pl.multiple_of(i * tile_rows, 8)
        phases = jnp.concatenate(
            [rows_back[f, 0, pl.ds(start, span), :], rows_back[f, 1, pl.ds(start, span), :]], axis=0
        )
        phase_high, phase_low = split(phases)
        both = dot(phase_high, high) + dot(phase_high, low) + dot(phase_low, high)
        turned = []
        for p in range(2):
            cos = both[:span, p * wide : (p + 1) * wide]
            sin = both[span:, p * wide : (p + 1) * wide]
            value = cos - sign * half_turn(sin)
            turned.append(value * twist[0, j, f : f + 1, :] - half_turn(value) * twist[1, j, f : f + 1, :])
        high, low = split(jnp.concatenate(turned, axis=0))
        left = jnp.concatenate(
            [jnp.concatenate([high, high], axis=1), jnp.concatenate([low, low], axis=1)], axis=0
        )
        both = dot(left, table[f])
        both = (both[: 2 * span] + both[2 * span :]) * inside
        for part in range(2):
            for s in range(2):
                start = part * width + s * tile_cols
                value = both[:, start : start + tile_cols]
                value = value * mask if s else value
                for p in range(2):
                    back[2 * p + s, pl.ds(part * NF + f, span, stride=waves), :] = value[p * span : (p + 1) * span]

    ext = tile_rows + 2 * BACK

    def source_row(r):
        spot = pl.ds(pl.multiple_of(r * waves, 8), waves)
        stores = []
        for p in range(2):
            high, low = split(jnp.concatenate([back[2 * p, spot, :], back[2 * p + 1, spot, :]], axis=1))
            both = dot(weights[...], jnp.concatenate([high, low, high], axis=0))
            for n in range(ITERS):
                for s in range(2):
                    value = both[n * depth : (n + 1) * depth, s * tile_cols : (s + 1) * tile_cols]
                    stores.append((source, (n, p, r, s), value))
        return stores

    sweep(0, ext, source_row)
    for copy in started[second:]:
        copy.wait()
    inner = pl.ds(PAD, depth)

    def masked(r):
        scale = 0.5 * row_mask(r, BACK, tile_rows, i, count_rows)
        return (scale, scale * mask)

    def take(n, r, value, own):
        stores = []
        total = accum[r - BACK] if own and n < ITERS - 1 else None
        for part in range(3):
            for s in range(2):
                now = value[part][s]
                if part < 2:
                    extra = source[n, part, r, s]
                    now = extra if now is None else now + extra
                elif now is None:
                    now = jnp.zeros((depth, tile_cols), F32)
                if n > 0:
                    stores.append((electric, (part, r, s), now))
                    stores.append((scaled, (part, r, s, inner), inverse[r + GHOST - BACK, s] * now))
                if own and s == 0:
                    term = now * kept[n, part, r - BACK]
                    total = term if total is None else total + term
        if own:
            stores.append((accum, r - BACK, total))
        return stores

    def first_row(own):
        return lambda r: take(ITERS - 1, r, [[None, None]] * 3, own)

    sweep(0, BACK, first_row(False))
    sweep(BACK, BACK + tile_rows, first_row(True))
    sweep(BACK + tile_rows, ext, first_row(False))
    for n in range(ITERS - 1, 0, -1):

        def magnetic_row(r):
            curl = curl_ahead(scaled, r)
            scale = masked(r)
            stores = []
            for part in range(3):
                for s in range(2):
                    spot = (part, r, s, inner)
                    value = scale[s] * curl[part][s]
                    stores.append((magnetic, spot, value if n == ITERS - 1 else value + magnetic[spot]))
            return stores

        def electric_row(own):
            def step(r):
                curl = curl_behind(magnetic, r)
                value = [[electric[part, r, s] - curl[part][s] for s in range(2)] for part in range(3)]
                return take(n - 1, r, value, own)

            return step

        low, high = BACK - n, BACK + tile_rows + n - 1
        sweep(low, high, magnetic_row)
        sweep(low + 1, BACK, electric_row(False))
        sweep(BACK, BACK + tile_rows, electric_row(True))
        sweep(BACK + tile_rows, high, electric_row(False))

    total = jnp.zeros((depth, tile_cols), F32)
    for x in range(tile_rows):
        value = inverse[GHOST + x, 0]
        value = -2.0 * (value * value) * accum[x]
        gradient[x] = value
        total = total + value * value
    squares[...] = jnp.broadcast_to(jnp.sum(total, keepdims=True), squares.shape)


def scale_kernel(cells, squares, gradient, result):
    total = jnp.sum(squares[...], keepdims=True) / squares.shape[1]
    scale = 1.0 / jnp.sqrt(total / cells + 1e-06)
    for x in range(gradient.shape[0]):
        result[x] = gradient[x] * scale


VMEM = pl.BlockSpec(memory_space=pltpu.VMEM)
HBM = pl.BlockSpec(memory_space=pltpu.HBM)
ANY = pl.BlockSpec(memory_space=pl.ANY)
DMA = pltpu.SemaphoreType.DMA


def call(kernel, name, specs, outs, scratch=(), out_specs=VMEM):
    return pl.pallas_call(
        kernel,
        name=name,
        in_specs=specs,
        out_specs=out_specs,
        out_shape=outs,
        scratch_shapes=scratch,
        compiler_params=pltpu.CompilerParams(vmem_limit_bytes=VMEM_BYTES),
    )


def array(*shape):
    return jax.ShapeDtypeStruct(shape, F32)


def buffer(*shape):
    return pltpu.VMEM(shape, F32)


def even_swaps(count):
    return [(k, k ^ 1) for k in range(count)]


def odd_swaps(count):
    return [(k, k + 1 if k % 2 else k - 1) for k in range(1, count - 1)]


def body(count_rows, count_cols, e_init, h_init, material, eps_table, target):
    tile_rows, depth, tile_cols = material.shape
    counts = (count_rows, count_cols)
    edge = array(7, GHOST, depth, tile_cols)
    side = array(4, depth, tile_cols)
    row_a, row_b = call(
        pack_rows_kernel,
        "pack_rows",
        [HBM] * 3,
        (edge, edge),
        [
            buffer(6, tile_rows, depth, tile_cols),
            pltpu.VMEM((tile_rows, depth, tile_cols), jnp.int32),
            buffer(2, GHOST, depth, tile_cols),
            DMA((4,)),
        ],
        (HBM, HBM),
    )(e_init, h_init, material)
    rows_a, rows_b = even_swaps(count_rows), odd_swaps(count_rows)
    cols_a, cols_b = even_swaps(count_cols), odd_swaps(count_cols)
    row_b = lax.ppermute(row_b, "gx", rows_b)
    row_a = lax.ppermute(row_a, "gx", rows_a)
    col_a, col_b = call(pack_columns_kernel, "pack_columns", [VMEM] * 3, (side, side), (), (VMEM, VMEM))(
        e_init, h_init, material
    )
    col_b = lax.ppermute(col_b, "gy", cols_b)
    col_a = lax.ppermute(col_a, "gy", cols_a)
    corner = jnp.stack([col_a, col_b])
    corner_b = lax.ppermute(corner, "gx", rows_b)
    corner_a = lax.ppermute(corner, "gx", rows_a)

    table = jnp.asarray(column_table(tile_cols, 2 * tile_cols))
    twist = jnp.asarray(column_twist(count_cols))
    weights = jnp.asarray(lens_table(depth))
    ext = tile_rows + 2 * GHOST
    waves = 2 * NF
    kept = (ITERS, 3, tile_rows, depth, tile_cols)
    inverse = (ext, 2, depth, tile_cols)
    kept_out, inverse_out, mid = call(
        functools.partial(forward_kernel, counts),
        "forward",
        [HBM] * 8 + [ANY] * 4 + [HBM],
        (array(*kept), array(*inverse), array(NF, 2 * tile_rows, 2 * FAR)),
        [
            buffer(3, ext, 2, depth + 2 * PAD, tile_cols),
            buffer(3, ext, 2, depth + 2 * PAD, tile_cols),
            buffer(*inverse),
            buffer(*kept),
            pltpu.VMEM((tile_rows, depth, tile_cols), jnp.int32),
            buffer(3, 2, 4, depth, tile_cols),
            pltpu.VMEM((NF, 4 * FAR, 2 * tile_cols), BF16),
            pltpu.VMEM((2, tile_rows // 2, 2 * ITERS * depth, 2 * tile_cols), BF16),
            buffer(2 * tile_rows * waves, tile_cols),
            pltpu.SMEM(eps_table.shape, F32),
            pltpu.VMEM(weights.shape, BF16),
            buffer(*twist.shape),
            DMA((24,)),
        ],
        (HBM, HBM, VMEM),
    )(
        eps_table, weights, twist, e_init, h_init, material, row_a, row_b, col_a, col_b,
        corner_a, corner_b, table,
    )

    whole = mid
    for k in range(1, count_cols):
        whole = whole + lax.ppermute(mid, "gy", [(n, n ^ k) for n in range(count_cols)])
    own = jnp.stack(
        [whole]
        + [lax.ppermute(whole, "gx", [(n, n ^ k) for n in range(count_rows)]) for k in range(2, count_rows, 2)]
    )
    sibling = lax.ppermute(own, "gx", rows_a)

    rows = count_rows * tile_rows
    ext = tile_rows + 2 * BACK
    span = tile_rows + 16
    devices = count_rows * count_cols
    grid = (3, ext, 2, depth + 2 * PAD, tile_cols)
    back_rows = row_back_table(rows)
    gradient, squares = call(
        functools.partial(backward_kernel, counts),
        "backward",
        [ANY] * 2 + [VMEM] * 3 + [HBM] * 2 + [VMEM] + [HBM] * 2,
        (array(tile_rows, depth, tile_cols), array(devices, 128)),
        [
            buffer(NF, rows, 4 * FAR),
            buffer(NF, FAR, 4 * FAR),
            buffer(NF, FAR, 2 * FAR),
            buffer(4, span * waves, tile_cols),
            buffer(ITERS, 2, ext, 2, depth, tile_cols),
            buffer(3, ext, 2, depth, tile_cols),
            buffer(*grid),
            buffer(*grid),
            buffer(tile_rows, depth, tile_cols),
            buffer(*kept),
            buffer(*inverse),
            buffer(*back_rows.shape),
            pltpu.VMEM((NF, 4 * FAR, 4 * tile_cols), BF16),
            DMA((2 * count_rows + 11,)),
        ],
        (VMEM, VMEM),
    )(
        own, sibling, target, twist, jnp.asarray(source_table(depth)),
        kept_out, inverse_out, jnp.asarray(row_table(rows)), jnp.asarray(back_rows), table,
    )
    squares = lax.all_to_all(squares, ("gx", "gy"), 0, 0, tiled=True)
    cells = rows * depth * tile_cols * count_cols
    return call(
        functools.partial(scale_kernel, cells), "scale", [VMEM, VMEM], array(tile_rows, depth, tile_cols)
    )(squares, gradient)


def solution(mesh):
    in_specs = (P(None, "gx", None, "gy"), P(None, "gx", None, "gy"), P("gx", None, "gy"), P(), P())
    out_specs = P("gx", None, "gy")
    part = functools.partial(body, mesh.shape["gx"], mesh.shape["gy"])
    return jax.shard_map(part, mesh=mesh, in_specs=in_specs, out_specs=out_specs, check_vma=False)
```

```python
import functools
import math

import jax
import jax.numpy as jnp
import ml_dtypes
import numpy as np
from jax import lax
from jax.experimental import pallas as pl
from jax.experimental.pallas import tpu as pltpu
from jax.sharding import PartitionSpec as P

ITERS = 6
NF = 8
FAR = 64
NMAT = 8
GHOST = ITERS
BACK = ITERS - 1
TWO_PI = 2.0 * math.pi
F32 = jnp.float32
BF16 = jnp.bfloat16
PAD = 8
VMEM_BYTES = 40 * 1024 * 1024
OWN_GROUP = 8
GROUP = 8


def split_table(table):
    high = table.astype(np.float32).astype(ml_dtypes.bfloat16)
    low = (table - high.astype(np.float64)).astype(np.float32).astype(ml_dtypes.bfloat16)
    return high, low


def time_table(depth):
    freq = np.arange(NF)[None, :, None]
    moment = np.arange(1, ITERS + 1)[:, None, None]
    turns = ((2 * freq + 1) * (7 * moment + np.arange(depth)[None, None, :])) % 64
    angle = turns * (TWO_PI / 64)
    return np.concatenate([np.cos(angle), -np.sin(angle)], axis=1)


def source_table(depth):
    flat = time_table(depth).transpose(0, 2, 1).reshape(ITERS * depth, 2 * NF)
    high, low = split_table(flat)
    return np.concatenate([high, high, low], axis=1)


def phase(cells, length):
    freq = np.arange(NF)[:, None, None]
    order = np.arange(FAR)[None, :, None] - FAR // 2
    period = 4 * length * NF
    turns = (order * (2 * cells[None, None, :] + 1) * (NF + freq)) % period
    angle = turns * (TWO_PI / period)
    return np.cos(angle), np.sin(angle)


def column_table(tile_cols, width):
    lanes = np.arange(width)
    cells = np.where(lanes >= width - GHOST, lanes - width, lanes)
    used = (lanes < tile_cols + GHOST) | (lanes >= width - GHOST)
    cos, sin = (t * used[None, None, :] for t in phase(cells, tile_cols))
    return np.stack([np.concatenate(split_table(t), axis=1) for t in (cos, sin, -sin)])


def column_blocks(table, target, lanes):
    pairs = []
    for half in range(2):
        for row, col, block in ((0, 0, 0), (0, 1, 1), (1, 0, 2), (1, 1, 0)):
            start = (2 * half + row) * FAR
            pairs.append(
                (
                    table.at[block, :, half * FAR : (half + 1) * FAR, 0:lanes],
                    target.at[:, start : start + FAR, col * lanes : (col + 1) * lanes],
                )
            )
    return pairs


def column_twist(count_cols):
    freq = np.arange(NF)[None, :, None]
    order = np.arange(FAR)[None, None, :] - FAR // 2
    place = np.arange(count_cols)[:, None, None]
    angle = ((order * (NF + freq) * place) % 16) * (TWO_PI / 16)
    cos, sin = np.cos(angle), np.sin(angle)
    return np.stack(
        [np.concatenate([cos, cos], axis=2), np.concatenate([sin, -sin], axis=2)]
    ).astype(np.float32)


def row_table(rows):
    table = np.concatenate(phase(np.arange(rows), rows), axis=1)
    high, low = split_table(table)
    return np.concatenate([high, high, low], axis=2)


def row_back_table(rows):
    cells = np.arange(rows + 16) - BACK
    cos, sin = phase(cells, rows)
    return np.stack([cos, sin], axis=1).transpose(0, 1, 3, 2).astype(np.float32)


def split(value):
    high = value.astype(BF16)
    return high, (value - high.astype(F32)).astype(BF16)


def dot(left, right):
    return jnp.dot(left, right, preferred_element_type=F32)


def lens_weights(depth):
    shape = (2 * NF, 2 * ITERS * depth)
    row = lax.broadcasted_iota(jnp.int32, shape, 0)
    lane = lax.broadcasted_iota(jnp.int32, shape, 1)
    moment = lane // (2 * depth) + 1
    turns = (2 * (row % NF) + 1) * (7 * moment + lane % depth)
    turns = (turns + jnp.where(row < NF, 0, 16)) % 64
    return jnp.concatenate(split(jnp.cos(turns.astype(F32) * (TWO_PI / 64))), axis=0)


def tile_twist(j):
    shape = (NF, 2 * FAR)
    freq = lax.broadcasted_iota(jnp.int32, shape, 0)
    lane = lax.broadcasted_iota(jnp.int32, shape, 1)
    turns = ((lane % FAR + FAR // 2) * (NF + freq) * j) % 16
    angle = turns.astype(F32) * (TWO_PI / 16)
    return jnp.cos(angle), jnp.where(lane < FAR, 1.0, -1.0) * jnp.sin(angle)


def half_turn(value):
    return pltpu.roll(value, FAR, 1)


def ahead_y(own, ghost):
    last = lax.broadcasted_iota(jnp.int32, own.shape, 1) == own.shape[1] - 1
    a, b = (pltpu.roll(v, v.shape[1] - 1, 1) for v in (own, ghost))
    return (jnp.where(last, b, a) - own, jnp.where(last, a, b) - ghost)


def behind_y(own, ghost):
    first = lax.broadcasted_iota(jnp.int32, own.shape, 1) == 0
    a, b = (pltpu.roll(v, 1, 1) for v in (own, ghost))
    return (own - jnp.where(first, b, a), ghost - jnp.where(first, a, b))


def depths(ref, shift=0):
    return slice(PAD + shift, ref.shape[3] - PAD + shift)


def curl_ahead(ref, r):
    def row(part, step=0, shift=0):
        return [ref[part, r + step, s, depths(ref, shift), :] for s in range(2)]

    x, y, z = row(0), row(1), row(2)
    y_next, z_next = row(1, 1), row(2, 1)
    x_deep, y_deep = row(0, 0, 1), row(1, 0, 1)
    zy, xy = ahead_y(*z), ahead_y(*x)
    return (
        [zy[s] - (y_deep[s] - y[s]) for s in range(2)],
        [(x_deep[s] - x[s]) - (z_next[s] - z[s]) for s in range(2)],
        [(y_next[s] - y[s]) - xy[s] for s in range(2)],
    )


def curl_behind(ref, r):
    def row(part, step=0, shift=0):
        return [ref[part, r + step, s, depths(ref, shift), :] for s in range(2)]

    x, y, z = row(0), row(1), row(2)
    y_prev, z_prev = row(1, -1), row(2, -1)
    x_deep, y_deep = row(0, 0, -1), row(1, 0, -1)
    zy, xy = behind_y(*z), behind_y(*x)
    return (
        [zy[s] - (y[s] - y_deep[s]) for s in range(2)],
        [(x[s] - x_deep[s]) - (z[s] - z_prev[s]) for s in range(2)],
        [(y[s] - y_prev[s]) - xy[s] for s in range(2)],
    )


def clear_pads(ref):
    for part in range(ref.shape[0]):
        for start in (0, ref.shape[3] - PAD):
            shape = ref.shape[1:3] + (PAD,) + ref.shape[4:]
            ref[part, :, :, start : start + PAD, :] = jnp.zeros(shape, F32)


def sweep(low, high, *steps):
    def group(start, rows):
        stores = []
        for k in range(rows):
            for step in steps:
                stores += step(start + k)
        for ref, index, value in stores:
            ref[index] = value

    whole = (high - low) // GROUP
    if whole:

        def body(k, carry):
            group(low + GROUP * k, GROUP)
            return carry

        lax.fori_loop(0, whole, body, 0)
    if (high - low) % GROUP:
        group(low + GROUP * whole, (high - low) % GROUP)


def copies(pairs, semaphores):
    started = []
    for k, (source, target) in enumerate(pairs):
        started.append(pltpu.make_async_copy(source, target, semaphores.at[k]))
        started[-1].start()
    return started


def ghost_mask(tile_cols, column, count_cols):
    lane = lax.broadcasted_iota(jnp.int32, (1, tile_cols), 1)
    upper = jnp.where(column < count_cols - 1, GHOST, 0)
    lower = tile_cols - jnp.where(column > 0, GHOST, 0)
    return jnp.where((lane < upper) | (lane >= lower), 1.0, 0.0)


def row_mask(row, ghost, tile_rows, place, count_rows):
    low = jnp.where(place > 0, 1.0, 0.0)
    high = jnp.where(place < count_rows - 1, 1.0, 0.0)
    return jnp.where(row < ghost, low, jnp.where(row >= ghost + tile_rows, high, 1.0))


def pack_rows_kernel(e, h, material, rows_a, rows_b, fields, cells, edges, semaphores):
    tile_rows = material.shape[0]
    even = lax.axis_index("gx") % 2 == 0
    last = tile_rows - GHOST
    starts = (jnp.where(even, last, 0), jnp.where(even, 0, last))
    loads = copies([(e, fields.at[0:3]), (h, fields.at[3:6]), (material, cells)], semaphores)
    for load in loads:
        load.wait()
    pairs = [(fields.at[:, pl.ds(starts[1], GHOST)], rows_b.at[0:6])]
    pairs.append((fields.at[:, pl.ds(starts[0], GHOST)], rows_a.at[0:6]))
    sends = copies(pairs, semaphores)
    for k, out in enumerate((rows_a, rows_b)):
        edges[k] = cells[pl.ds(starts[k], GHOST)].astype(F32)
    sends += copies([(edges.at[0], rows_a.at[6]), (edges.at[1], rows_b.at[6])], semaphores.at[2:4])
    for send in sends:
        send.wait()


def pack_columns_kernel(e, h, material, cols_a, cols_b):
    tile_rows, depth, tile_cols = material.shape
    even = lax.axis_index("gy") % 2 == 0
    lane = lax.broadcasted_iota(jnp.int32, (depth, tile_cols), 1)
    used = GHOST * tile_rows
    for pair in range(4):
        first = last = jnp.zeros((depth, tile_cols), F32)
        for part in range(2 * pair, min(2 * pair + 2, 7)):
            for x in range(tile_rows):
                if part < 3:
                    plane = e[part, x]
                elif part < 6:
                    plane = h[part - 3, x]
                else:
                    plane = material[x].astype(F32)
                shift = used * (part % 2) + GHOST * x
                spot = (lane >= shift) & (lane < shift + GHOST)
                first = jnp.where(spot, pltpu.roll(plane, shift, 1) if shift else plane, first)
                shift = (shift + GHOST) % tile_cols
                last = jnp.where(spot, pltpu.roll(plane, shift, 1) if shift else plane, last)
        cols_a[pair] = jnp.where(even, last, first)
        cols_b[pair] = jnp.where(even, first, last)


def forward_kernel(
    counts, eps_in, e, h, material, row_a, row_b, own_a, own_b, corner_a, corner_b, table,
    kept_out, inverse_out, mid, electric, magnetic, inverse, kept, index, cols, phases, stash, lens, eps, semaphores,
):
    tile_rows, depth, tile_cols = material.shape
    count_rows, count_cols = counts
    i, j = lax.axis_index("gx"), lax.axis_index("gy")
    even_x = i % 2 == 0
    even_y = j % 2 == 0
    far_edge = GHOST + tile_rows
    ext = tile_rows + 2 * GHOST
    spots = [
        pl.ds(jnp.where(even_x, far_edge, 0), GHOST),
        pl.ds(jnp.where(even_x, 0, far_edge), GHOST),
    ]
    own = pl.ds(GHOST, tile_rows)
    inner = pl.ds(PAD, depth)
    pairs = [(material, index)]
    pairs += [(own_a, cols.at[0, 0]), (own_b, cols.at[0, 1]), (corner_a, cols.at[1]), (corner_b, cols.at[2])]
    for part, spot in ((row_a, spots[0]), (row_b, spots[1])):
        pairs.append((part.at[6], inverse.at[spot, 0]))
        pairs.append((part.at[0:3], electric.at[:, spot, 0, inner, :]))
        pairs.append((part.at[3:6], magnetic.at[:, spot, 0, inner, :]))
    pairs.append((e, electric.at[:, own, 0, inner, :]))
    pairs.append((h, magnetic.at[:, own, 0, inner, :]))
    pairs.append((eps_in, eps))
    early = len(pairs)
    pairs += column_blocks(table, phases, tile_cols)
    started = copies(pairs, semaphores)
    clear_pads(electric)
    clear_pads(magnetic)
    weights = lens_weights(depth)
    twist = tile_twist(j)
    for copy in started[:early]:
        copy.wait()

    lane = lax.broadcasted_iota(jnp.int32, (depth, tile_cols), 1)
    right_at = jnp.where(even_y, 0, 1)
    left_at = jnp.where(even_y, 1, 0)
    used = GHOST * tile_rows

    def turn(value, shift):
        shift = shift % tile_cols
        return pltpu.roll(value, shift, 1) if shift else value

    inverse[GHOST:far_edge, 0] = index[...].astype(F32)
    for part in range(7):
        for base, block, skip, rows in (
            (GHOST, 0, 0, tile_rows),
            (0, jnp.where(even_x, 2, 1), tile_rows - GHOST, GHOST),
            (far_edge, jnp.where(even_x, 1, 2), 0, GHOST),
        ):
            right = cols[block, right_at, part // 2]
            left = cols[block, left_at, part // 2]
            for x in range(rows):
                shift = used * (part % 2) + GHOST * (skip + x)
                value = jnp.where(lane >= tile_cols - GHOST, turn(left, -GHOST - shift), 0.0)
                value = jnp.where(lane < GHOST, turn(right, -shift), value)
                if part < 6:
                    (electric, magnetic)[part // 3][part % 3, base + x, 1, inner, :] = value
                else:
                    inverse[base + x, 1] = value

    mask = ghost_mask(tile_cols, j, count_cols)

    def masked(row):
        scale = 0.5 * row_mask(row, GHOST, tile_rows, i, count_rows)
        return (scale, scale * mask)

    def invert(row, carry):
        scale = masked(row)
        for s in range(2):
            value = inverse[row, s]
            permittivity = jnp.full(value.shape, eps[0], F32)
            for m in range(1, NMAT):
                permittivity = jnp.where(value == float(m), eps[m], permittivity)
            inverse[row, s] = scale[s] / permittivity
        return carry

    lax.fori_loop(0, ext, invert, 0)
    sends = copies([(inverse, inverse_out)], semaphores)

    for n in range(ITERS):

        def magnetic_row(r):
            curl = curl_ahead(electric, r)
            scale = masked(r)
            stores = []
            for part in range(3):
                for s in range(2):
                    spot = (part, r, s, inner)
                    stores.append((magnetic, spot, magnetic[spot] - scale[s] * curl[part][s]))
            return stores

        def electric_row(r, x=None, q=None, side=0):
            curl = curl_behind(magnetic, r)
            stores = []
            for part in range(3):
                for s in range(2):
                    spot = (part, r, s, inner)
                    value = electric[spot] + inverse[r, s] * curl[part][s]
                    stores.append((electric, spot, value))
                    if s == 0 and x is not None:
                        stores.append((kept, (n, part, x), curl[part][0]))
                        if part < 2:
                            lanes = slice(side * tile_cols, (side + 1) * tile_cols)
                            for k, half in enumerate(split(value)):
                                start = (2 * n + k) * depth
                                stores.append((stash, (part, q, slice(start, start + depth), lanes), half))
            return stores

        def own_rows(k, carry):
            stores = []
            for step in range(OWN_GROUP):
                q, side = OWN_GROUP // 2 * k + step // 2, step % 2
                x = 2 * q + side
                stores += electric_row(GHOST + x, x, q, side)
            for ref, index, value in stores:
                ref[index] = value
            return carry

        sweep(n, ext - 1 - n, magnetic_row)
        sweep(n + 1, GHOST, electric_row)
        lax.fori_loop(0, tile_rows // OWN_GROUP, own_rows, 0)
        sweep(far_edge, ext - 1 - n, electric_row)
        sends += copies([(kept.at[n], kept_out.at[n])], semaphores.at[n + 1 : n + 2])

    for copy in started[early:]:
        copy.wait()
    waves = 2 * NF
    for p in range(2):
        for q in range(tile_rows // 2):
            value = dot(weights, stash[p, q])
            value = value[:waves] + value[waves:]
            for s in range(2):
                base = (p * tile_rows + 2 * q + s) * waves
                lens[base : base + waves, :] = value[:, s * tile_cols : (s + 1) * tile_cols]
    planes = 2 * tile_rows
    for f in range(NF):
        real = lens[pl.ds(f, planes, stride=waves), :]
        imag = lens[pl.ds(NF + f, planes, stride=waves), :]
        high, low = split(jnp.concatenate([real, imag], axis=1))
        value = lax.dot_general(
            jnp.concatenate([high, low], axis=0), phases[f], (((1,), (1,)), ((), ())), preferred_element_type=F32
        )
        value = value[:planes] + value[planes:]
        value = value[:, : 2 * FAR] + value[:, 2 * FAR :]
        mid[f] = value * twist[0][f : f + 1] + half_turn(value) * twist[1][f : f + 1]
    for copy in sends:
        copy.wait()


def backward_kernel(
    counts, own, sibling, target, twist, weights, kept_in, inverse_in, rows_far, rows_back_in, table_in,
    gradient, squares, mid, far, intensity, back, source, electric, magnetic, scaled, accum,
    kept, inverse, rows_back, table, semaphores,
):
    tile_rows, depth, tile_cols = gradient.shape
    width = 2 * tile_cols
    count_rows, count_cols = counts
    i, j = lax.axis_index("gx"), lax.axis_index("gy")
    samples = NF * FAR * FAR
    wide = 2 * FAR
    pairs = []
    for k in range(count_rows // 2):
        near = i ^ (2 * k)
        for block, index in ((own, near), (sibling, near ^ 1)):
            spot = pl.ds(pl.multiple_of(index * tile_rows, 8), tile_rows)
            for p in range(2):
                pairs.append(
                    (block.at[k, :, p * tile_rows : (p + 1) * tile_rows], mid.at[:, spot, p * wide : (p + 1) * wide])
                )
    first = len(pairs)
    pairs += [(rows_back_in, rows_back)] + column_blocks(table_in, table, width)
    second = len(pairs)
    pairs += [(inverse_in, inverse), (kept_in, kept)]
    started = copies(pairs, semaphores)
    clear_pads(scaled)
    clear_pads(magnetic)
    for copy in started[:first]:
        copy.wait()
    sign = jnp.where(lax.broadcasted_iota(jnp.int32, (1, wide), 1) < FAR, 1.0, -1.0)
    total = jnp.zeros((FAR, wide), F32)
    for f in range(NF):
        high, low = split(mid[f])
        both = dot(rows_far[f], jnp.concatenate([high, low, high], axis=0))
        level = jnp.zeros((FAR, wide), F32)
        for p in range(2):
            cos = both[:FAR, p * wide : (p + 1) * wide]
            sin = both[FAR:, p * wide : (p + 1) * wide]
            value = cos + sign * half_turn(sin)
            far[f, :, p * wide : (p + 1) * wide] = value
            level = level + value * value
        level = level + half_turn(level)
        intensity[f] = level
        total = total + level
    def wanted(f):
        return jnp.concatenate([target[f], target[f]], axis=1)

    power = jnp.sum(total, keepdims=True) / (2.0 * samples)
    total = jnp.zeros((FAR, wide), F32)
    for f in range(NF):
        level = intensity[f]
        total = total + (level / power - wanted(f)) * level
    spread = jnp.sum(total, keepdims=True) / (2.0 * samples * power)

    for copy in started[first:second]:
        copy.wait()
    mask = ghost_mask(tile_cols, j, count_cols)
    span = rows_back.shape[2] - count_rows * tile_rows + tile_rows
    row = lax.broadcasted_iota(jnp.int32, (2 * span, 1), 0)
    row = jnp.where(row >= span, row - span, row)
    lowest = jnp.where(i > 0, 0, BACK)
    highest = jnp.where(i < count_rows - 1, span, BACK + tile_rows)
    inside = jnp.where((row >= lowest) & (row < highest), 1.0, 0.0)
    waves = 2 * NF
    for f in range(NF):
        slope = 2.0 / power * (intensity[f] / power - wanted(f) - spread)
        slope = 2.0 * slope
        high, low = split(far[f] * jnp.concatenate([slope, slope], axis=1))
        start = pl.multiple_of(i * tile_rows, 8)
        phases = jnp.concatenate(
            [rows_back[f, 0, pl.ds(start, span), :], rows_back[f, 1, pl.ds(start, span), :]], axis=0
        )
        phase_high, phase_low = split(phases)
        both = dot(phase_high, high) + dot(phase_high, low) + dot(phase_low, high)
        turned = []
        for p in range(2):
            cos = both[:span, p * wide : (p + 1) * wide]
            sin = both[span:, p * wide : (p + 1) * wide]
            value = cos - sign * half_turn(sin)
            turned.append(value * twist[0, j, f : f + 1, :] - half_turn(value) * twist[1, j, f : f + 1, :])
        high, low = split(jnp.concatenate(turned, axis=0))
        left = jnp.concatenate(
            [jnp.concatenate([high, high], axis=1), jnp.concatenate([low, low], axis=1)], axis=0
        )
        both = dot(left, table[f])
        both = (both[: 2 * span] + both[2 * span :]) * inside
        for part in range(2):
            for s in range(2):
                start = part * width + s * tile_cols
                value = both[:, start : start + tile_cols]
                value = value * mask if s else value
                for p in range(2):
                    back[2 * p + s, pl.ds(part * NF + f, span, stride=waves), :] = value[p * span : (p + 1) * span]

    ext = tile_rows + 2 * BACK

    def source_row(r):
        spot = pl.ds(pl.multiple_of(r * waves, 8), waves)
        stores = []
        for p in range(2):
            high, low = split(jnp.concatenate([back[2 * p, spot, :], back[2 * p + 1, spot, :]], axis=1))
            both = dot(weights[...], jnp.concatenate([high, low, high], axis=0))
            for n in range(ITERS):
                for s in range(2):
                    value = both[n * depth : (n + 1) * depth, s * tile_cols : (s + 1) * tile_cols]
                    stores.append((source, (n, p, r, s), value))
        return stores

    sweep(0, ext, source_row)
    for copy in started[second:]:
        copy.wait()
    inner = pl.ds(PAD, depth)

    def masked(r):
        scale = 0.5 * row_mask(r, BACK, tile_rows, i, count_rows)
        return (scale, scale * mask)

    def take(n, r, value, own):
        stores = []
        total = accum[r - BACK] if own and n < ITERS - 1 else None
        for part in range(3):
            for s in range(2):
                now = value[part][s]
                if part < 2:
                    extra = source[n, part, r, s]
                    now = extra if now is None else now + extra
                elif now is None:
                    now = jnp.zeros((depth, tile_cols), F32)
                if n > 0:
                    stores.append((electric, (part, r, s), now))
                    stores.append((scaled, (part, r, s, inner), inverse[r + GHOST - BACK, s] * now))
                if own and s == 0:
                    term = now * kept[n, part, r - BACK]
                    total = term if total is None else total + term
        if own:
            stores.append((accum, r - BACK, total))
        return stores

    def first_row(own):
        return lambda r: take(ITERS - 1, r, [[None, None]] * 3, own)

    sweep(0, BACK, first_row(False))
    sweep(BACK, BACK + tile_rows, first_row(True))
    sweep(BACK + tile_rows, ext, first_row(False))
    for n in range(ITERS - 1, 0, -1):

        def magnetic_row(r):
            curl = curl_ahead(scaled, r)
            scale = masked(r)
            stores = []
            for part in range(3):
                for s in range(2):
                    spot = (part, r, s, inner)
                    value = scale[s] * curl[part][s]
                    stores.append((magnetic, spot, value if n == ITERS - 1 else value + magnetic[spot]))
            return stores

        def electric_row(own):
            def step(r):
                curl = curl_behind(magnetic, r)
                value = [[electric[part, r, s] - curl[part][s] for s in range(2)] for part in range(3)]
                return take(n - 1, r, value, own)

            return step

        low, high = BACK - n, BACK + tile_rows + n - 1
        sweep(low, high, magnetic_row)
        sweep(low + 1, BACK, electric_row(False))
        sweep(BACK, BACK + tile_rows, electric_row(True))
        sweep(BACK + tile_rows, high, electric_row(False))

    total = jnp.zeros((depth, tile_cols), F32)
    for x in range(tile_rows):
        value = inverse[GHOST + x, 0]
        value = -2.0 * (value * value) * accum[x]
        gradient[x] = value
        total = total + value * value
    squares[...] = jnp.broadcast_to(jnp.sum(total, keepdims=True), squares.shape)


def scale_kernel(cells, squares, gradient, result):
    total = jnp.sum(squares[...], keepdims=True) / squares.shape[1]
    scale = 1.0 / jnp.sqrt(total / cells + 1e-06)
    for x in range(gradient.shape[0]):
        result[x] = gradient[x] * scale


VMEM = pl.BlockSpec(memory_space=pltpu.VMEM)
HBM = pl.BlockSpec(memory_space=pltpu.HBM)
ANY = pl.BlockSpec(memory_space=pl.ANY)
DMA = pltpu.SemaphoreType.DMA


def call(kernel, name, specs, outs, scratch=(), out_specs=VMEM):
    return pl.pallas_call(
        kernel,
        name=name,
        in_specs=specs,
        out_specs=out_specs,
        out_shape=outs,
        scratch_shapes=scratch,
        compiler_params=pltpu.CompilerParams(vmem_limit_bytes=VMEM_BYTES),
    )


def array(*shape):
    return jax.ShapeDtypeStruct(shape, F32)


def buffer(*shape):
    return pltpu.VMEM(shape, F32)


def even_swaps(count):
    return [(k, k ^ 1) for k in range(count)]


def odd_swaps(count):
    return [(k, k + 1 if k % 2 else k - 1) for k in range(1, count - 1)]


def body(count_rows, count_cols, e_init, h_init, material, eps_table, target):
    tile_rows, depth, tile_cols = material.shape
    counts = (count_rows, count_cols)
    edge = array(7, GHOST, depth, tile_cols)
    side = array(4, depth, tile_cols)
    row_a, row_b = call(
        pack_rows_kernel,
        "pack_rows",
        [HBM] * 3,
        (edge, edge),
        [
            buffer(6, tile_rows, depth, tile_cols),
            pltpu.VMEM((tile_rows, depth, tile_cols), jnp.int32),
            buffer(2, GHOST, depth, tile_cols),
            DMA((4,)),
        ],
        (HBM, HBM),
    )(e_init, h_init, material)
    rows_a, rows_b = even_swaps(count_rows), odd_swaps(count_rows)
    cols_a, cols_b = even_swaps(count_cols), odd_swaps(count_cols)
    row_b = lax.ppermute(row_b, "gx", rows_b)
    row_a = lax.ppermute(row_a, "gx", rows_a)
    col_a, col_b = call(pack_columns_kernel, "pack_columns", [VMEM] * 3, (side, side), (), (VMEM, VMEM))(
        e_init, h_init, material
    )
    col_b = lax.ppermute(col_b, "gy", cols_b)
    col_a = lax.ppermute(col_a, "gy", cols_a)
    corner = jnp.stack([col_a, col_b])
    corner_b = lax.ppermute(corner, "gx", rows_b)
    corner_a = lax.ppermute(corner, "gx", rows_a)

    table = jnp.asarray(column_table(tile_cols, 2 * tile_cols))
    twist = jnp.asarray(column_twist(count_cols))
    ext = tile_rows + 2 * GHOST
    waves = 2 * NF
    kept = (ITERS, 3, tile_rows, depth, tile_cols)
    inverse = (ext, 2, depth, tile_cols)
    kept_out, inverse_out, mid = call(
        functools.partial(forward_kernel, counts),
        "forward",
        [HBM] * 6 + [ANY] * 4 + [HBM],
        (array(*kept), array(*inverse), array(NF, 2 * tile_rows, 2 * FAR)),
        [
            buffer(3, ext, 2, depth + 2 * PAD, tile_cols),
            buffer(3, ext, 2, depth + 2 * PAD, tile_cols),
            buffer(*inverse),
            buffer(*kept),
            pltpu.VMEM((tile_rows, depth, tile_cols), jnp.int32),
            buffer(3, 2, 4, depth, tile_cols),
            pltpu.VMEM((NF, 4 * FAR, 2 * tile_cols), BF16),
            pltpu.VMEM((2, tile_rows // 2, 2 * ITERS * depth, 2 * tile_cols), BF16),
            buffer(2 * tile_rows * waves, tile_cols),
            pltpu.SMEM(eps_table.shape, F32),
            DMA((22,)),
        ],
        (HBM, HBM, VMEM),
    )(
        eps_table, e_init, h_init, material, row_a, row_b, col_a, col_b,
        corner_a, corner_b, table,
    )

    whole = mid
    for k in range(1, count_cols):
        whole = whole + lax.ppermute(mid, "gy", [(n, n ^ k) for n in range(count_cols)])
    own = jnp.stack(
        [whole]
        + [lax.ppermute(whole, "gx", [(n, n ^ k) for n in range(count_rows)]) for k in range(2, count_rows, 2)]
    )
    sibling = lax.ppermute(own, "gx", rows_a)

    rows = count_rows * tile_rows
    ext = tile_rows + 2 * BACK
    span = tile_rows + 16
    devices = count_rows * count_cols
    grid = (3, ext, 2, depth + 2 * PAD, tile_cols)
    back_rows = row_back_table(rows)
    gradient, squares = call(
        functools.partial(backward_kernel, counts),
        "backward",
        [ANY] * 2 + [VMEM] * 3 + [HBM] * 2 + [VMEM] + [HBM] * 2,
        (array(tile_rows, depth, tile_cols), array(devices, 128)),
        [
            buffer(NF, rows, 4 * FAR),
            buffer(NF, FAR, 4 * FAR),
            buffer(NF, FAR, 2 * FAR),
            buffer(4, span * waves, tile_cols),
            buffer(ITERS, 2, ext, 2, depth, tile_cols),
            buffer(3, ext, 2, depth, tile_cols),
            buffer(*grid),
            buffer(*grid),
            buffer(tile_rows, depth, tile_cols),
            buffer(*kept),
            buffer(*inverse),
            buffer(*back_rows.shape),
            pltpu.VMEM((NF, 4 * FAR, 4 * tile_cols), BF16),
            DMA((2 * count_rows + 11,)),
        ],
        (VMEM, VMEM),
    )(
        own, sibling, target, twist, jnp.asarray(source_table(depth)),
        kept_out, inverse_out, jnp.asarray(row_table(rows)), jnp.asarray(back_rows), table,
    )
    squares = lax.all_to_all(squares, ("gx", "gy"), 0, 0, tiled=True)
    cells = rows * depth * tile_cols * count_cols
    return call(
        functools.partial(scale_kernel, cells), "scale", [VMEM, VMEM], array(tile_rows, depth, tile_cols)
    )(squares, gradient)


def solution(mesh):
    in_specs = (P(None, "gx", None, "gy"), P(None, "gx", None, "gy"), P("gx", None, "gy"), P(), P())
    out_specs = P("gx", None, "gy")
    part = functools.partial(body, mesh.shape["gx"], mesh.shape["gy"])
    return jax.shard_map(part, mesh=mesh, in_specs=in_specs, out_specs=out_specs, check_vma=False)
```

```python
import functools
import math

import jax
import jax.numpy as jnp
import ml_dtypes
import numpy as np
from jax import lax
from jax.experimental import pallas as pl
from jax.experimental.pallas import tpu as pltpu
from jax.sharding import PartitionSpec as P

ITERS = 6
NF = 8
FAR = 64
NMAT = 8
GHOST = ITERS
BACK = ITERS - 1
TWO_PI = 2.0 * math.pi
F32 = jnp.float32
BF16 = jnp.bfloat16
PAD = 8
VMEM_BYTES = 40 * 1024 * 1024
OWN_GROUP = 8
GROUP = 8


def split_table(table):
    high = table.astype(np.float32).astype(ml_dtypes.bfloat16)
    low = (table - high.astype(np.float64)).astype(np.float32).astype(ml_dtypes.bfloat16)
    return high, low


def time_table(depth):
    freq = np.arange(NF)[None, :, None]
    moment = np.arange(1, ITERS + 1)[:, None, None]
    turns = ((2 * freq + 1) * (7 * moment + np.arange(depth)[None, None, :])) % 64
    angle = turns * (TWO_PI / 64)
    return np.concatenate([np.cos(angle), -np.sin(angle)], axis=1)


def source_table(depth):
    flat = time_table(depth).transpose(0, 2, 1).reshape(ITERS * depth, 2 * NF)
    high, low = split_table(flat)
    return np.concatenate([high, high, low], axis=1)


def phase(cells, length):
    freq = np.arange(NF)[:, None, None]
    order = np.arange(FAR)[None, :, None] - FAR // 2
    period = 4 * length * NF
    turns = (order * (2 * cells[None, None, :] + 1) * (NF + freq)) % period
    angle = turns * (TWO_PI / period)
    return np.cos(angle), np.sin(angle)


def column_table(tile_cols, width):
    lanes = np.arange(width)
    cells = np.where(lanes >= width - GHOST, lanes - width, lanes)
    used = (lanes < tile_cols + GHOST) | (lanes >= width - GHOST)
    cos, sin = (t * used[None, None, :] for t in phase(cells, tile_cols))
    return np.stack([np.concatenate(split_table(t), axis=1) for t in (cos, sin, -sin)])


def column_blocks(table, target, lanes):
    pairs = []
    for half in range(2):
        for row, col, block in ((0, 0, 0), (0, 1, 1), (1, 0, 2), (1, 1, 0)):
            start = (2 * half + row) * FAR
            pairs.append(
                (
                    table.at[block, :, half * FAR : (half + 1) * FAR, 0:lanes],
                    target.at[:, start : start + FAR, col * lanes : (col + 1) * lanes],
                )
            )
    return pairs


def column_twist(count_cols):
    freq = np.arange(NF)[None, :, None]
    order = np.arange(FAR)[None, None, :] - FAR // 2
    place = np.arange(count_cols)[:, None, None]
    angle = ((order * (NF + freq) * place) % 16) * (TWO_PI / 16)
    cos, sin = np.cos(angle), np.sin(angle)
    return np.stack(
        [np.concatenate([cos, cos], axis=2), np.concatenate([sin, -sin], axis=2)]
    ).astype(np.float32)


def row_table(rows):
    table = np.concatenate(phase(np.arange(rows), rows), axis=1)
    high, low = split_table(table)
    return np.concatenate([high, high, low], axis=2)


def row_back_table(rows):
    cells = np.arange(rows + 16) - BACK
    cos, sin = phase(cells, rows)
    return np.stack([cos, sin], axis=1).transpose(0, 1, 3, 2).astype(np.float32)


def split(value):
    high = value.astype(BF16)
    return high, (value - high.astype(F32)).astype(BF16)


def dot(left, right):
    return jnp.dot(left, right, preferred_element_type=F32)


def lens_weights(depth):
    shape = (2 * NF, 2 * ITERS * depth)
    row = lax.broadcasted_iota(jnp.int32, shape, 0)
    lane = lax.broadcasted_iota(jnp.int32, shape, 1)
    moment = lane // (2 * depth) + 1
    turns = (2 * (row % NF) + 1) * (7 * moment + lane % depth)
    turns = (turns + jnp.where(row < NF, 0, 16)) % 64
    return jnp.concatenate(split(jnp.cos(turns.astype(F32) * (TWO_PI / 64))), axis=0)


def tile_twist(j):
    shape = (NF, 2 * FAR)
    freq = lax.broadcasted_iota(jnp.int32, shape, 0)
    lane = lax.broadcasted_iota(jnp.int32, shape, 1)
    turns = ((lane % FAR + FAR // 2) * (NF + freq) * j) % 16
    angle = turns.astype(F32) * (TWO_PI / 16)
    return jnp.cos(angle), jnp.where(lane < FAR, 1.0, -1.0) * jnp.sin(angle)


def half_turn(value):
    return pltpu.roll(value, FAR, 1)


def ahead_y(own, ghost):
    last = lax.broadcasted_iota(jnp.int32, own.shape, 1) == own.shape[1] - 1
    a, b = (pltpu.roll(v, v.shape[1] - 1, 1) for v in (own, ghost))
    return (jnp.where(last, b, a) - own, jnp.where(last, a, b) - ghost)


def behind_y(own, ghost):
    first = lax.broadcasted_iota(jnp.int32, own.shape, 1) == 0
    a, b = (pltpu.roll(v, 1, 1) for v in (own, ghost))
    return (own - jnp.where(first, b, a), ghost - jnp.where(first, a, b))


def depths(ref, shift=0):
    return slice(PAD + shift, ref.shape[3] - PAD + shift)


def curl_ahead(ref, r):
    def row(part, step=0, shift=0):
        return [ref[part, r + step, s, depths(ref, shift), :] for s in range(2)]

    x, y, z = row(0), row(1), row(2)
    y_next, z_next = row(1, 1), row(2, 1)
    x_deep, y_deep = row(0, 0, 1), row(1, 0, 1)
    zy, xy = ahead_y(*z), ahead_y(*x)
    return (
        [zy[s] - (y_deep[s] - y[s]) for s in range(2)],
        [(x_deep[s] - x[s]) - (z_next[s] - z[s]) for s in range(2)],
        [(y_next[s] - y[s]) - xy[s] for s in range(2)],
    )


def curl_behind(ref, r):
    def row(part, step=0, shift=0):
        return [ref[part, r + step, s, depths(ref, shift), :] for s in range(2)]

    x, y, z = row(0), row(1), row(2)
    y_prev, z_prev = row(1, -1), row(2, -1)
    x_deep, y_deep = row(0, 0, -1), row(1, 0, -1)
    zy, xy = behind_y(*z), behind_y(*x)
    return (
        [zy[s] - (y[s] - y_deep[s]) for s in range(2)],
        [(x[s] - x_deep[s]) - (z[s] - z_prev[s]) for s in range(2)],
        [(y[s] - y_prev[s]) - xy[s] for s in range(2)],
    )


def clear_pads(ref):
    for part in range(ref.shape[0]):
        for start in (0, ref.shape[3] - PAD):
            shape = ref.shape[1:3] + (PAD,) + ref.shape[4:]
            ref[part, :, :, start : start + PAD, :] = jnp.zeros(shape, F32)


def sweep(low, high, *steps):
    def group(start, rows):
        stores = []
        for k in range(rows):
            for step in steps:
                stores += step(start + k)
        for ref, index, value in stores:
            ref[index] = value

    whole = (high - low) // GROUP
    if whole:

        def body(k, carry):
            group(low + GROUP * k, GROUP)
            return carry

        lax.fori_loop(0, whole, body, 0)
    if (high - low) % GROUP:
        group(low + GROUP * whole, (high - low) % GROUP)


def copies(pairs, semaphores):
    started = []
    for k, (source, target) in enumerate(pairs):
        started.append(pltpu.make_async_copy(source, target, semaphores.at[k]))
        started[-1].start()
    return started


def ghost_mask(tile_cols, column, count_cols):
    lane = lax.broadcasted_iota(jnp.int32, (1, tile_cols), 1)
    upper = jnp.where(column < count_cols - 1, GHOST, 0)
    lower = tile_cols - jnp.where(column > 0, GHOST, 0)
    return jnp.where((lane < upper) | (lane >= lower), 1.0, 0.0)


def row_mask(row, ghost, tile_rows, place, count_rows):
    low = jnp.where(place > 0, 1.0, 0.0)
    high = jnp.where(place < count_rows - 1, 1.0, 0.0)
    return jnp.where(row < ghost, low, jnp.where(row >= ghost + tile_rows, high, 1.0))


def pack_rows_kernel(e, h, material, rows_a, rows_b, fields, cells, edges, semaphores):
    tile_rows = material.shape[0]
    even = lax.axis_index("gx") % 2 == 0
    last = tile_rows - GHOST
    starts = (jnp.where(even, last, 0), jnp.where(even, 0, last))
    loads = copies([(e, fields.at[0:3]), (h, fields.at[3:6]), (material, cells)], semaphores)
    for load in loads:
        load.wait()
    pairs = [(fields.at[:, pl.ds(starts[1], GHOST)], rows_b.at[0:6])]
    pairs.append((fields.at[:, pl.ds(starts[0], GHOST)], rows_a.at[0:6]))
    sends = copies(pairs, semaphores)
    for k, out in enumerate((rows_a, rows_b)):
        edges[k] = cells[pl.ds(starts[k], GHOST)].astype(F32)
    sends += copies([(edges.at[0], rows_a.at[6]), (edges.at[1], rows_b.at[6])], semaphores.at[2:4])
    for send in sends:
        send.wait()


def pack_columns_kernel(e, h, material, cols_a, cols_b):
    tile_rows, depth, tile_cols = material.shape
    even = lax.axis_index("gy") % 2 == 0
    lane = lax.broadcasted_iota(jnp.int32, (depth, tile_cols), 1)
    used = GHOST * tile_rows
    for pair in range(4):
        first = last = jnp.zeros((depth, tile_cols), F32)
        for part in range(2 * pair, min(2 * pair + 2, 7)):
            for x in range(tile_rows):
                if part < 3:
                    plane = e[part, x]
                elif part < 6:
                    plane = h[part - 3, x]
                else:
                    plane = material[x].astype(F32)
                shift = used * (part % 2) + GHOST * x
                spot = (lane >= shift) & (lane < shift + GHOST)
                first = jnp.where(spot, pltpu.roll(plane, shift, 1) if shift else plane, first)
                shift = (shift + GHOST) % tile_cols
                last = jnp.where(spot, pltpu.roll(plane, shift, 1) if shift else plane, last)
        cols_a[pair] = jnp.where(even, last, first)
        cols_b[pair] = jnp.where(even, first, last)


def forward_kernel(
    counts, eps_in, e, h, material, row_a, row_b, own_a, own_b, corner_a, corner_b, table,
    kept_out, inverse_out, mid, electric, magnetic, inverse, kept, index, cols, phases, stash, lens, eps, semaphores,
):
    tile_rows, depth, tile_cols = material.shape
    count_rows, count_cols = counts
    i, j = lax.axis_index("gx"), lax.axis_index("gy")
    even_x = i % 2 == 0
    even_y = j % 2 == 0
    far_edge = GHOST + tile_rows
    ext = tile_rows + 2 * GHOST
    spots = [
        pl.ds(jnp.where(even_x, far_edge, 0), GHOST),
        pl.ds(jnp.where(even_x, 0, far_edge), GHOST),
    ]
    own = pl.ds(GHOST, tile_rows)
    inner = pl.ds(PAD, depth)
    pairs = [(material, index)]
    pairs += [(own_a, cols.at[0, 0]), (own_b, cols.at[0, 1]), (corner_a, cols.at[1]), (corner_b, cols.at[2])]
    for part, spot in ((row_a, spots[0]), (row_b, spots[1])):
        pairs.append((part.at[6], inverse.at[spot, 0]))
        pairs.append((part.at[0:3], electric.at[:, spot, 0, inner, :]))
        pairs.append((part.at[3:6], magnetic.at[:, spot, 0, inner, :]))
    pairs.append((e, electric.at[:, own, 0, inner, :]))
    pairs.append((h, magnetic.at[:, own, 0, inner, :]))
    pairs.append((eps_in, eps))
    early = len(pairs)
    pairs += column_blocks(table, phases, tile_cols)
    started = copies(pairs, semaphores)
    clear_pads(electric)
    clear_pads(magnetic)
    weights = lens_weights(depth)
    twist = tile_twist(j)
    for copy in started[1:5]:
        copy.wait()

    lane = lax.broadcasted_iota(jnp.int32, (depth, tile_cols), 1)
    right_at = jnp.where(even_y, 0, 1)
    left_at = jnp.where(even_y, 1, 0)
    used = GHOST * tile_rows

    def turn(value, shift):
        shift = shift % tile_cols
        return pltpu.roll(value, shift, 1) if shift else value

    for part in range(7):
        for base, block, skip, rows in (
            (GHOST, 0, 0, tile_rows),
            (0, jnp.where(even_x, 2, 1), tile_rows - GHOST, GHOST),
            (far_edge, jnp.where(even_x, 1, 2), 0, GHOST),
        ):
            right = cols[block, right_at, part // 2]
            left = cols[block, left_at, part // 2]
            for x in range(rows):
                shift = used * (part % 2) + GHOST * (skip + x)
                value = jnp.where(lane >= tile_cols - GHOST, turn(left, -GHOST - shift), 0.0)
                value = jnp.where(lane < GHOST, turn(right, -shift), value)
                if part < 6:
                    (electric, magnetic)[part // 3][part % 3, base + x, 1, inner, :] = value
                else:
                    inverse[base + x, 1] = value

    for copy in started[:1] + started[5:early]:
        copy.wait()
    inverse[GHOST:far_edge, 0] = index[...].astype(F32)
    mask = ghost_mask(tile_cols, j, count_cols)

    def masked(row):
        scale = 0.5 * row_mask(row, GHOST, tile_rows, i, count_rows)
        return (scale, scale * mask)

    def invert(row, carry):
        scale = masked(row)
        for s in range(2):
            value = inverse[row, s]
            permittivity = jnp.full(value.shape, eps[0], F32)
            for m in range(1, NMAT):
                permittivity = jnp.where(value == float(m), eps[m], permittivity)
            inverse[row, s] = scale[s] / permittivity
        return carry

    lax.fori_loop(0, ext, invert, 0)
    sends = copies([(inverse, inverse_out)], semaphores)

    for n in range(ITERS):

        def magnetic_row(r):
            curl = curl_ahead(electric, r)
            scale = masked(r)
            stores = []
            for part in range(3):
                for s in range(2):
                    spot = (part, r, s, inner)
                    stores.append((magnetic, spot, magnetic[spot] - scale[s] * curl[part][s]))
            return stores

        def electric_row(r, x=None, q=None, side=0):
            curl = curl_behind(magnetic, r)
            stores = []
            for part in range(3):
                for s in range(2):
                    spot = (part, r, s, inner)
                    value = electric[spot] + inverse[r, s] * curl[part][s]
                    stores.append((electric, spot, value))
                    if s == 0 and x is not None:
                        stores.append((kept, (n, part, x), curl[part][0]))
                        if part < 2:
                            lanes = slice(side * tile_cols, (side + 1) * tile_cols)
                            for k, half in enumerate(split(value)):
                                start = (2 * n + k) * depth
                                stores.append((stash, (part, q, slice(start, start + depth), lanes), half))
            return stores

        def own_rows(k, carry):
            stores = []
            for step in range(OWN_GROUP):
                q, side = OWN_GROUP // 2 * k + step // 2, step % 2
                x = 2 * q + side
                stores += electric_row(GHOST + x, x, q, side)
            for ref, index, value in stores:
                ref[index] = value
            return carry

        sweep(n, ext - 1 - n, magnetic_row)
        sweep(n + 1, GHOST, electric_row)
        lax.fori_loop(0, tile_rows // OWN_GROUP, own_rows, 0)
        sweep(far_edge, ext - 1 - n, electric_row)
        sends += copies([(kept.at[n], kept_out.at[n])], semaphores.at[n + 1 : n + 2])

    for copy in started[early:]:
        copy.wait()
    waves = 2 * NF
    for p in range(2):
        for q in range(tile_rows // 2):
            value = dot(weights, stash[p, q])
            value = value[:waves] + value[waves:]
            for s in range(2):
                base = (p * tile_rows + 2 * q + s) * waves
                lens[base : base + waves, :] = value[:, s * tile_cols : (s + 1) * tile_cols]
    planes = 2 * tile_rows
    for f in range(NF):
        real = lens[pl.ds(f, planes, stride=waves), :]
        imag = lens[pl.ds(NF + f, planes, stride=waves), :]
        high, low = split(jnp.concatenate([real, imag], axis=1))
        value = lax.dot_general(
            jnp.concatenate([high, low], axis=0), phases[f], (((1,), (1,)), ((), ())), preferred_element_type=F32
        )
        value = value[:planes] + value[planes:]
        value = value[:, : 2 * FAR] + value[:, 2 * FAR :]
        mid[f] = value * twist[0][f : f + 1] + half_turn(value) * twist[1][f : f + 1]
    for copy in sends:
        copy.wait()


def backward_kernel(
    counts, own, sibling, target, twist, weights, kept_in, inverse_in, rows_far, rows_back_in, table_in,
    gradient, squares, mid, far, intensity, back, source, electric, magnetic, scaled, accum,
    kept, inverse, rows_back, table, semaphores,
):
    tile_rows, depth, tile_cols = gradient.shape
    width = 2 * tile_cols
    count_rows, count_cols = counts
    i, j = lax.axis_index("gx"), lax.axis_index("gy")
    samples = NF * FAR * FAR
    wide = 2 * FAR
    pairs = []
    for k in range(count_rows // 2):
        near = i ^ (2 * k)
        for block, index in ((own, near), (sibling, near ^ 1)):
            spot = pl.ds(pl.multiple_of(index * tile_rows, 8), tile_rows)
            for p in range(2):
                pairs.append(
                    (block.at[k, :, p * tile_rows : (p + 1) * tile_rows], mid.at[:, spot, p * wide : (p + 1) * wide])
                )
    first = len(pairs)
    pairs += [(rows_back_in, rows_back)] + column_blocks(table_in, table, width)
    second = len(pairs)
    pairs += [(inverse_in, inverse), (kept_in, kept)]
    started = copies(pairs, semaphores)
    clear_pads(scaled)
    clear_pads(magnetic)
    for copy in started[:first]:
        copy.wait()
    sign = jnp.where(lax.broadcasted_iota(jnp.int32, (1, wide), 1) < FAR, 1.0, -1.0)
    total = jnp.zeros((FAR, wide), F32)
    for f in range(NF):
        high, low = split(mid[f])
        both = dot(rows_far[f], jnp.concatenate([high, low, high], axis=0))
        level = jnp.zeros((FAR, wide), F32)
        for p in range(2):
            cos = both[:FAR, p * wide : (p + 1) * wide]
            sin = both[FAR:, p * wide : (p + 1) * wide]
            value = cos + sign * half_turn(sin)
            far[f, :, p * wide : (p + 1) * wide] = value
            level = level + value * value
        level = level + half_turn(level)
        intensity[f] = level
        total = total + level
    def wanted(f):
        return jnp.concatenate([target[f], target[f]], axis=1)

    power = jnp.sum(total, keepdims=True) / (2.0 * samples)
    over = 1.0 / power
    total = jnp.zeros((FAR, wide), F32)
    for f in range(NF):
        level = intensity[f]
        total = total + (level * over - wanted(f)) * level
    spread = jnp.sum(total, keepdims=True) / (2.0 * samples * power)

    for copy in started[first:second]:
        copy.wait()
    mask = ghost_mask(tile_cols, j, count_cols)
    span = rows_back.shape[2] - count_rows * tile_rows + tile_rows
    row = lax.broadcasted_iota(jnp.int32, (2 * span, 1), 0)
    row = jnp.where(row >= span, row - span, row)
    lowest = jnp.where(i > 0, 0, BACK)
    highest = jnp.where(i < count_rows - 1, span, BACK + tile_rows)
    inside = jnp.where((row >= lowest) & (row < highest), 1.0, 0.0)
    waves = 2 * NF
    gradients = []
    for f in range(NF):
        slope = 2.0 * ((2.0 * over) * (intensity[f] * over - wanted(f) - spread))
        gradients.append(split(far[f] * jnp.concatenate([slope, slope], axis=1)))
    start = pl.multiple_of(i * tile_rows, 8)
    crossed = []
    for f in range(NF):
        high, low = gradients[f]
        phases = jnp.concatenate(
            [rows_back[f, 0, pl.ds(start, span), :], rows_back[f, 1, pl.ds(start, span), :]], axis=0
        )
        phase_high, phase_low = split(phases)
        crossed.append(dot(phase_high, high) + dot(phase_high, low) + dot(phase_low, high))
    lefts = []
    for f in range(NF):
        turned = []
        for p in range(2):
            cos = crossed[f][:span, p * wide : (p + 1) * wide]
            sin = crossed[f][span:, p * wide : (p + 1) * wide]
            value = cos - sign * half_turn(sin)
            turned.append(value * twist[0, j, f : f + 1, :] - half_turn(value) * twist[1, j, f : f + 1, :])
        high, low = split(jnp.concatenate(turned, axis=0) * inside)
        lefts.append(
            jnp.concatenate(
                [jnp.concatenate([high, high], axis=1), jnp.concatenate([low, low], axis=1)], axis=0
            )
        )
    for f in range(NF):
        both = dot(lefts[f], table[f])
        both = both[: 2 * span] + both[2 * span :]
        for part in range(2):
            for s in range(2):
                begin = part * width + s * tile_cols
                value = both[:, begin : begin + tile_cols]
                value = value * mask if s else value
                for p in range(2):
                    back[2 * p + s, pl.ds(part * NF + f, span, stride=waves), :] = value[p * span : (p + 1) * span]

    ext = tile_rows + 2 * BACK

    def source_row(r):
        spot = pl.ds(pl.multiple_of(r * waves, 8), waves)
        stores = []
        for p in range(2):
            high, low = split(jnp.concatenate([back[2 * p, spot, :], back[2 * p + 1, spot, :]], axis=1))
            both = dot(weights[...], jnp.concatenate([high, low, high], axis=0))
            for n in range(ITERS):
                for s in range(2):
                    value = both[n * depth : (n + 1) * depth, s * tile_cols : (s + 1) * tile_cols]
                    stores.append((source, (n, p, r, s), value))
        return stores

    sweep(0, ext, source_row)
    for copy in started[second:]:
        copy.wait()
    inner = pl.ds(PAD, depth)

    def masked(r):
        scale = 0.5 * row_mask(r, BACK, tile_rows, i, count_rows)
        return (scale, scale * mask)

    def take(n, r, value, own):
        stores = []
        total = accum[r - BACK] if own and n < ITERS - 1 else None
        for part in range(3):
            for s in range(2):
                now = value[part][s]
                if part < 2:
                    extra = source[n, part, r, s]
                    now = extra if now is None else now + extra
                elif now is None:
                    now = jnp.zeros((depth, tile_cols), F32)
                if n > 0:
                    stores.append((electric, (part, r, s), now))
                    stores.append((scaled, (part, r, s, inner), inverse[r + GHOST - BACK, s] * now))
                if own and s == 0:
                    term = now * kept[n, part, r - BACK]
                    total = term if total is None else total + term
        if own:
            stores.append((accum, r - BACK, total))
        return stores

    def first_row(own):
        return lambda r: take(ITERS - 1, r, [[None, None]] * 3, own)

    sweep(0, BACK, first_row(False))
    sweep(BACK, BACK + tile_rows, first_row(True))
    sweep(BACK + tile_rows, ext, first_row(False))
    for n in range(ITERS - 1, 0, -1):

        def magnetic_row(r):
            curl = curl_ahead(scaled, r)
            scale = masked(r)
            stores = []
            for part in range(3):
                for s in range(2):
                    spot = (part, r, s, inner)
                    value = scale[s] * curl[part][s]
                    stores.append((magnetic, spot, value if n == ITERS - 1 else value + magnetic[spot]))
            return stores

        def electric_row(own):
            def step(r):
                curl = curl_behind(magnetic, r)
                value = [[electric[part, r, s] - curl[part][s] for s in range(2)] for part in range(3)]
                return take(n - 1, r, value, own)

            return step

        low, high = BACK - n, BACK + tile_rows + n - 1
        sweep(low, high, magnetic_row)
        sweep(low + 1, BACK, electric_row(False))
        sweep(BACK, BACK + tile_rows, electric_row(True))
        sweep(BACK + tile_rows, high, electric_row(False))

    total = jnp.zeros((depth, tile_cols), F32)
    for x in range(tile_rows):
        value = inverse[GHOST + x, 0]
        value = -2.0 * (value * value) * accum[x]
        gradient[x] = value
        total = total + value * value
    squares[...] = jnp.broadcast_to(jnp.sum(total, keepdims=True), squares.shape)


def scale_kernel(cells, squares, gradient, result):
    total = jnp.sum(squares[...], keepdims=True) / squares.shape[1]
    scale = 1.0 / jnp.sqrt(total / cells + 1e-06)
    for x in range(gradient.shape[0]):
        result[x] = gradient[x] * scale


VMEM = pl.BlockSpec(memory_space=pltpu.VMEM)
HBM = pl.BlockSpec(memory_space=pltpu.HBM)
ANY = pl.BlockSpec(memory_space=pl.ANY)
DMA = pltpu.SemaphoreType.DMA


def call(kernel, name, specs, outs, scratch=(), out_specs=VMEM):
    return pl.pallas_call(
        kernel,
        name=name,
        in_specs=specs,
        out_specs=out_specs,
        out_shape=outs,
        scratch_shapes=scratch,
        compiler_params=pltpu.CompilerParams(vmem_limit_bytes=VMEM_BYTES),
    )


def array(*shape):
    return jax.ShapeDtypeStruct(shape, F32)


def buffer(*shape):
    return pltpu.VMEM(shape, F32)


def even_swaps(count):
    return [(k, k ^ 1) for k in range(count)]


def odd_swaps(count):
    return [(k, k + 1 if k % 2 else k - 1) for k in range(1, count - 1)]


def body(count_rows, count_cols, e_init, h_init, material, eps_table, target):
    tile_rows, depth, tile_cols = material.shape
    counts = (count_rows, count_cols)
    edge = array(7, GHOST, depth, tile_cols)
    side = array(4, depth, tile_cols)
    row_a, row_b = call(
        pack_rows_kernel,
        "pack_rows",
        [HBM] * 3,
        (edge, edge),
        [
            buffer(6, tile_rows, depth, tile_cols),
            pltpu.VMEM((tile_rows, depth, tile_cols), jnp.int32),
            buffer(2, GHOST, depth, tile_cols),
            DMA((4,)),
        ],
        (HBM, HBM),
    )(e_init, h_init, material)
    rows_a, rows_b = even_swaps(count_rows), odd_swaps(count_rows)
    cols_a, cols_b = even_swaps(count_cols), odd_swaps(count_cols)
    row_b = lax.ppermute(row_b, "gx", rows_b)
    row_a = lax.ppermute(row_a, "gx", rows_a)
    col_a, col_b = call(pack_columns_kernel, "pack_columns", [VMEM] * 3, (side, side), (), (VMEM, VMEM))(
        e_init, h_init, material
    )
    col_b = lax.ppermute(col_b, "gy", cols_b)
    col_a = lax.ppermute(col_a, "gy", cols_a)
    corner = jnp.stack([col_a, col_b])
    corner_b = lax.ppermute(corner, "gx", rows_b)
    corner_a = lax.ppermute(corner, "gx", rows_a)

    table = jnp.asarray(column_table(tile_cols, 2 * tile_cols))
    twist = jnp.asarray(column_twist(count_cols))
    ext = tile_rows + 2 * GHOST
    waves = 2 * NF
    kept = (ITERS, 3, tile_rows, depth, tile_cols)
    inverse = (ext, 2, depth, tile_cols)
    kept_out, inverse_out, mid = call(
        functools.partial(forward_kernel, counts),
        "forward",
        [HBM] * 6 + [ANY] * 4 + [HBM],
        (array(*kept), array(*inverse), array(NF, 2 * tile_rows, 2 * FAR)),
        [
            buffer(3, ext, 2, depth + 2 * PAD, tile_cols),
            buffer(3, ext, 2, depth + 2 * PAD, tile_cols),
            buffer(*inverse),
            buffer(*kept),
            pltpu.VMEM((tile_rows, depth, tile_cols), jnp.int32),
            buffer(3, 2, 4, depth, tile_cols),
            pltpu.VMEM((NF, 4 * FAR, 2 * tile_cols), BF16),
            pltpu.VMEM((2, tile_rows // 2, 2 * ITERS * depth, 2 * tile_cols), BF16),
            buffer(2 * tile_rows * waves, tile_cols),
            pltpu.SMEM(eps_table.shape, F32),
            DMA((22,)),
        ],
        (HBM, HBM, VMEM),
    )(
        eps_table, e_init, h_init, material, row_a, row_b, col_a, col_b,
        corner_a, corner_b, table,
    )

    whole = mid
    for k in range(1, count_cols):
        whole = whole + lax.ppermute(mid, "gy", [(n, n ^ k) for n in range(count_cols)])
    own = jnp.stack(
        [whole]
        + [lax.ppermute(whole, "gx", [(n, n ^ k) for n in range(count_rows)]) for k in range(2, count_rows, 2)]
    )
    sibling = lax.ppermute(own, "gx", rows_a)

    rows = count_rows * tile_rows
    ext = tile_rows + 2 * BACK
    span = tile_rows + 16
    devices = count_rows * count_cols
    grid = (3, ext, 2, depth + 2 * PAD, tile_cols)
    back_rows = row_back_table(rows)
    gradient, squares = call(
        functools.partial(backward_kernel, counts),
        "backward",
        [ANY] * 2 + [VMEM] * 3 + [HBM] * 2 + [VMEM] + [HBM] * 2,
        (array(tile_rows, depth, tile_cols), array(devices, 128)),
        [
            buffer(NF, rows, 4 * FAR),
            buffer(NF, FAR, 4 * FAR),
            buffer(NF, FAR, 2 * FAR),
            buffer(4, span * waves, tile_cols),
            buffer(ITERS, 2, ext, 2, depth, tile_cols),
            buffer(3, ext, 2, depth, tile_cols),
            buffer(*grid),
            buffer(*grid),
            buffer(tile_rows, depth, tile_cols),
            buffer(*kept),
            buffer(*inverse),
            buffer(*back_rows.shape),
            pltpu.VMEM((NF, 4 * FAR, 4 * tile_cols), BF16),
            DMA((2 * count_rows + 11,)),
        ],
        (VMEM, VMEM),
    )(
        own, sibling, target, twist, jnp.asarray(source_table(depth)),
        kept_out, inverse_out, jnp.asarray(row_table(rows)), jnp.asarray(back_rows), table,
    )
    squares = lax.all_to_all(squares, ("gx", "gy"), 0, 0, tiled=True)
    cells = rows * depth * tile_cols * count_cols
    return call(
        functools.partial(scale_kernel, cells), "scale", [VMEM, VMEM], array(tile_rows, depth, tile_cols)
    )(squares, gradient)


def solution(mesh):
    in_specs = (P(None, "gx", None, "gy"), P(None, "gx", None, "gy"), P("gx", None, "gy"), P(), P())
    out_specs = P("gx", None, "gy")
    part = functools.partial(body, mesh.shape["gx"], mesh.shape["gy"])
    return jax.shard_map(part, mesh=mesh, in_specs=in_specs, out_specs=out_specs, check_vma=False)
```

```python
import functools
import math

import jax
import jax.numpy as jnp
import ml_dtypes
import numpy as np
from jax import lax
from jax.experimental import pallas as pl
from jax.experimental.pallas import tpu as pltpu
from jax.sharding import PartitionSpec as P

ITERS = 6
NF = 8
FAR = 64
NMAT = 8
GHOST = ITERS
BACK = ITERS - 1
TWO_PI = 2.0 * math.pi
F32 = jnp.float32
BF16 = jnp.bfloat16
PAD = 8
VMEM_BYTES = 40 * 1024 * 1024
OWN_GROUP = 8
GROUP = 10


def split_table(table):
    high = table.astype(np.float32).astype(ml_dtypes.bfloat16)
    low = (table - high.astype(np.float64)).astype(np.float32).astype(ml_dtypes.bfloat16)
    return high, low


def time_table(depth):
    freq = np.arange(NF)[None, :, None]
    moment = np.arange(1, ITERS + 1)[:, None, None]
    turns = ((2 * freq + 1) * (7 * moment + np.arange(depth)[None, None, :])) % 64
    angle = turns * (TWO_PI / 64)
    return np.concatenate([np.cos(angle), -np.sin(angle)], axis=1)


def source_table(depth):
    flat = time_table(depth).transpose(0, 2, 1).reshape(ITERS * depth, 2 * NF)
    high, low = split_table(flat)
    return np.concatenate([high, high, low], axis=1)


def phase(cells, length):
    freq = np.arange(NF)[:, None, None]
    order = np.arange(FAR)[None, :, None] - FAR // 2
    period = 4 * length * NF
    turns = (order * (2 * cells[None, None, :] + 1) * (NF + freq)) % period
    angle = turns * (TWO_PI / period)
    return np.cos(angle), np.sin(angle)


def column_table(tile_cols, width):
    lanes = np.arange(width)
    cells = np.where(lanes >= width - GHOST, lanes - width, lanes)
    used = (lanes < tile_cols + GHOST) | (lanes >= width - GHOST)
    cos, sin = (t * used[None, None, :] for t in phase(cells, tile_cols))
    return np.stack([np.concatenate(split_table(t), axis=1) for t in (cos, sin, -sin)])


def column_blocks(table, target, lanes):
    pairs = []
    for half in range(2):
        for row, col, block in ((0, 0, 0), (0, 1, 1), (1, 0, 2), (1, 1, 0)):
            start = (2 * half + row) * FAR
            pairs.append(
                (
                    table.at[block, :, half * FAR : (half + 1) * FAR, 0:lanes],
                    target.at[:, start : start + FAR, col * lanes : (col + 1) * lanes],
                )
            )
    return pairs


def column_twist(count_cols):
    freq = np.arange(NF)[None, :, None]
    order = np.arange(FAR)[None, None, :] - FAR // 2
    place = np.arange(count_cols)[:, None, None]
    angle = ((order * (NF + freq) * place) % 16) * (TWO_PI / 16)
    cos, sin = np.cos(angle), np.sin(angle)
    return np.stack(
        [np.concatenate([cos, cos], axis=2), np.concatenate([sin, -sin], axis=2)]
    ).astype(np.float32)


def row_table(rows):
    table = np.concatenate(phase(np.arange(rows), rows), axis=1)
    high, low = split_table(table)
    return np.concatenate([high, high, low], axis=2)


def row_back_table(rows):
    cells = np.arange(rows + 16) - BACK
    cos, sin = phase(cells, rows)
    return np.stack([cos, sin], axis=1).transpose(0, 1, 3, 2).astype(np.float32)


def split(value):
    high = value.astype(BF16)
    return high, (value - high.astype(F32)).astype(BF16)


def dot(left, right):
    return jnp.dot(left, right, preferred_element_type=F32)


def lens_weights(depth):
    shape = (2 * NF, 2 * ITERS * depth)
    row = lax.broadcasted_iota(jnp.int32, shape, 0)
    lane = lax.broadcasted_iota(jnp.int32, shape, 1)
    moment = lane // (2 * depth) + 1
    turns = (2 * (row % NF) + 1) * (7 * moment + lane % depth)
    turns = (turns + jnp.where(row < NF, 0, 16)) % 64
    return jnp.concatenate(split(jnp.cos(turns.astype(F32) * (TWO_PI / 64))), axis=0)


def tile_twist(j):
    shape = (NF, 2 * FAR)
    freq = lax.broadcasted_iota(jnp.int32, shape, 0)
    lane = lax.broadcasted_iota(jnp.int32, shape, 1)
    turns = ((lane % FAR + FAR // 2) * (NF + freq) * j) % 16
    angle = turns.astype(F32) * (TWO_PI / 16)
    return jnp.cos(angle), jnp.where(lane < FAR, 1.0, -1.0) * jnp.sin(angle)


def half_turn(value):
    return pltpu.roll(value, FAR, 1)


def ahead_y(own, ghost):
    last = lax.broadcasted_iota(jnp.int32, own.shape, 1) == own.shape[1] - 1
    a, b = (pltpu.roll(v, v.shape[1] - 1, 1) for v in (own, ghost))
    return (jnp.where(last, b, a) - own, jnp.where(last, a, b) - ghost)


def behind_y(own, ghost):
    first = lax.broadcasted_iota(jnp.int32, own.shape, 1) == 0
    a, b = (pltpu.roll(v, 1, 1) for v in (own, ghost))
    return (own - jnp.where(first, b, a), ghost - jnp.where(first, a, b))


def depths(ref, shift=0):
    return slice(PAD + shift, ref.shape[3] - PAD + shift)


def curl_ahead(ref, r):
    def row(part, step=0, shift=0):
        return [ref[part, r + step, s, depths(ref, shift), :] for s in range(2)]

    x, y, z = row(0), row(1), row(2)
    y_next, z_next = row(1, 1), row(2, 1)
    x_deep, y_deep = row(0, 0, 1), row(1, 0, 1)
    zy, xy = ahead_y(*z), ahead_y(*x)
    return (
        [zy[s] - (y_deep[s] - y[s]) for s in range(2)],
        [(x_deep[s] - x[s]) - (z_next[s] - z[s]) for s in range(2)],
        [(y_next[s] - y[s]) - xy[s] for s in range(2)],
    )


def curl_behind(ref, r):
    def row(part, step=0, shift=0):
        return [ref[part, r + step, s, depths(ref, shift), :] for s in range(2)]

    x, y, z = row(0), row(1), row(2)
    y_prev, z_prev = row(1, -1), row(2, -1)
    x_deep, y_deep = row(0, 0, -1), row(1, 0, -1)
    zy, xy = behind_y(*z), behind_y(*x)
    return (
        [zy[s] - (y[s] - y_deep[s]) for s in range(2)],
        [(x[s] - x_deep[s]) - (z[s] - z_prev[s]) for s in range(2)],
        [(y[s] - y_prev[s]) - xy[s] for s in range(2)],
    )


def clear_pads(ref):
    for part in range(ref.shape[0]):
        for start in (0, ref.shape[3] - PAD):
            shape = ref.shape[1:3] + (PAD,) + ref.shape[4:]
            ref[part, :, :, start : start + PAD, :] = jnp.zeros(shape, F32)


def sweep(low, high, *steps):
    def group(start, rows):
        stores = []
        for k in range(rows):
            for step in steps:
                stores += step(start + k)
        for ref, index, value in stores:
            ref[index] = value

    count = high - low
    groups = -(-count // GROUP)
    size, longer = divmod(count, max(groups, 1))
    start = low
    for number, rows in ((longer, size + 1), (groups - longer, size)):
        if number == 1:
            group(start, rows)
        elif number:

            def body(k, carry, start=start, rows=rows):
                group(start + rows * k, rows)
                return carry

            lax.fori_loop(0, number, body, 0)
        start += number * rows


def copies(pairs, semaphores):
    started = []
    for k, (source, target) in enumerate(pairs):
        started.append(pltpu.make_async_copy(source, target, semaphores.at[k]))
        started[-1].start()
    return started


def ghost_mask(tile_cols, column, count_cols):
    lane = lax.broadcasted_iota(jnp.int32, (1, tile_cols), 1)
    upper = jnp.where(column < count_cols - 1, GHOST, 0)
    lower = tile_cols - jnp.where(column > 0, GHOST, 0)
    return jnp.where((lane < upper) | (lane >= lower), 1.0, 0.0)


def row_mask(row, ghost, tile_rows, place, count_rows):
    low = jnp.where(place > 0, 1.0, 0.0)
    high = jnp.where(place < count_rows - 1, 1.0, 0.0)
    return jnp.where(row < ghost, low, jnp.where(row >= ghost + tile_rows, high, 1.0))


def pack_rows_kernel(e, h, material, rows_a, rows_b, fields, cells, edges, semaphores):
    tile_rows = material.shape[0]
    even = lax.axis_index("gx") % 2 == 0
    last = tile_rows - GHOST
    starts = (jnp.where(even, last, 0), jnp.where(even, 0, last))
    loads = copies([(e, fields.at[0:3]), (h, fields.at[3:6]), (material, cells)], semaphores)
    for load in loads:
        load.wait()
    pairs = [(fields.at[:, pl.ds(starts[1], GHOST)], rows_b.at[0:6])]
    pairs.append((fields.at[:, pl.ds(starts[0], GHOST)], rows_a.at[0:6]))
    sends = copies(pairs, semaphores)
    for k, out in enumerate((rows_a, rows_b)):
        edges[k] = cells[pl.ds(starts[k], GHOST)].astype(F32)
    sends += copies([(edges.at[0], rows_a.at[6]), (edges.at[1], rows_b.at[6])], semaphores.at[2:4])
    for send in sends:
        send.wait()


def pack_columns_kernel(e, h, material, cols_a, cols_b):
    tile_rows, depth, tile_cols = material.shape
    even = lax.axis_index("gy") % 2 == 0
    lane = lax.broadcasted_iota(jnp.int32, (depth, tile_cols), 1)
    used = GHOST * tile_rows
    for pair in range(4):
        first = last = jnp.zeros((depth, tile_cols), F32)
        for part in range(2 * pair, min(2 * pair + 2, 7)):
            for x in range(tile_rows):
                if part < 3:
                    plane = e[part, x]
                elif part < 6:
                    plane = h[part - 3, x]
                else:
                    plane = material[x].astype(F32)
                shift = used * (part % 2) + GHOST * x
                spot = (lane >= shift) & (lane < shift + GHOST)
                first = jnp.where(spot, pltpu.roll(plane, shift, 1) if shift else plane, first)
                shift = (shift + GHOST) % tile_cols
                last = jnp.where(spot, pltpu.roll(plane, shift, 1) if shift else plane, last)
        cols_a[pair] = jnp.where(even, last, first)
        cols_b[pair] = jnp.where(even, first, last)


def forward_kernel(
    counts, eps_in, e, h, material, row_a, row_b, own_a, own_b, corner_a, corner_b, table,
    kept_out, inverse_out, mid, electric, magnetic, inverse, kept, index, cols, phases, stash, lens, eps, semaphores,
):
    tile_rows, depth, tile_cols = material.shape
    count_rows, count_cols = counts
    i, j = lax.axis_index("gx"), lax.axis_index("gy")
    even_x = i % 2 == 0
    even_y = j % 2 == 0
    far_edge = GHOST + tile_rows
    ext = tile_rows + 2 * GHOST
    spots = [
        pl.ds(jnp.where(even_x, far_edge, 0), GHOST),
        pl.ds(jnp.where(even_x, 0, far_edge), GHOST),
    ]
    own = pl.ds(GHOST, tile_rows)
    inner = pl.ds(PAD, depth)
    pairs = [(material, index)]
    pairs += [(own_a, cols.at[0, 0]), (own_b, cols.at[0, 1]), (corner_a, cols.at[1]), (corner_b, cols.at[2])]
    for part, spot in ((row_a, spots[0]), (row_b, spots[1])):
        pairs.append((part.at[6], inverse.at[spot, 0]))
        pairs.append((part.at[0:3], electric.at[:, spot, 0, inner, :]))
        pairs.append((part.at[3:6], magnetic.at[:, spot, 0, inner, :]))
    pairs.append((e, electric.at[:, own, 0, inner, :]))
    pairs.append((h, magnetic.at[:, own, 0, inner, :]))
    pairs.append((eps_in, eps))
    early = len(pairs)
    pairs += column_blocks(table, phases, tile_cols)
    started = copies(pairs, semaphores)
    clear_pads(electric)
    clear_pads(magnetic)
    weights = lens_weights(depth)
    twist = tile_twist(j)
    for copy in started[1:5]:
        copy.wait()

    lane = lax.broadcasted_iota(jnp.int32, (depth, tile_cols), 1)
    right_at = jnp.where(even_y, 0, 1)
    left_at = jnp.where(even_y, 1, 0)
    used = GHOST * tile_rows

    def turn(value, shift):
        shift = shift % tile_cols
        return pltpu.roll(value, shift, 1) if shift else value

    for part in range(7):
        for base, block, skip, rows in (
            (GHOST, 0, 0, tile_rows),
            (0, jnp.where(even_x, 2, 1), tile_rows - GHOST, GHOST),
            (far_edge, jnp.where(even_x, 1, 2), 0, GHOST),
        ):
            right = cols[block, right_at, part // 2]
            left = cols[block, left_at, part // 2]
            for x in range(rows):
                shift = used * (part % 2) + GHOST * (skip + x)
                value = jnp.where(lane >= tile_cols - GHOST, turn(left, -GHOST - shift), 0.0)
                value = jnp.where(lane < GHOST, turn(right, -shift), value)
                if part < 6:
                    (electric, magnetic)[part // 3][part % 3, base + x, 1, inner, :] = value
                else:
                    inverse[base + x, 1] = value

    for copy in started[:1] + started[5:early]:
        copy.wait()
    inverse[GHOST:far_edge, 0] = index[...].astype(F32)
    mask = ghost_mask(tile_cols, j, count_cols)

    def masked(row):
        scale = 0.5 * row_mask(row, GHOST, tile_rows, i, count_rows)
        return (scale, scale * mask)

    def invert(row, carry):
        scale = masked(row)
        for s in range(2):
            value = inverse[row, s]
            permittivity = jnp.full(value.shape, eps[0], F32)
            for m in range(1, NMAT):
                permittivity = jnp.where(value == float(m), eps[m], permittivity)
            inverse[row, s] = scale[s] / permittivity
        return carry

    lax.fori_loop(0, ext, invert, 0)
    sends = copies([(inverse, inverse_out)], semaphores)

    for n in range(ITERS):

        def magnetic_row(r):
            curl = curl_ahead(electric, r)
            scale = masked(r)
            stores = []
            for part in range(3):
                for s in range(2):
                    spot = (part, r, s, inner)
                    stores.append((magnetic, spot, magnetic[spot] - scale[s] * curl[part][s]))
            return stores

        def electric_row(r, x=None, q=None, side=0):
            curl = curl_behind(magnetic, r)
            stores = []
            for part in range(3):
                for s in range(2):
                    spot = (part, r, s, inner)
                    value = electric[spot] + inverse[r, s] * curl[part][s]
                    stores.append((electric, spot, value))
                    if s == 0 and x is not None:
                        stores.append((kept, (n, part, x), curl[part][0]))
                        if part < 2:
                            lanes = slice(side * tile_cols, (side + 1) * tile_cols)
                            for k, half in enumerate(split(value)):
                                start = (2 * n + k) * depth
                                stores.append((stash, (part, q, slice(start, start + depth), lanes), half))
            return stores

        def own_rows(k, carry):
            stores = []
            for step in range(OWN_GROUP):
                q, side = OWN_GROUP // 2 * k + step // 2, step % 2
                x = 2 * q + side
                stores += electric_row(GHOST + x, x, q, side)
            for ref, index, value in stores:
                ref[index] = value
            return carry

        sweep(n, ext - 1 - n, magnetic_row)
        sweep(n + 1, GHOST, electric_row)
        lax.fori_loop(0, tile_rows // OWN_GROUP, own_rows, 0)
        sweep(far_edge, ext - 1 - n, electric_row)
        sends += copies([(kept.at[n], kept_out.at[n])], semaphores.at[n + 1 : n + 2])

    for copy in started[early:]:
        copy.wait()
    waves = 2 * NF
    for p in range(2):
        for q in range(tile_rows // 2):
            value = dot(weights, stash[p, q])
            value = value[:waves] + value[waves:]
            for s in range(2):
                base = (p * tile_rows + 2 * q + s) * waves
                lens[base : base + waves, :] = value[:, s * tile_cols : (s + 1) * tile_cols]
    planes = 2 * tile_rows
    for f in range(NF):
        real = lens[pl.ds(f, planes, stride=waves), :]
        imag = lens[pl.ds(NF + f, planes, stride=waves), :]
        high, low = split(jnp.concatenate([real, imag], axis=1))
        value = lax.dot_general(
            jnp.concatenate([high, low], axis=0), phases[f], (((1,), (1,)), ((), ())), preferred_element_type=F32
        )
        value = value[:planes] + value[planes:]
        value = value[:, : 2 * FAR] + value[:, 2 * FAR :]
        mid[f] = value * twist[0][f : f + 1] + half_turn(value) * twist[1][f : f + 1]
    for copy in sends:
        copy.wait()


def backward_kernel(
    counts, own, sibling, target, twist, weights, kept_in, inverse_in, rows_far, rows_back_in, table_in,
    gradient, squares, mid, far, intensity, back, source, electric, magnetic, scaled, accum,
    kept, inverse, rows_back, table, semaphores,
):
    tile_rows, depth, tile_cols = gradient.shape
    width = 2 * tile_cols
    count_rows, count_cols = counts
    i, j = lax.axis_index("gx"), lax.axis_index("gy")
    samples = NF * FAR * FAR
    wide = 2 * FAR
    pairs = []
    for k in range(count_rows // 2):
        near = i ^ (2 * k)
        for block, index in ((own, near), (sibling, near ^ 1)):
            spot = pl.ds(pl.multiple_of(index * tile_rows, 8), tile_rows)
            for p in range(2):
                pairs.append(
                    (block.at[k, :, p * tile_rows : (p + 1) * tile_rows], mid.at[:, spot, p * wide : (p + 1) * wide])
                )
    first = len(pairs)
    pairs += [(rows_back_in, rows_back)] + column_blocks(table_in, table, width)
    second = len(pairs)
    pairs += [(inverse_in, inverse), (kept_in, kept)]
    started = copies(pairs, semaphores)
    clear_pads(scaled)
    clear_pads(magnetic)
    for copy in started[:first]:
        copy.wait()
    sign = jnp.where(lax.broadcasted_iota(jnp.int32, (1, wide), 1) < FAR, 1.0, -1.0)
    total = jnp.zeros((FAR, wide), F32)
    for f in range(NF):
        high, low = split(mid[f])
        both = dot(rows_far[f], jnp.concatenate([high, low, high], axis=0))
        level = jnp.zeros((FAR, wide), F32)
        for p in range(2):
            cos = both[:FAR, p * wide : (p + 1) * wide]
            sin = both[FAR:, p * wide : (p + 1) * wide]
            value = cos + sign * half_turn(sin)
            far[f, :, p * wide : (p + 1) * wide] = value
            level = level + value * value
        level = level + half_turn(level)
        intensity[f] = level
        total = total + level
    def wanted(f):
        return jnp.concatenate([target[f], target[f]], axis=1)

    power = jnp.sum(total, keepdims=True) / (2.0 * samples)
    over = 1.0 / power
    total = jnp.zeros((FAR, wide), F32)
    for f in range(NF):
        level = intensity[f]
        total = total + (level * over - wanted(f)) * level
    spread = jnp.sum(total, keepdims=True) / (2.0 * samples * power)

    for copy in started[first:second]:
        copy.wait()
    mask = ghost_mask(tile_cols, j, count_cols)
    span = rows_back.shape[2] - count_rows * tile_rows + tile_rows
    row = lax.broadcasted_iota(jnp.int32, (2 * span, 1), 0)
    row = jnp.where(row >= span, row - span, row)
    lowest = jnp.where(i > 0, 0, BACK)
    highest = jnp.where(i < count_rows - 1, span, BACK + tile_rows)
    inside = jnp.where((row >= lowest) & (row < highest), 1.0, 0.0)
    waves = 2 * NF
    gradients = []
    for f in range(NF):
        slope = 2.0 * ((2.0 * over) * (intensity[f] * over - wanted(f) - spread))
        gradients.append(split(far[f] * jnp.concatenate([slope, slope], axis=1)))
    start = pl.multiple_of(i * tile_rows, 8)
    crossed = []
    for f in range(NF):
        high, low = gradients[f]
        phases = jnp.concatenate(
            [rows_back[f, 0, pl.ds(start, span), :], rows_back[f, 1, pl.ds(start, span), :]], axis=0
        )
        phase_high, phase_low = split(phases)
        crossed.append(dot(phase_high, high) + dot(phase_high, low) + dot(phase_low, high))
    lefts = []
    for f in range(NF):
        turned = []
        for p in range(2):
            cos = crossed[f][:span, p * wide : (p + 1) * wide]
            sin = crossed[f][span:, p * wide : (p + 1) * wide]
            value = cos - sign * half_turn(sin)
            turned.append(value * twist[0, j, f : f + 1, :] - half_turn(value) * twist[1, j, f : f + 1, :])
        high, low = split(jnp.concatenate(turned, axis=0) * inside)
        lefts.append(
            jnp.concatenate(
                [jnp.concatenate([high, high], axis=1), jnp.concatenate([low, low], axis=1)], axis=0
            )
        )
    for f in range(NF):
        both = dot(lefts[f], table[f])
        both = both[: 2 * span] + both[2 * span :]
        for part in range(2):
            for s in range(2):
                begin = part * width + s * tile_cols
                value = both[:, begin : begin + tile_cols]
                value = value * mask if s else value
                for p in range(2):
                    back[2 * p + s, pl.ds(part * NF + f, span, stride=waves), :] = value[p * span : (p + 1) * span]

    ext = tile_rows + 2 * BACK

    def source_row(r):
        spot = pl.ds(pl.multiple_of(r * waves, 8), waves)
        stores = []
        for p in range(2):
            high, low = split(jnp.concatenate([back[2 * p, spot, :], back[2 * p + 1, spot, :]], axis=1))
            both = dot(weights[...], jnp.concatenate([high, low, high], axis=0))
            for n in range(ITERS):
                for s in range(2):
                    value = both[n * depth : (n + 1) * depth, s * tile_cols : (s + 1) * tile_cols]
                    stores.append((source, (n, p, r, s), value))
        return stores

    sweep(0, ext, source_row)
    for copy in started[second:]:
        copy.wait()
    inner = pl.ds(PAD, depth)

    def masked(r):
        scale = 0.5 * row_mask(r, BACK, tile_rows, i, count_rows)
        return (scale, scale * mask)

    def take(n, r, value, own):
        stores = []
        total = accum[r - BACK] if own and n < ITERS - 1 else None
        for part in range(3):
            for s in range(2):
                now = value[part][s]
                if part < 2:
                    extra = source[n, part, r, s]
                    now = extra if now is None else now + extra
                elif now is None:
                    now = jnp.zeros((depth, tile_cols), F32)
                if n > 0:
                    stores.append((electric, (part, r, s), now))
                    stores.append((scaled, (part, r, s, inner), inverse[r + GHOST - BACK, s] * now))
                if own and s == 0:
                    term = now * kept[n, part, r - BACK]
                    total = term if total is None else total + term
        if own:
            stores.append((accum, r - BACK, total))
        return stores

    def first_row(own):
        return lambda r: take(ITERS - 1, r, [[None, None]] * 3, own)

    sweep(0, BACK, first_row(False))
    sweep(BACK, BACK + tile_rows, first_row(True))
    sweep(BACK + tile_rows, ext, first_row(False))
    for n in range(ITERS - 1, 0, -1):

        def magnetic_row(r):
            curl = curl_ahead(scaled, r)
            scale = masked(r)
            stores = []
            for part in range(3):
                for s in range(2):
                    spot = (part, r, s, inner)
                    value = scale[s] * curl[part][s]
                    stores.append((magnetic, spot, value if n == ITERS - 1 else value + magnetic[spot]))
            return stores

        def electric_row(own):
            def step(r):
                curl = curl_behind(magnetic, r)
                value = [[electric[part, r, s] - curl[part][s] for s in range(2)] for part in range(3)]
                return take(n - 1, r, value, own)

            return step

        low, high = BACK - n, BACK + tile_rows + n - 1
        sweep(low, high, magnetic_row)
        sweep(low + 1, BACK, electric_row(False))
        sweep(BACK, BACK + tile_rows, electric_row(True))
        sweep(BACK + tile_rows, high, electric_row(False))

    total = jnp.zeros((depth, tile_cols), F32)
    for x in range(tile_rows):
        value = inverse[GHOST + x, 0]
        value = -2.0 * (value * value) * accum[x]
        gradient[x] = value
        total = total + value * value
    squares[...] = jnp.broadcast_to(jnp.sum(total, keepdims=True), squares.shape)


def scale_kernel(cells, squares, gradient, result):
    total = jnp.sum(squares[...], keepdims=True) / squares.shape[1]
    scale = 1.0 / jnp.sqrt(total / cells + 1e-06)
    for x in range(gradient.shape[0]):
        result[x] = gradient[x] * scale


VMEM = pl.BlockSpec(memory_space=pltpu.VMEM)
HBM = pl.BlockSpec(memory_space=pltpu.HBM)
ANY = pl.BlockSpec(memory_space=pl.ANY)
DMA = pltpu.SemaphoreType.DMA


def call(kernel, name, specs, outs, scratch=(), out_specs=VMEM):
    return pl.pallas_call(
        kernel,
        name=name,
        in_specs=specs,
        out_specs=out_specs,
        out_shape=outs,
        scratch_shapes=scratch,
        compiler_params=pltpu.CompilerParams(vmem_limit_bytes=VMEM_BYTES),
    )


def array(*shape):
    return jax.ShapeDtypeStruct(shape, F32)


def buffer(*shape):
    return pltpu.VMEM(shape, F32)


def even_swaps(count):
    return [(k, k ^ 1) for k in range(count)]


def odd_swaps(count):
    return [(k, k + 1 if k % 2 else k - 1) for k in range(1, count - 1)]


def body(count_rows, count_cols, e_init, h_init, material, eps_table, target):
    tile_rows, depth, tile_cols = material.shape
    counts = (count_rows, count_cols)
    edge = array(7, GHOST, depth, tile_cols)
    side = array(4, depth, tile_cols)
    row_a, row_b = call(
        pack_rows_kernel,
        "pack_rows",
        [HBM] * 3,
        (edge, edge),
        [
            buffer(6, tile_rows, depth, tile_cols),
            pltpu.VMEM((tile_rows, depth, tile_cols), jnp.int32),
            buffer(2, GHOST, depth, tile_cols),
            DMA((4,)),
        ],
        (HBM, HBM),
    )(e_init, h_init, material)
    rows_a, rows_b = even_swaps(count_rows), odd_swaps(count_rows)
    cols_a, cols_b = even_swaps(count_cols), odd_swaps(count_cols)
    row_b = lax.ppermute(row_b, "gx", rows_b)
    row_a = lax.ppermute(row_a, "gx", rows_a)
    col_a, col_b = call(pack_columns_kernel, "pack_columns", [VMEM] * 3, (side, side), (), (VMEM, VMEM))(
        e_init, h_init, material
    )
    col_b = lax.ppermute(col_b, "gy", cols_b)
    col_a = lax.ppermute(col_a, "gy", cols_a)
    corner = jnp.stack([col_a, col_b])
    corner_b = lax.ppermute(corner, "gx", rows_b)
    corner_a = lax.ppermute(corner, "gx", rows_a)

    table = jnp.asarray(column_table(tile_cols, 2 * tile_cols))
    twist = jnp.asarray(column_twist(count_cols))
    ext = tile_rows + 2 * GHOST
    waves = 2 * NF
    kept = (ITERS, 3, tile_rows, depth, tile_cols)
    inverse = (ext, 2, depth, tile_cols)
    kept_out, inverse_out, mid = call(
        functools.partial(forward_kernel, counts),
        "forward",
        [HBM] * 6 + [ANY] * 4 + [HBM],
        (array(*kept), array(*inverse), array(NF, 2 * tile_rows, 2 * FAR)),
        [
            buffer(3, ext, 2, depth + 2 * PAD, tile_cols),
            buffer(3, ext, 2, depth + 2 * PAD, tile_cols),
            buffer(*inverse),
            buffer(*kept),
            pltpu.VMEM((tile_rows, depth, tile_cols), jnp.int32),
            buffer(3, 2, 4, depth, tile_cols),
            pltpu.VMEM((NF, 4 * FAR, 2 * tile_cols), BF16),
            pltpu.VMEM((2, tile_rows // 2, 2 * ITERS * depth, 2 * tile_cols), BF16),
            buffer(2 * tile_rows * waves, tile_cols),
            pltpu.SMEM(eps_table.shape, F32),
            DMA((22,)),
        ],
        (HBM, HBM, VMEM),
    )(
        eps_table, e_init, h_init, material, row_a, row_b, col_a, col_b,
        corner_a, corner_b, table,
    )

    whole = mid
    for k in range(1, count_cols):
        whole = whole + lax.ppermute(mid, "gy", [(n, n ^ k) for n in range(count_cols)])
    own = jnp.stack(
        [whole]
        + [lax.ppermute(whole, "gx", [(n, n ^ k) for n in range(count_rows)]) for k in range(2, count_rows, 2)]
    )
    sibling = lax.ppermute(own, "gx", rows_a)

    rows = count_rows * tile_rows
    ext = tile_rows + 2 * BACK
    span = tile_rows + 16
    devices = count_rows * count_cols
    grid = (3, ext, 2, depth + 2 * PAD, tile_cols)
    back_rows = row_back_table(rows)
    gradient, squares = call(
        functools.partial(backward_kernel, counts),
        "backward",
        [ANY] * 2 + [VMEM] * 3 + [HBM] * 2 + [VMEM] + [HBM] * 2,
        (array(tile_rows, depth, tile_cols), array(devices, 128)),
        [
            buffer(NF, rows, 4 * FAR),
            buffer(NF, FAR, 4 * FAR),
            buffer(NF, FAR, 2 * FAR),
            buffer(4, span * waves, tile_cols),
            buffer(ITERS, 2, ext, 2, depth, tile_cols),
            buffer(3, ext, 2, depth, tile_cols),
            buffer(*grid),
            buffer(*grid),
            buffer(tile_rows, depth, tile_cols),
            buffer(*kept),
            buffer(*inverse),
            buffer(*back_rows.shape),
            pltpu.VMEM((NF, 4 * FAR, 4 * tile_cols), BF16),
            DMA((2 * count_rows + 11,)),
        ],
        (VMEM, VMEM),
    )(
        own, sibling, target, twist, jnp.asarray(source_table(depth)),
        kept_out, inverse_out, jnp.asarray(row_table(rows)), jnp.asarray(back_rows), table,
    )
    squares = lax.all_to_all(squares, ("gx", "gy"), 0, 0, tiled=True)
    cells = rows * depth * tile_cols * count_cols
    return call(
        functools.partial(scale_kernel, cells), "scale", [VMEM, VMEM], array(tile_rows, depth, tile_cols)
    )(squares, gradient)


def solution(mesh):
    in_specs = (P(None, "gx", None, "gy"), P(None, "gx", None, "gy"), P("gx", None, "gy"), P(), P())
    out_specs = P("gx", None, "gy")
    part = functools.partial(body, mesh.shape["gx"], mesh.shape["gy"])
    return jax.shard_map(part, mesh=mesh, in_specs=in_specs, out_specs=out_specs, check_vma=False)
```

```python
import functools
import math

import jax
import jax.numpy as jnp
import ml_dtypes
import numpy as np
from jax import lax
from jax.experimental import pallas as pl
from jax.experimental.pallas import tpu as pltpu
from jax.sharding import PartitionSpec as P

ITERS = 6
NF = 8
FAR = 64
NMAT = 8
GHOST = ITERS
BACK = ITERS - 1
TWO_PI = 2.0 * math.pi
F32 = jnp.float32
BF16 = jnp.bfloat16
PAD = 8
VMEM_BYTES = 40 * 1024 * 1024
OWN_GROUP = 8
GROUP = 10


def split_table(table):
    high = table.astype(np.float32).astype(ml_dtypes.bfloat16)
    low = (table - high.astype(np.float64)).astype(np.float32).astype(ml_dtypes.bfloat16)
    return high, low


def time_table(depth):
    freq = np.arange(NF)[None, :, None]
    moment = np.arange(1, ITERS + 1)[:, None, None]
    turns = ((2 * freq + 1) * (7 * moment + np.arange(depth)[None, None, :])) % 64
    angle = turns * (TWO_PI / 64)
    return np.concatenate([np.cos(angle), -np.sin(angle)], axis=1)


def source_table(depth):
    flat = time_table(depth).transpose(0, 2, 1).reshape(ITERS * depth, 2 * NF)
    high, low = split_table(flat)
    return np.concatenate([high, high, low], axis=1)


def phase(cells, length):
    freq = np.arange(NF)[:, None, None]
    order = np.arange(FAR)[None, :, None] - FAR // 2
    period = 4 * length * NF
    turns = (order * (2 * cells[None, None, :] + 1) * (NF + freq)) % period
    angle = turns * (TWO_PI / period)
    return np.cos(angle), np.sin(angle)


def column_table(tile_cols, width):
    lanes = np.arange(width)
    cells = np.where(lanes >= width - GHOST, lanes - width, lanes)
    used = (lanes < tile_cols + GHOST) | (lanes >= width - GHOST)
    cos, sin = (t * used[None, None, :] for t in phase(cells, tile_cols))
    return np.stack([np.concatenate(split_table(t), axis=1) for t in (cos, sin, -sin)])


def column_blocks(table, target, lanes):
    pairs = []
    for half in range(2):
        for row, col, block in ((0, 0, 0), (0, 1, 1), (1, 0, 2), (1, 1, 0)):
            start = (2 * half + row) * FAR
            pairs.append(
                (
                    table.at[block, :, half * FAR : (half + 1) * FAR, 0:lanes],
                    target.at[:, start : start + FAR, col * lanes : (col + 1) * lanes],
                )
            )
    return pairs


def column_twist(count_cols):
    freq = np.arange(NF)[None, :, None]
    order = np.arange(FAR)[None, None, :] - FAR // 2
    place = np.arange(count_cols)[:, None, None]
    angle = ((order * (NF + freq) * place) % 16) * (TWO_PI / 16)
    cos, sin = np.cos(angle), np.sin(angle)
    return np.stack(
        [np.concatenate([cos, cos], axis=2), np.concatenate([sin, -sin], axis=2)]
    ).astype(np.float32)


def row_table(rows):
    table = np.concatenate(phase(np.arange(rows), rows), axis=1)
    high, low = split_table(table)
    return np.concatenate([high, high, low], axis=2)


def row_back_table(rows):
    cells = np.arange(rows + 16) - BACK
    cos, sin = phase(cells, rows)
    return np.stack([cos, sin], axis=1).transpose(0, 1, 3, 2).astype(np.float32)


def split(value):
    high = value.astype(BF16)
    return high, (value - high.astype(F32)).astype(BF16)


def dot(left, right):
    return jnp.dot(left, right, preferred_element_type=F32)


def lens_weights(depth):
    shape = (2 * NF, 2 * ITERS * depth)
    row = lax.broadcasted_iota(jnp.int32, shape, 0)
    lane = lax.broadcasted_iota(jnp.int32, shape, 1)
    moment = lane // (2 * depth) + 1
    turns = (2 * (row % NF) + 1) * (7 * moment + lane % depth)
    turns = (turns + jnp.where(row < NF, 0, 16)) % 64
    return jnp.concatenate(split(jnp.cos(turns.astype(F32) * (TWO_PI / 64))), axis=0)


def tile_twist(j):
    shape = (NF, 2 * FAR)
    freq = lax.broadcasted_iota(jnp.int32, shape, 0)
    lane = lax.broadcasted_iota(jnp.int32, shape, 1)
    turns = ((lane % FAR + FAR // 2) * (NF + freq) * j) % 16
    angle = turns.astype(F32) * (TWO_PI / 16)
    return jnp.cos(angle), jnp.where(lane < FAR, 1.0, -1.0) * jnp.sin(angle)


def half_turn(value):
    return pltpu.roll(value, FAR, 1)


def ahead_y(own, ghost):
    last = lax.broadcasted_iota(jnp.int32, own.shape, 1) == own.shape[1] - 1
    a, b = (pltpu.roll(v, v.shape[1] - 1, 1) for v in (own, ghost))
    return (jnp.where(last, b, a) - own, jnp.where(last, a, b) - ghost)


def behind_y(own, ghost):
    first = lax.broadcasted_iota(jnp.int32, own.shape, 1) == 0
    a, b = (pltpu.roll(v, 1, 1) for v in (own, ghost))
    return (own - jnp.where(first, b, a), ghost - jnp.where(first, a, b))


def depths(ref, shift=0):
    return slice(PAD + shift, ref.shape[3] - PAD + shift)


def curl_ahead(ref, r):
    def row(part, step=0, shift=0):
        return [ref[part, r + step, s, depths(ref, shift), :] for s in range(2)]

    x, y, z = row(0), row(1), row(2)
    y_next, z_next = row(1, 1), row(2, 1)
    x_deep, y_deep = row(0, 0, 1), row(1, 0, 1)
    zy, xy = ahead_y(*z), ahead_y(*x)
    return (
        [zy[s] - (y_deep[s] - y[s]) for s in range(2)],
        [(x_deep[s] - x[s]) - (z_next[s] - z[s]) for s in range(2)],
        [(y_next[s] - y[s]) - xy[s] for s in range(2)],
    )


def curl_behind(ref, r):
    def row(part, step=0, shift=0):
        return [ref[part, r + step, s, depths(ref, shift), :] for s in range(2)]

    x, y, z = row(0), row(1), row(2)
    y_prev, z_prev = row(1, -1), row(2, -1)
    x_deep, y_deep = row(0, 0, -1), row(1, 0, -1)
    zy, xy = behind_y(*z), behind_y(*x)
    return (
        [zy[s] - (y[s] - y_deep[s]) for s in range(2)],
        [(x[s] - x_deep[s]) - (z[s] - z_prev[s]) for s in range(2)],
        [(y[s] - y_prev[s]) - xy[s] for s in range(2)],
    )


def clear_pads(ref):
    for part in range(ref.shape[0]):
        for start in (0, ref.shape[3] - PAD):
            shape = ref.shape[1:3] + (PAD,) + ref.shape[4:]
            ref[part, :, :, start : start + PAD, :] = jnp.zeros(shape, F32)


def sweep(low, high, *steps):
    def group(start, rows):
        stores = []
        for k in range(rows):
            for step in steps:
                stores += step(start + k)
        for ref, index, value in stores:
            ref[index] = value

    count = high - low
    groups = -(-count // GROUP)
    size, longer = divmod(count, max(groups, 1))
    start = low
    for number, rows in ((longer, size + 1), (groups - longer, size)):
        if number == 1:
            group(start, rows)
        elif number:

            def body(k, carry, start=start, rows=rows):
                group(start + rows * k, rows)
                return carry

            lax.fori_loop(0, number, body, 0)
        start += number * rows


def copies(pairs, semaphores):
    started = []
    for k, (source, target) in enumerate(pairs):
        started.append(pltpu.make_async_copy(source, target, semaphores.at[k]))
        started[-1].start()
    return started


def ghost_mask(tile_cols, column, count_cols):
    lane = lax.broadcasted_iota(jnp.int32, (1, tile_cols), 1)
    upper = jnp.where(column < count_cols - 1, GHOST, 0)
    lower = tile_cols - jnp.where(column > 0, GHOST, 0)
    return jnp.where((lane < upper) | (lane >= lower), 1.0, 0.0)


def row_mask(row, ghost, tile_rows, place, count_rows):
    low = jnp.where(place > 0, 1.0, 0.0)
    high = jnp.where(place < count_rows - 1, 1.0, 0.0)
    return jnp.where(row < ghost, low, jnp.where(row >= ghost + tile_rows, high, 1.0))


def pack_rows_kernel(e, h, material, rows_a, rows_b, fields, cells, edges, semaphores):
    tile_rows = material.shape[0]
    even = lax.axis_index("gx") % 2 == 0
    last = tile_rows - GHOST
    starts = (jnp.where(even, last, 0), jnp.where(even, 0, last))
    loads = copies([(e, fields.at[0:3]), (h, fields.at[3:6]), (material, cells)], semaphores)
    for load in loads:
        load.wait()
    pairs = [(fields.at[:, pl.ds(starts[1], GHOST)], rows_b.at[0:6])]
    pairs.append((fields.at[:, pl.ds(starts[0], GHOST)], rows_a.at[0:6]))
    sends = copies(pairs, semaphores)
    for k, out in enumerate((rows_a, rows_b)):
        edges[k] = cells[pl.ds(starts[k], GHOST)].astype(F32)
    sends += copies([(edges.at[0], rows_a.at[6]), (edges.at[1], rows_b.at[6])], semaphores.at[2:4])
    for send in sends:
        send.wait()


def pack_columns_kernel(e, h, material, cols_a, cols_b):
    tile_rows, depth, tile_cols = material.shape
    even = lax.axis_index("gy") % 2 == 0
    lane = lax.broadcasted_iota(jnp.int32, (depth, tile_cols), 1)
    used = GHOST * tile_rows
    for pair in range(4):
        first = last = jnp.zeros((depth, tile_cols), F32)
        for part in range(2 * pair, min(2 * pair + 2, 7)):
            for x in range(tile_rows):
                if part < 3:
                    plane = e[part, x]
                elif part < 6:
                    plane = h[part - 3, x]
                else:
                    plane = material[x].astype(F32)
                shift = used * (part % 2) + GHOST * x
                spot = (lane >= shift) & (lane < shift + GHOST)
                first = jnp.where(spot, pltpu.roll(plane, shift, 1) if shift else plane, first)
                shift = (shift + GHOST) % tile_cols
                last = jnp.where(spot, pltpu.roll(plane, shift, 1) if shift else plane, last)
        cols_a[pair] = jnp.where(even, last, first)
        cols_b[pair] = jnp.where(even, first, last)


def forward_kernel(
    counts, eps_in, e, h, material, row_a, row_b, own_a, own_b, corner_a, corner_b, table,
    kept_out, inverse_out, mid, electric, magnetic, inverse, kept, index, cols, phases, stash, lens, eps, semaphores,
):
    tile_rows, depth, tile_cols = material.shape
    count_rows, count_cols = counts
    i, j = lax.axis_index("gx"), lax.axis_index("gy")
    even_x = i % 2 == 0
    even_y = j % 2 == 0
    far_edge = GHOST + tile_rows
    ext = tile_rows + 2 * GHOST
    spots = [
        pl.ds(jnp.where(even_x, far_edge, 0), GHOST),
        pl.ds(jnp.where(even_x, 0, far_edge), GHOST),
    ]
    own = pl.ds(GHOST, tile_rows)
    inner = pl.ds(PAD, depth)
    pairs = [(material, index)]
    pairs += [(own_a, cols.at[0, 0]), (own_b, cols.at[0, 1]), (corner_a, cols.at[1]), (corner_b, cols.at[2])]
    for part, spot in ((row_a, spots[0]), (row_b, spots[1])):
        pairs.append((part.at[6], inverse.at[spot, 0]))
        pairs.append((part.at[0:3], electric.at[:, spot, 0, inner, :]))
        pairs.append((part.at[3:6], magnetic.at[:, spot, 0, inner, :]))
    pairs.append((e, electric.at[:, own, 0, inner, :]))
    pairs.append((h, magnetic.at[:, own, 0, inner, :]))
    pairs.append((eps_in, eps))
    early = len(pairs)
    pairs += column_blocks(table, phases, tile_cols)
    started = copies(pairs, semaphores)
    clear_pads(electric)
    clear_pads(magnetic)
    weights = lens_weights(depth)
    twist = tile_twist(j)
    for copy in started[1:5]:
        copy.wait()

    lane = lax.broadcasted_iota(jnp.int32, (depth, tile_cols), 1)
    right_at = jnp.where(even_y, 0, 1)
    left_at = jnp.where(even_y, 1, 0)
    used = GHOST * tile_rows

    def turn(value, shift):
        shift = shift % tile_cols
        return pltpu.roll(value, shift, 1) if shift else value

    for part in range(7):
        for base, block, skip, rows in (
            (GHOST, 0, 0, tile_rows),
            (0, jnp.where(even_x, 2, 1), tile_rows - GHOST, GHOST),
            (far_edge, jnp.where(even_x, 1, 2), 0, GHOST),
        ):
            right = cols[block, right_at, part // 2]
            left = cols[block, left_at, part // 2]
            for x in range(rows):
                shift = used * (part % 2) + GHOST * (skip + x)
                value = jnp.where(lane >= tile_cols - GHOST, turn(left, -GHOST - shift), 0.0)
                value = jnp.where(lane < GHOST, turn(right, -shift), value)
                if part < 6:
                    (electric, magnetic)[part // 3][part % 3, base + x, 1, inner, :] = value
                else:
                    inverse[base + x, 1] = value

    for copy in started[:1] + started[5:early]:
        copy.wait()
    inverse[GHOST:far_edge, 0] = index[...].astype(F32)
    mask = ghost_mask(tile_cols, j, count_cols)

    def masked(row):
        scale = 0.5 * row_mask(row, GHOST, tile_rows, i, count_rows)
        return (scale, scale * mask)

    def invert(row, carry):
        scale = masked(row)
        for s in range(2):
            value = inverse[row, s]
            permittivity = jnp.full(value.shape, eps[0], F32)
            for m in range(1, NMAT):
                permittivity = jnp.where(value == float(m), eps[m], permittivity)
            inverse[row, s] = scale[s] / permittivity
        return carry

    lax.fori_loop(0, ext, invert, 0)
    sends = copies([(inverse, inverse_out)], semaphores)

    for n in range(ITERS):

        def magnetic_row(r):
            curl = curl_ahead(electric, r)
            scale = masked(r)
            stores = []
            for part in range(3):
                for s in range(2):
                    spot = (part, r, s, inner)
                    stores.append((magnetic, spot, magnetic[spot] - scale[s] * curl[part][s]))
            return stores

        def electric_row(r, x=None, q=None, side=0):
            curl = curl_behind(magnetic, r)
            stores = []
            for part in range(3):
                for s in range(2):
                    spot = (part, r, s, inner)
                    value = electric[spot] + inverse[r, s] * curl[part][s]
                    if n < ITERS - 1:
                        stores.append((electric, spot, value))
                    if s == 0 and x is not None:
                        stores.append((kept, (n, part, x), curl[part][0]))
                        if part < 2:
                            lanes = slice(side * tile_cols, (side + 1) * tile_cols)
                            for k, half in enumerate(split(value)):
                                start = (2 * n + k) * depth
                                stores.append((stash, (part, q, slice(start, start + depth), lanes), half))
            return stores

        def own_rows(k, carry):
            stores = []
            for step in range(OWN_GROUP):
                q, side = OWN_GROUP // 2 * k + step // 2, step % 2
                x = 2 * q + side
                stores += electric_row(GHOST + x, x, q, side)
            for ref, index, value in stores:
                ref[index] = value
            return carry

        sweep(n, ext - 1 - n, magnetic_row)
        sweep(n + 1, GHOST, electric_row)
        lax.fori_loop(0, tile_rows // OWN_GROUP, own_rows, 0)
        sweep(far_edge, ext - 1 - n, electric_row)
        sends += copies([(kept.at[n], kept_out.at[n])], semaphores.at[n + 1 : n + 2])

    for copy in started[early:]:
        copy.wait()
    waves = 2 * NF
    for p in range(2):
        for q in range(tile_rows // 2):
            value = dot(weights, stash[p, q])
            value = value[:waves] + value[waves:]
            for s in range(2):
                base = (p * tile_rows + 2 * q + s) * waves
                lens[base : base + waves, :] = value[:, s * tile_cols : (s + 1) * tile_cols]
    planes = 2 * tile_rows
    for f in range(NF):
        real = lens[pl.ds(f, planes, stride=waves), :]
        imag = lens[pl.ds(NF + f, planes, stride=waves), :]
        high, low = split(jnp.concatenate([real, imag], axis=1))
        value = lax.dot_general(
            jnp.concatenate([high, low], axis=0), phases[f], (((1,), (1,)), ((), ())), preferred_element_type=F32
        )
        value = value[:planes] + value[planes:]
        value = value[:, : 2 * FAR] + value[:, 2 * FAR :]
        mid[f] = value * twist[0][f : f + 1] + half_turn(value) * twist[1][f : f + 1]
    for copy in sends:
        copy.wait()


def backward_kernel(
    counts, blocks, target, twist, weights, kept_in, inverse_in, rows_far, rows_back_in, table_in,
    gradient, squares, mid, far, intensity, back, source, electric, magnetic, scaled, accum,
    kept, inverse, rows_back, table, semaphores,
):
    tile_rows, depth, tile_cols = gradient.shape
    width = 2 * tile_cols
    count_rows, count_cols = counts
    i, j = lax.axis_index("gx"), lax.axis_index("gy")
    samples = NF * FAR * FAR
    wide = 2 * FAR
    pairs = []
    for k in range(count_rows // 2):
        near = i ^ (2 * k)
        for block, index in ((blocks[2 * k], near), (blocks[2 * k + 1], near ^ 1)):
            spot = pl.ds(pl.multiple_of(index * tile_rows, 8), tile_rows)
            for p in range(2):
                pairs.append(
                    (block.at[:, p * tile_rows : (p + 1) * tile_rows], mid.at[:, spot, p * wide : (p + 1) * wide])
                )
    first = len(pairs)
    pairs += [(rows_back_in, rows_back)] + column_blocks(table_in, table, width)
    second = len(pairs)
    pairs += [(inverse_in, inverse), (kept_in, kept)]
    started = copies(pairs, semaphores)
    clear_pads(scaled)
    clear_pads(magnetic)
    for copy in started[:first]:
        copy.wait()
    sign = jnp.where(lax.broadcasted_iota(jnp.int32, (1, wide), 1) < FAR, 1.0, -1.0)
    total = jnp.zeros((FAR, wide), F32)
    for f in range(NF):
        high, low = split(mid[f])
        both = dot(rows_far[f], jnp.concatenate([high, low, high], axis=0))
        level = jnp.zeros((FAR, wide), F32)
        for p in range(2):
            cos = both[:FAR, p * wide : (p + 1) * wide]
            sin = both[FAR:, p * wide : (p + 1) * wide]
            value = cos + sign * half_turn(sin)
            far[f, :, p * wide : (p + 1) * wide] = value
            level = level + value * value
        level = level + half_turn(level)
        intensity[f] = level
        total = total + level
    def wanted(f):
        return jnp.concatenate([target[f], target[f]], axis=1)

    power = jnp.sum(total, keepdims=True) / (2.0 * samples)
    over = 1.0 / power
    total = jnp.zeros((FAR, wide), F32)
    for f in range(NF):
        level = intensity[f]
        total = total + (level * over - wanted(f)) * level
    spread = jnp.sum(total, keepdims=True) / (2.0 * samples * power)

    for copy in started[first:second]:
        copy.wait()
    mask = ghost_mask(tile_cols, j, count_cols)
    span = rows_back.shape[2] - count_rows * tile_rows + tile_rows
    row = lax.broadcasted_iota(jnp.int32, (2 * span, 1), 0)
    row = jnp.where(row >= span, row - span, row)
    lowest = jnp.where(i > 0, 0, BACK)
    highest = jnp.where(i < count_rows - 1, span, BACK + tile_rows)
    inside = jnp.where((row >= lowest) & (row < highest), 1.0, 0.0)
    waves = 2 * NF
    gradients = []
    for f in range(NF):
        slope = 2.0 * ((2.0 * over) * (intensity[f] * over - wanted(f) - spread))
        gradients.append(split(far[f] * jnp.concatenate([slope, slope], axis=1)))
    start = pl.multiple_of(i * tile_rows, 8)
    crossed = []
    for f in range(NF):
        high, low = gradients[f]
        phases = jnp.concatenate(
            [rows_back[f, 0, pl.ds(start, span), :], rows_back[f, 1, pl.ds(start, span), :]], axis=0
        )
        phase_high, phase_low = split(phases)
        crossed.append(dot(phase_high, high) + dot(phase_high, low) + dot(phase_low, high))
    lefts = []
    for f in range(NF):
        turned = []
        for p in range(2):
            cos = crossed[f][:span, p * wide : (p + 1) * wide]
            sin = crossed[f][span:, p * wide : (p + 1) * wide]
            value = cos - sign * half_turn(sin)
            turned.append(value * twist[0, j, f : f + 1, :] - half_turn(value) * twist[1, j, f : f + 1, :])
        high, low = split(jnp.concatenate(turned, axis=0) * inside)
        lefts.append(
            jnp.concatenate(
                [jnp.concatenate([high, high], axis=1), jnp.concatenate([low, low], axis=1)], axis=0
            )
        )
    for f in range(NF):
        both = dot(lefts[f], table[f])
        both = both[: 2 * span] + both[2 * span :]
        for part in range(2):
            for s in range(2):
                begin = part * width + s * tile_cols
                value = both[:, begin : begin + tile_cols]
                value = value * mask if s else value
                for p in range(2):
                    back[2 * p + s, pl.ds(part * NF + f, span, stride=waves), :] = value[p * span : (p + 1) * span]

    ext = tile_rows + 2 * BACK

    def source_row(r):
        spot = pl.ds(pl.multiple_of(r * waves, 8), waves)
        stores = []
        for p in range(2):
            high, low = split(jnp.concatenate([back[2 * p, spot, :], back[2 * p + 1, spot, :]], axis=1))
            both = dot(weights[...], jnp.concatenate([high, low, high], axis=0))
            for n in range(ITERS):
                for s in range(2):
                    value = both[n * depth : (n + 1) * depth, s * tile_cols : (s + 1) * tile_cols]
                    stores.append((source, (n, p, r, s), value))
        return stores

    sweep(0, ext, source_row)
    for copy in started[second:]:
        copy.wait()
    inner = pl.ds(PAD, depth)

    def masked(r):
        scale = 0.5 * row_mask(r, BACK, tile_rows, i, count_rows)
        return (scale, scale * mask)

    def take(n, r, value, own):
        stores = []
        total = accum[r - BACK] if own and n < ITERS - 1 else None
        for part in range(3):
            for s in range(2):
                now = value[part][s]
                if part < 2:
                    extra = source[n, part, r, s]
                    now = extra if now is None else now + extra
                elif now is None:
                    now = jnp.zeros((depth, tile_cols), F32)
                if n > 0:
                    stores.append((electric, (part, r, s), now))
                    stores.append((scaled, (part, r, s, inner), inverse[r + GHOST - BACK, s] * now))
                if own and s == 0:
                    term = now * kept[n, part, r - BACK]
                    total = term if total is None else total + term
        if own:
            stores.append((accum, r - BACK, total))
        return stores

    def first_row(own):
        return lambda r: take(ITERS - 1, r, [[None, None]] * 3, own)

    sweep(0, BACK, first_row(False))
    sweep(BACK, BACK + tile_rows, first_row(True))
    sweep(BACK + tile_rows, ext, first_row(False))
    for n in range(ITERS - 1, 0, -1):

        def magnetic_row(r):
            curl = curl_ahead(scaled, r)
            scale = masked(r)
            stores = []
            for part in range(3):
                for s in range(2):
                    spot = (part, r, s, inner)
                    value = scale[s] * curl[part][s]
                    stores.append((magnetic, spot, value if n == ITERS - 1 else value + magnetic[spot]))
            return stores

        def electric_row(own):
            def step(r):
                curl = curl_behind(magnetic, r)
                value = [[electric[part, r, s] - curl[part][s] for s in range(2)] for part in range(3)]
                return take(n - 1, r, value, own)

            return step

        low, high = BACK - n, BACK + tile_rows + n - 1
        sweep(low, high, magnetic_row)
        sweep(low + 1, BACK, electric_row(False))
        sweep(BACK, BACK + tile_rows, electric_row(True))
        sweep(BACK + tile_rows, high, electric_row(False))

    total = jnp.zeros((depth, tile_cols), F32)
    for x in range(tile_rows):
        value = inverse[GHOST + x, 0]
        value = -2.0 * (value * value) * accum[x]
        gradient[x] = value
        total = total + value * value
    squares[...] = jnp.broadcast_to(jnp.sum(total, keepdims=True), squares.shape)


def scale_kernel(cells, squares, gradient, result):
    total = jnp.sum(squares[...], keepdims=True) / squares.shape[1]
    scale = 1.0 / jnp.sqrt(total / cells + 1e-06)
    for x in range(gradient.shape[0]):
        result[x] = gradient[x] * scale


VMEM = pl.BlockSpec(memory_space=pltpu.VMEM)
HBM = pl.BlockSpec(memory_space=pltpu.HBM)
ANY = pl.BlockSpec(memory_space=pl.ANY)
DMA = pltpu.SemaphoreType.DMA


def call(kernel, name, specs, outs, scratch=(), out_specs=VMEM):
    return pl.pallas_call(
        kernel,
        name=name,
        in_specs=specs,
        out_specs=out_specs,
        out_shape=outs,
        scratch_shapes=scratch,
        compiler_params=pltpu.CompilerParams(vmem_limit_bytes=VMEM_BYTES),
    )


def array(*shape):
    return jax.ShapeDtypeStruct(shape, F32)


def buffer(*shape):
    return pltpu.VMEM(shape, F32)


def even_swaps(count):
    return [(k, k ^ 1) for k in range(count)]


def odd_swaps(count):
    return [(k, k + 1 if k % 2 else k - 1) for k in range(1, count - 1)]


def body(count_rows, count_cols, e_init, h_init, material, eps_table, target):
    tile_rows, depth, tile_cols = material.shape
    counts = (count_rows, count_cols)
    edge = array(7, GHOST, depth, tile_cols)
    side = array(4, depth, tile_cols)
    row_a, row_b = call(
        pack_rows_kernel,
        "pack_rows",
        [HBM] * 3,
        (edge, edge),
        [
            buffer(6, tile_rows, depth, tile_cols),
            pltpu.VMEM((tile_rows, depth, tile_cols), jnp.int32),
            buffer(2, GHOST, depth, tile_cols),
            DMA((4,)),
        ],
        (HBM, HBM),
    )(e_init, h_init, material)
    rows_a, rows_b = even_swaps(count_rows), odd_swaps(count_rows)
    cols_a, cols_b = even_swaps(count_cols), odd_swaps(count_cols)
    row_b = lax.ppermute(row_b, "gx", rows_b)
    row_a = lax.ppermute(row_a, "gx", rows_a)
    col_a, col_b = call(pack_columns_kernel, "pack_columns", [VMEM] * 3, (side, side), (), (VMEM, VMEM))(
        e_init, h_init, material
    )
    col_a = lax.ppermute(col_a, "gy", cols_a)
    col_b = lax.ppermute(col_b, "gy", cols_b)
    corner = jnp.stack([col_a, col_b])
    corner_b = lax.ppermute(corner, "gx", rows_b)
    corner_a = lax.ppermute(corner, "gx", rows_a)

    table = jnp.asarray(column_table(tile_cols, 2 * tile_cols))
    twist = jnp.asarray(column_twist(count_cols))
    ext = tile_rows + 2 * GHOST
    waves = 2 * NF
    kept = (ITERS, 3, tile_rows, depth, tile_cols)
    inverse = (ext, 2, depth, tile_cols)
    kept_out, inverse_out, mid = call(
        functools.partial(forward_kernel, counts),
        "forward",
        [HBM] * 6 + [ANY] * 4 + [HBM],
        (array(*kept), array(*inverse), array(NF, 2 * tile_rows, 2 * FAR)),
        [
            buffer(3, ext, 2, depth + 2 * PAD, tile_cols),
            buffer(3, ext, 2, depth + 2 * PAD, tile_cols),
            buffer(*inverse),
            buffer(*kept),
            pltpu.VMEM((tile_rows, depth, tile_cols), jnp.int32),
            buffer(3, 2, 4, depth, tile_cols),
            pltpu.VMEM((NF, 4 * FAR, 2 * tile_cols), BF16),
            pltpu.VMEM((2, tile_rows // 2, 2 * ITERS * depth, 2 * tile_cols), BF16),
            buffer(2 * tile_rows * waves, tile_cols),
            pltpu.SMEM(eps_table.shape, F32),
            DMA((22,)),
        ],
        (HBM, HBM, VMEM),
    )(
        eps_table, e_init, h_init, material, row_a, row_b, col_a, col_b,
        corner_a, corner_b, table,
    )

    whole = mid
    for k in range(1, count_cols):
        whole = whole + lax.ppermute(mid, "gy", [(n, n ^ k) for n in range(count_cols)])
    blocks = []
    for k in range(0, count_rows, 2):
        part = lax.ppermute(whole, "gx", [(n, n ^ k) for n in range(count_rows)]) if k else whole
        blocks += [part, lax.ppermute(part, "gx", rows_a)]

    rows = count_rows * tile_rows
    ext = tile_rows + 2 * BACK
    span = tile_rows + 16
    devices = count_rows * count_cols
    grid = (3, ext, 2, depth + 2 * PAD, tile_cols)
    back_rows = row_back_table(rows)
    gradient, squares = call(
        lambda *refs: backward_kernel(counts, refs[:count_rows], *refs[count_rows:]),
        "backward",
        [ANY] * count_rows + [VMEM] * 3 + [HBM] * 2 + [VMEM] + [HBM] * 2,
        (array(tile_rows, depth, tile_cols), array(devices, 128)),
        [
            buffer(NF, rows, 4 * FAR),
            buffer(NF, FAR, 4 * FAR),
            buffer(NF, FAR, 2 * FAR),
            buffer(4, span * waves, tile_cols),
            buffer(ITERS, 2, ext, 2, depth, tile_cols),
            buffer(3, ext, 2, depth, tile_cols),
            buffer(*grid),
            buffer(*grid),
            buffer(tile_rows, depth, tile_cols),
            buffer(*kept),
            buffer(*inverse),
            buffer(*back_rows.shape),
            pltpu.VMEM((NF, 4 * FAR, 4 * tile_cols), BF16),
            DMA((2 * count_rows + 11,)),
        ],
        (VMEM, VMEM),
    )(
        *blocks, target, twist, jnp.asarray(source_table(depth)),
        kept_out, inverse_out, jnp.asarray(row_table(rows)), jnp.asarray(back_rows), table,
    )
    squares = lax.all_to_all(squares, ("gx", "gy"), 0, 0, tiled=True)
    cells = rows * depth * tile_cols * count_cols
    return call(
        functools.partial(scale_kernel, cells), "scale", [VMEM, VMEM], array(tile_rows, depth, tile_cols)
    )(squares, gradient)


def solution(mesh):
    in_specs = (P(None, "gx", None, "gy"), P(None, "gx", None, "gy"), P("gx", None, "gy"), P(), P())
    out_specs = P("gx", None, "gy")
    part = functools.partial(body, mesh.shape["gx"], mesh.shape["gy"])
    return jax.shard_map(part, mesh=mesh, in_specs=in_specs, out_specs=out_specs, check_vma=False)
```
